256 devices in a mesh: lat: 4 (over x_lo, core), lon: 64 (over x_hi, y, z).
Axes of the slice: x: 4 (x_hi: 2, x_lo: 2; x = x_hi * 2 + x_lo), y: 4, z: 8, core: 2. Of those that a mesh axis runs over, the one named last changes fastest.
Arguments:
- field: bfloat16 [512, 2048, 128], P('lat', 'lon'), may hold values from -6 to 6
- land: int32 [512, 2048], P('lat', 'lon'), may hold values 0 or 1
- mirror: int32 [2048], replicated, may hold values from 0 to 2047, as said below
- depth_weight: bfloat16 [49, 128], replicated, may hold values from -2 to 2
- norm_gain: bfloat16 [128], replicated, may hold values from 0.5 to 2
- up_weight: bfloat16 [128, 512], replicated, may hold values from -0.5 to 0.5
- up_bias: bfloat16 [512], replicated, may hold values from -3 to 3
- down_proj: bfloat16 [512, 128], replicated, may hold values from -0.25 to 0.25
- layer_scale: bfloat16 [128], replicated, may hold values from 0.25 to 1
- section_gain: bfloat16 [3, 128], replicated, may hold values from 0.5 to 2
- section_weight: bfloat16 [3, 512, 128], replicated, may hold values from -0.25 to 0.25
- section_bias: bfloat16 [3, 128], replicated, may hold values from -3 to 3
- cotangent: bfloat16 [64, 256, 128], P('lat', 'lon'), may hold values from -6 to 6
Outputs:
- bottleneck: bfloat16 [64, 256, 128], P('lat', 'lon')
- grad_field: bfloat16 [512, 2048, 128], P('lat', 'lon')
- grad_depth: float32 [49, 128], replicated
- grad_up: float32 [128, 512], replicated
- grad_down: float32 [512, 128], replicated
- grad_section: float32 [3, 512, 128], replicated
The draws below stay inside these ranges and needn't reach their ends.
Inputs may be any that keep to these rules, and one draw needn't show every extreme that they name: mirror[i] = (s - i) mod 2048 for one s, the same for all i; mirror is its own inverse.
All inputs are finite; a program needn't handle non-finite values. No bound on the sum of `land` on one device may be relied on, other than what follows from the above.
Results may differ from the reference program's by a relative error of at most 0.017.
Values may be sent and summed in bfloat16 or wider, within the bound.
A program may use at most 128 MiB of HBM per device.

```python
import math
import jax
import jax.numpy as jnp
from jax import lax

C = 128
HID = 512
SECTIONS = 3
ROWS = 512
LON = 2048


def draw_mirror(key, part):
    pivot = jax.random.randint(jax.random.fold_in(key, 11), (), 0, LON, dtype=jnp.int32)
    return jnp.mod(pivot - jnp.arange(LON, dtype=jnp.int32), LON).astype(jnp.int32)


def touch_ends(values, stream_key, least, top_value):
    longest = values.shape.index(max(values.shape))
    spots = []
    for shift in (0, 1):
        where = [jax.random.randint(jax.random.fold_in(stream_key, axis), (), 0, length) for axis, length in enumerate(values.shape)]
        where[longest] = (where[longest] + shift) % values.shape[longest]
        spots.append(tuple(where))
    return values.at[spots[0]].set(least).at[spots[1]].set(top_value)


def block_scale(rng, dims, shards, low, top_value):
    factor_of, own = 1.0, jax.random.fold_in(rng, 6)
    for axis_at, shards_of in shards:
        draws = jnp.exp(jax.random.uniform(jax.random.fold_in(own, axis_at), (shards_of,), jnp.float32, low / len(shards), top_value / len(shards)))
        factor_of = factor_of * jnp.repeat(draws, dims[axis_at] // shards_of).reshape([-1 if axis == axis_at else 1 for axis in range(len(dims))])
    return factor_of


def scatter_about(key, shape, deviation, limit, pieces=(), held_as=jnp.bfloat16):
    values = deviation * jax.random.normal(key, shape, jnp.float32)
    if pieces:
        values = values * block_scale(key, shape, pieces, -0.22, 0.18)
    return jnp.clip(values, -limit, limit).astype(held_as)


def setup_inputs(seed: int = 0) -> dict:
    key_of = jax.random.split(jax.random.key(seed), 14)
    return {
        "field": scatter_about(key_of[0], (ROWS, LON, C), 1.0, 6.0, ((0, 4), (1, 64))),
        "land": touch_ends((jax.random.randint(key_of[1], (ROWS, LON), 0, 4) < 3).astype(jnp.int32), jax.random.fold_in(key_of[1], 1), 0, 1),
        "mirror": draw_mirror(jax.random.fold_in(key_of[13], 71), 0),
        "depth_weight": scatter_about(key_of[3], (49, C), 7 ** -0.5, 2.0),
        "norm_gain": jnp.clip(jnp.exp(jax.random.uniform(key_of[4], (C,), jnp.float32, math.log(0.5), math.log(2.0))), 0.5, 2.0).astype(jnp.bfloat16),
        "up_weight": scatter_about(key_of[5], (C, HID), C ** -0.5, 0.5),
        "up_bias": scatter_about(key_of[6], (HID,), 0.5, 3.0),
        "down_proj": scatter_about(key_of[7], (HID, C), HID ** -0.5, 0.25),
        "layer_scale": jnp.clip(jnp.exp(jax.random.uniform(key_of[8], (C,), jnp.float32, math.log(0.25), math.log(1.0))), 0.25, 1.0).astype(jnp.bfloat16),
        "section_gain": jnp.clip(jnp.exp(jax.random.uniform(key_of[9], (SECTIONS, C), jnp.float32, math.log(0.5), math.log(2.0))), 0.5, 2.0).astype(jnp.bfloat16),
        "section_weight": scatter_about(key_of[10], (SECTIONS, 4 * C, C), (4 * C) ** -0.5, 0.25),
        "section_bias": scatter_about(key_of[11], (SECTIONS, C), 0.5, 3.0),
        "cotangent": scatter_about(key_of[12], (ROWS // 8, LON // 8, C), 1.0, 6.0, ((0, 4), (1, 64))),
    }


epsilon = 1e-06

def norm_parts(values):
    center = values - lax.optimization_barrier(jnp.mean(values, axis=-1, keepdims=True))
    rstd = lax.rsqrt(lax.optimization_barrier(jnp.mean(center * center, axis=-1, keepdims=True)) + epsilon)
    return (center * rstd, rstd)

def norm_back(grad_hat, normed_hat, rstd):
    first = lax.optimization_barrier(jnp.mean(grad_hat, axis=-1, keepdims=True))
    second = lax.optimization_barrier(jnp.mean(grad_hat * normed_hat, axis=-1, keepdims=True))
    return rstd * (grad_hat - first - normed_hat * second)

def gelu_parts(hidden):
    cdf = 0.5 * (1.0 + jax.scipy.special.erf(hidden * 0.7071067811865476))
    dens = jnp.exp(-0.5 * hidden * hidden) * 0.3989422804014327
    return (hidden * cdf, cdf + hidden * dens)

def block_pass(ext_rows, x_rows, land_rows, cot_rows, taps, norm_gain, up_weight, up_bias, down_proj, layer_scale, section_gain, section_weight, section_bias):
    block_rows = x_rows.shape[0]
    block_cols = x_rows.shape[1]
    chans = x_rows.shape[2]
    depth_out = jnp.zeros((block_rows, block_cols, chans), jnp.float32)
    for tap in range(49):
        tap_row = tap // 7
        tap_col = tap % 7
        depth_out = depth_out + ext_rows[tap_row:tap_row + block_rows, tap_col:tap_col + block_cols] * taps[tap]
    depth_hat, depth_rstd = norm_parts(depth_out)
    normed = (depth_hat * norm_gain.astype(jnp.float32)).astype(jnp.bfloat16)
    flat = normed.reshape(-1, chans)
    hidden = jnp.dot(flat, up_weight, preferred_element_type=jnp.float32) + up_bias.astype(jnp.float32)
    active_full, slope = gelu_parts(hidden)
    active = active_full.astype(jnp.bfloat16)
    mixed = jnp.dot(active, down_proj, preferred_element_type=jnp.float32).reshape(block_rows, block_cols, chans)
    scale_f = layer_scale.astype(jnp.float32)
    level = (land_rows * (x_rows.astype(jnp.float32) + scale_f * mixed)).astype(jnp.bfloat16)
    saved = []
    for section in range(SECTIONS):
        section_hat, section_rstd = norm_parts(level.astype(jnp.float32))
        section_norm = (section_hat * section_gain[section].astype(jnp.float32)).astype(jnp.bfloat16)
        size_r = section_norm.shape[0]
        size_c = section_norm.shape[1]
        patches = section_norm.reshape(size_r // 2, 2, size_c // 2, 2, chans).astype(jnp.float32)
        kernel = section_weight[section].reshape(2, 2, chans, chans).astype(jnp.float32)
        level = (jnp.einsum('iajbc,abcd->ijd', patches, kernel, precision=lax.Precision.HIGHEST) + section_bias[section].astype(jnp.float32)).astype(jnp.bfloat16)
        saved.append((section_hat, section_rstd, patches, kernel))
    upstream = cot_rows
    section_list = [None] * SECTIONS
    for section in range(SECTIONS - 1, -1, -1):
        section_hat, section_rstd, patches, kernel = saved[section]
        up_f = upstream.astype(jnp.float32)
        section_list[section] = jnp.einsum('iajbc,ijd->abcd', patches, up_f, precision=lax.Precision.HIGHEST).reshape(4 * chans, chans)
        spread = jnp.einsum('ijd,abcd->iajbc', up_f, kernel, precision=lax.Precision.HIGHEST).reshape(section_hat.shape)
        upstream = norm_back(spread * section_gain[section].astype(jnp.float32), section_hat, section_rstd).astype(jnp.bfloat16)
    section_total = jnp.stack(section_list)
    direct = land_rows * upstream.astype(jnp.float32)
    mix_grad = (direct * scale_f).astype(jnp.bfloat16).reshape(-1, chans)
    down_sums = jnp.dot(active.T, mix_grad, preferred_element_type=jnp.float32)
    act_grad = jnp.dot(mix_grad, down_proj.T, preferred_element_type=jnp.float32)
    hidden_grad = (act_grad * slope).astype(jnp.bfloat16)
    up_sums = jnp.dot(flat.T, hidden_grad, preferred_element_type=jnp.float32)
    normed_grad = jnp.dot(hidden_grad, up_weight.T, preferred_element_type=jnp.float32).reshape(block_rows, block_cols, chans)
    depth_grad = norm_back(normed_grad * norm_gain.astype(jnp.float32), depth_hat, depth_rstd).astype(jnp.bfloat16)
    depth_f = depth_grad.astype(jnp.float32)
    tap_list = []
    for tap in range(49):
        tap_row = tap // 7
        tap_col = tap % 7
        tap_list.append(lax.optimization_barrier(jnp.sum(ext_rows[tap_row:tap_row + block_rows, tap_col:tap_col + block_cols] * depth_f, axis=(0, 1))))
    tap_sums = jnp.stack(tap_list)
    padded = jnp.pad(depth_f, ((6, 6), (6, 6), (0, 0)))
    back_sum = jnp.zeros((block_rows + 6, block_cols + 6, chans), jnp.float32)
    for tap in range(49):
        tap_row = tap // 7
        tap_col = tap % 7
        back_sum = back_sum + padded[6 - tap_row:12 - tap_row + block_rows, 6 - tap_col:12 - tap_col + block_cols] * taps[tap]
    return (level, direct, back_sum, (tap_sums, up_sums, down_sums, section_total))

def reference(field, land, mirror, depth_weight, norm_gain, up_weight, up_bias, down_proj, layer_scale, section_gain, section_weight, section_bias, cotangent):
    x_full = field.astype(jnp.float32)
    fold = jnp.take(x_full[ROWS - 3:][::-1], mirror, axis=1)
    core = jnp.concatenate([jnp.zeros((3, LON, C), jnp.float32), x_full, fold], axis=0)
    extended = jnp.concatenate([core[:, LON - 3:], core, core[:, :3]], axis=1)
    taps = depth_weight.astype(jnp.float32)

    def step(carry, index):
        grad_ext, acc_taps, acc_up, acc_down, acc_section = carry
        start = (index * 8).astype(jnp.int32)
        ext_rows = lax.dynamic_slice_in_dim(extended, start, 14, 0)
        x_rows = lax.dynamic_slice_in_dim(field, start, 8, 0)
        land_rows = lax.dynamic_slice_in_dim(land, start, 8, 0).astype(jnp.float32)[:, :, None]
        cot_rows = lax.dynamic_slice_in_dim(cotangent, index.astype(jnp.int32), 1, 0)
        out_rows, direct, back_sum, grads = block_pass(ext_rows, x_rows, land_rows, cot_rows, taps, norm_gain, up_weight, up_bias, down_proj, layer_scale, section_gain, section_weight, section_bias)
        old = lax.dynamic_slice_in_dim(grad_ext, start, 14, 0)
        grad_ext = lax.dynamic_update_slice_in_dim(grad_ext, old + back_sum, start, 0)
        carry = (grad_ext, acc_taps + grads[0], acc_up + grads[1], acc_down + grads[2], acc_section + grads[3])
        return (carry, (out_rows, direct))
    start_carry = (jnp.zeros((ROWS + 6, LON + 6, C), jnp.float32), jnp.zeros((49, C), jnp.float32), jnp.zeros((C, HID), jnp.float32), jnp.zeros((HID, C), jnp.float32), jnp.zeros((SECTIONS, 4 * C, C), jnp.float32))
    carry, stacked = lax.scan(step, start_carry, jnp.arange(ROWS // 8, dtype=jnp.int32))
    bottleneck = stacked[0].reshape(ROWS // 8, LON // 8, C)
    direct_all = stacked[1].reshape(ROWS, LON, C)
    grad_ext = carry[0]
    core_grad = grad_ext[:, 3:3 + LON]
    core_grad = core_grad.at[:, LON - 3:].add(grad_ext[:, :3])
    core_grad = core_grad.at[:, :3].add(grad_ext[:, LON + 3:])
    grad_x = core_grad[3:3 + ROWS]
    fold_grad = lax.optimization_barrier(core_grad[ROWS + 3:ROWS + 6].astype(jnp.bfloat16)).astype(jnp.float32)
    for level_k in range(3):
        grad_x = grad_x.at[ROWS - 1 - level_k, mirror].add(fold_grad[level_k])
    grad_field = (direct_all + grad_x).astype(jnp.bfloat16)
    factor = 1.0 / math.sqrt(ROWS * LON / 64.0)
    return (bottleneck, grad_field, carry[1] * factor, carry[2] * factor, carry[3] * factor, carry[4] * factor)
```

```python
import functools
import math

import jax
import jax.numpy as jnp
from jax import lax
from jax.experimental import pallas as pl
from jax.experimental.pallas import tpu as pltpu
from jax.sharding import PartitionSpec as P

MESH = pl.DeviceIdType.MESH
F32 = jnp.float32
BF16 = jnp.bfloat16
epsilon = 1e-06

G = 16
RR = 8
CC = 32
C = 128
PITCH = 48
EC = CC + 6
ER = RR + 6
NZ = 8
NH = 8
M = 256
CHUNKS = RR * CC * G // M
POS = M // G


def norm_parts(values):
    center = values - jnp.mean(values, axis=-1, keepdims=True)
    rstd = lax.rsqrt(jnp.mean(center * center, axis=-1, keepdims=True) + epsilon)
    return center * rstd, rstd


def norm_back(grad_hat, normed_hat, rstd):
    first = jnp.mean(grad_hat, axis=-1, keepdims=True)
    second = jnp.mean(grad_hat * normed_hat, axis=-1, keepdims=True)
    return rstd * (grad_hat - first - normed_hat * second)


def gelu_parts(h):
    e = jnp.exp(h * h * -0.5)
    t = 1.0 / (1.0 + jnp.abs(h) * 0.23164189)
    q = ((((0.5307027145 * t - 0.726576013) * t + 0.7107068705) * t - 0.142248368) * t + 0.127414796) * t
    q = q * e
    cdf = jnp.where(h >= 0.0, 1.0 - q, q)
    return h * cdf, cdf + h * (e * 0.3989422804014327)


def dot(a, b, ca, cb):
    return lax.dot_general(a, b, (((ca,), (cb,)), ((), ())), preferred_element_type=F32)


def rows(start, size, align=16):
    return pl.ds(pl.multiple_of(start, align), size)


def kernel(
    factor,
    mirror,
    field,
    land,
    taps_in,
    gain_in,
    up,
    bias_in,
    down,
    scale_in,
    sgain_in,
    sw,
    sbias_in,
    cot,
    bott,
    gfield,
    gtaps,
    gup,
    gdown,
    gsec,
    fbuf,
    ext,
    ext2,
    obuf,
    sh,
    wb,
    hat,
    rstd,
    normed,
    act,
    slope,
    landb,
    lev0,
    lev1,
    lev2,
    hat1,
    rstd1,
    hat2,
    rstd2,
    hat3,
    rstd3,
    p1,
    p2,
    p3,
    back1,
    back2,
    direct,
    dgb,
    upacc,
    dtacc,
    secacc,
    tapacc,
    a32,
    s1,
    r1,
    s2f,
    s2,
    r2,
    s3,
    r3,
    r4,
    g3,
    g2,
    g1a,
    g1b,
    tl,
    th,
    tz,
    stl,
    str_,
    cl,
    cr,
    rs,
    rn,
    csl,
    csr,
    cnl,
    cnr,
    dcl,
    dcr,
    rst,
    rsb,
    drs,
    drn,
    dsl,
    dsr,
    dnl,
    dnr,
    fr1,
    fs2,
    fr2,
    fcat,
    zbuf,
    fg,
    hr1,
    hs2,
    hr2,
    ssem,
    rsem,
):
    lat = lax.axis_index("lat")
    lon = lax.axis_index("lon")
    hi, z = lon // NZ, lax.rem(lon, NZ)
    core, xl = lax.rem(lat, 2), lat // 2
    right, left = lax.rem(lon + 1, NH * NZ), lax.rem(lon + NH * NZ - 1, NH * NZ)
    north, south = lat == 3, lat == 0

    counter = [0]

    def take(n):
        counter[0] += n
        return counter[0] - n

    def remote(src, dst, sem, to):
        return pltpu.make_async_remote_copy(
            src_ref=src,
            dst_ref=dst,
            send_sem=ssem.at[sem],
            recv_sem=rsem.at[sem],
            device_id=to,
            device_id_type=MESH,
        )

    def hi_peer(j):
        h = lax.rem(hi + j, NH)
        return h, (lat, h * NZ + z)

    def z_peer(j):
        t = lax.rem(z + j, NZ)
        return t, (lat, hi * NZ + t)

    barrier = pltpu.get_barrier_semaphore()

    def greet(to):
        pl.semaphore_signal(barrier, inc=1, device_id=to, device_id_type=MESH)

    greet((lat, left))
    greet((lat, right))
    for dl in (-1, 1):

        @pl.when((lat + dl >= 0) & (lat + dl < 4))
        def _():
            greet((lat + dl, left))
            greet((lat + dl, right))

    for j in range(1, 4):
        greet((lax.rem(lat + j, 4), lon))
    for j in range(1, NH):
        greet(hi_peer(j)[1])
    for j in range(1, NZ):
        greet(z_peer(j)[1])

    @pl.loop(0, 128)
    def _(i):
        fbuf[rows((i + 3) * PITCH + 8, CC, 8), :] = field[i].astype(F32)

    for j in range(3):
        stl[j] = fbuf[pl.ds(3 * PITCH + 8 + j, 128, stride=PITCH), :].astype(BF16)
        str_[j] = fbuf[pl.ds(3 * PITCH + 8 + CC - 3 + j, 128, stride=PITCH), :].astype(BF16)

    waits = 2 + 3 + (NH - 1) + (NZ - 1)
    pl.semaphore_wait(barrier, waits + jnp.where(south | north, 2, 4))

    def halo_copies(pieces):
        made = []
        for dl, dn, src, dst in pieces:
            sem = take(1)
            to_lon = right if dn == 1 else left if dn == -1 else lon
            copy = remote(src, dst, sem, (lat + dl, to_lon))
            made.append((dl, copy))
        return made

    def when_lat(dl, ok, fn):
        if dl == 0:
            fn()
        else:
            pl.when(ok)(fn)

    def halo_start(made):
        for dl, copy in made:
            when_lat(dl, (lat + dl >= 0) & (lat + dl < 4), copy.start)

    def halo_wait(made):
        for dl, copy in made:
            when_lat(dl, (lat + dl >= 0) & (lat + dl < 4), copy.wait_send)
            when_lat(dl, (lat - dl >= 0) & (lat - dl < 4), copy.wait_recv)

    halo = halo_copies(
        [
            (0, -1, stl, cr),
            (0, 1, str_, cl),
            (1, 0, field.at[pl.ds(125, 3)], rs),
            (-1, 0, field.at[pl.ds(0, 3)], rn),
            (1, 1, str_.at[:, pl.ds(112, 16)], csl),
            (1, -1, stl.at[:, pl.ds(112, 16)], csr),
            (-1, 1, str_.at[:, pl.ds(0, 16)], cnl),
            (-1, -1, stl.at[:, pl.ds(0, 16)], cnr),
        ]
    )
    halo_start(halo)

    shift = mirror[0]
    total = NH * NZ * CC

    def first_block(dev, width):
        base = lax.rem(shift - CC * dev - (width - 1) + (3 if width > CC else 0) + 2 * total, total)
        return base // CC, lax.rem(base, CC)

    def fold_exchange(src, buf1, stage2, buf2, width):
        sem1, sem2 = take(NH - 1), take(NZ - 1)

        def first():
            for j in range(1, NH):
                remote(src, buf1.at[hi], sem1 + j - 1, hi_peer(j)[1]).start()
            buf1[hi] = src[...]

        def held(dev):
            q = first_block(dev, width)[0]
            block = lax.rem(q + lax.rem(z + NH * NZ - q, NZ), NH * NZ)
            return block // NZ

        def second():
            for j in range(1, NH):
                h = lax.rem(hi + NH - j, NH)
                copy = remote(src, buf1.at[h], sem1 + j - 1, hi_peer(j)[1])
                copy.wait_send()
                copy.wait_recv()
            for j in range(1, NZ):
                t, to = z_peer(j)
                stage2[j - 1] = buf1[held(hi * NZ + t)]
                remote(stage2.at[j - 1], buf2.at[z], sem2 + j - 1, to).start()
            buf2[z] = buf1[held(lon)]

        def last():
            for j in range(1, NZ):
                t = lax.rem(z + NZ - j, NZ)
                copy = remote(stage2.at[j - 1], buf2.at[t], sem2 + j - 1, z_peer(j)[1])
                copy.wait_send()
                copy.wait_recv()
            q, off = first_block(lon, width)
            for m in range(3 if width > CC else 2):
                fcat[:, pl.ds(m * CC, CC), :] = buf2[lax.rem(q + m, NZ)].astype(F32)
            return off

        return first, second, last

    fold1, fold2, fold3 = fold_exchange(field.at[pl.ds(125, 3)], fr1, fs2, fr2, CC + 6)
    pl.when(north)(fold1)

    tapf = taps_in[...].astype(F32)
    for t in range(49):
        wb[t] = jnp.broadcast_to(tapf[t : t + 1], (G, C))
    gain = gain_in[...].astype(F32)
    bias = bias_in[...].astype(F32)
    scale = scale_in[...].astype(F32)

    @pl.loop(0, CHUNKS)
    def _(k):
        turned = pltpu.roll(land[...], lax.rem(256 - k * POS, 256), 1)
        for j in range(POS):
            landb[rows((k * POS + j) * G, G), :] = jnp.broadcast_to(turned[:, j : j + 1], (G, C))

    def gather_rows(r0, r1, c0, c1):
        @pl.loop(r0, r1)
        def _(r):
            for c in range(c0, c1):
                ext[rows((r * EC + c) * G, G), :] = fbuf[
                    pl.ds(r * PITCH + 5 + c, G, stride=RR * PITCH), :
                ]

    halo_wait(halo)
    for j in range(3):
        fbuf[pl.ds(3 * PITCH + 5 + j, 128, stride=PITCH), :] = cl[j].astype(F32)
        fbuf[pl.ds(3 * PITCH + 8 + CC + j, 128, stride=PITCH), :] = cr[j].astype(F32)

    @pl.when(south)
    def _():
        fbuf[pl.ds(0, 3 * PITCH), :] = jnp.zeros((3 * PITCH, C), F32)

    @pl.when(jnp.logical_not(south))
    def _():
        for k in range(3):
            fbuf[pl.ds(k * PITCH + 8, CC), :] = rs[k].astype(F32)
            for j in range(3):
                fbuf[pl.ds(k * PITCH + 5 + j, 1), :] = csl[j].astype(F32)[13 + k : 14 + k]
                fbuf[pl.ds(k * PITCH + 8 + CC + j, 1), :] = csr[j].astype(F32)[13 + k : 14 + k]

    @pl.when(jnp.logical_not(north))
    def _():
        for k in range(3):
            fbuf[pl.ds((131 + k) * PITCH + 8, CC), :] = rn[k].astype(F32)
            for j in range(3):
                fbuf[pl.ds((131 + k) * PITCH + 5 + j, 1), :] = cnl[j].astype(F32)[k : k + 1]
                fbuf[pl.ds((131 + k) * PITCH + 8 + CC + j, 1), :] = cnr[j].astype(F32)[k : k + 1]

    gather_rows(0, 11, 0, EC)
    pl.when(north)(fold2)

    def conv(src, r, cb, flip):
        total_ = None
        for a in range(7):
            for b in range(7):
                t = 48 - (7 * a + b) if flip else 7 * a + b
                x = src[rows(((r + a) * EC + cb * 8 + b) * G, 8 * G), :].reshape(8, G, C)
                term = x * wb[t][None]
                total_ = term if total_ is None else total_ + term
        return total_

    def depth_rows(r0, r1):
        @pl.loop(r0, r1)
        def _(r):
            @pl.loop(0, 4)
            def _(cb):
                h, s = norm_parts(conv(ext, r, cb, False).reshape(8 * G, C))
                at = rows((r * CC + cb * 8) * G, 8 * G)
                hat[at, :] = h
                rstd[at, :] = jnp.broadcast_to(s, h.shape)
                normed[at, :] = (h * gain).astype(BF16)

    depth_rows(0, 5)

    @pl.when(north)
    def _():
        off = fold3()
        for k in range(3):
            for i in range(EC):
                fbuf[pl.ds((131 + k) * PITCH + 5 + i, 1), :] = fcat[2 - k, pl.ds(off + EC - 1 - i, 1), :]

    gather_rows(11, 14, 0, EC)
    depth_rows(5, 8)

    @pl.loop(0, CHUNKS)
    def _(k):
        at = rows(k * M, M)
        r, c0 = k // 2, lax.rem(k, 2) * POS
        h = dot(normed[at, :], up[...], 1, 0) + bias
        active, slp = gelu_parts(h)
        active = active.astype(BF16)
        act[at, :] = active
        slope[at, :] = slp.astype(BF16)
        mixed = dot(active, down[...], 1, 0)
        x = ext[rows(((r + 3) * EC + 3 + c0) * G, M), :]
        lev0[at, :] = (landb[at, :] * (x + scale * mixed)).astype(BF16)

    def section(s, count, cols, src, hats, rstds, patches, put):
        sg = sgain_in[s : s + 1].astype(F32)
        sb = sbias_in[s : s + 1].astype(F32)
        n = cols * G
        half = cols // 2

        def step(i):
            parts = []
            for a in range(2):
                at = rows((2 * i + a) * n, n)
                h, rs_ = norm_parts(src[at, :].astype(F32))
                hats[at, :] = h
                rstds[at, :] = jnp.broadcast_to(rs_, h.shape)
                sn = (h * sg).astype(BF16).reshape(half, 2, G, C)
                parts += [sn[:, b].reshape(half * G, C) for b in range(2)]
            p = jnp.concatenate(parts, axis=1)
            patches[rows(i * half * G, half * G), :] = p
            put(i, (dot(p, sw[s], 1, 0) + sb).astype(BF16))

        if count == 1:
            step(0)
        else:
            pl.loop(0, count)(step)

    def put1(i, v):
        lev1[rows(i * 256, 256), :] = v

    def put2(i, v):
        lev2[rows(i * 128, 128), :] = v

    def put3(i, v):
        bott[...] = v

    section(0, 4, 32, lev0, hat1, rstd1, p1, put1)
    section(1, 2, 16, lev1, hat2, rstd2, p2, put2)
    section(2, 1, 8, lev2, hat3, rstd3, p3, put3)

    def section_back(s, count, cols, src, hats, rstds, patches, put):
        sg = sgain_in[s : s + 1].astype(F32)
        n = cols * G
        half = cols // 2
        secacc[s] = jnp.zeros((4 * C, C), F32)

        def step(i):
            at = rows(i * half * G, half * G)
            u = src[at, :]
            secacc[s] += dot(patches[at, :], u, 0, 0)
            spread = dot(u, sw[s], 1, 1)
            for a in range(2):
                at2 = rows((2 * i + a) * n, n)
                hh = hats[at2, :].reshape(half, 2, G, C)
                rr = rstds[at2, :].reshape(half, 2, G, C)
                outs = []
                for b in range(2):
                    q = 2 * a + b
                    g = (spread[:, q * C : (q + 1) * C] * sg).reshape(half, G, C)
                    outs.append(norm_back(g, hh[:, b], rr[:, b]).astype(BF16))
                put(at2, jnp.stack(outs, axis=1).reshape(n, C))

        if count == 1:
            step(0)
        else:
            pl.loop(0, count)(step)

    def putb2(at, v):
        back2[at, :] = v

    def putb1(at, v):
        back1[at, :] = v

    def putb0(at, v):
        direct[at, :] = (landb[at, :] * v.astype(F32)).astype(BF16)

    section_back(2, 1, 8, cot, hat3, rstd3, p3, putb2)
    section_back(1, 2, 16, back2, hat2, rstd2, p2, putb1)
    section_back(0, 4, 32, back1, hat1, rstd1, p1, putb0)

    upacc[...] = jnp.zeros_like(upacc)
    dtacc[...] = jnp.zeros_like(dtacc)

    @pl.loop(0, CHUNKS)
    def _(k):
        at = rows(k * M, M)
        r, c0 = k // 2, lax.rem(k, 2) * POS
        mg = (direct[at, :].astype(F32) * scale).astype(BF16)
        dtacc[...] += dot(mg, act[at, :], 0, 0)
        hg = (dot(mg, down[...], 1, 1) * slope[at, :].astype(F32)).astype(BF16)
        upacc[...] += dot(normed[at, :], hg, 0, 0)
        ng = dot(hg, up[...], 1, 1) * gain
        dg = norm_back(ng, hat[at, :], rstd[at, :]).astype(BF16)
        dgb[r, pl.ds(c0, POS)] = dg.reshape(POS, G, C)
        ext2[rows(((r + 3) * EC + 3 + c0) * G, M), :] = dg.astype(F32)

    for i in range(3):
        rst[i] = ext2[pl.ds(((8 + i) * EC + 3) * G + 15, CC, stride=G), :].astype(BF16)
        rsb[i] = ext2[pl.ds(((3 + i) * EC + 3) * G, CC, stride=G), :].astype(BF16)

    halo2 = halo_copies(
        [
            (0, -1, dgb.at[:, pl.ds(0, 3)], dcr),
            (0, 1, dgb.at[:, pl.ds(CC - 3, 3)], dcl),
            (1, 0, rst, drs),
            (-1, 0, rsb, drn),
            (1, 1, rst.at[:, pl.ds(16, 16)], dsl),
            (1, -1, rst.at[:, pl.ds(0, 16)], dsr),
            (-1, 1, rsb.at[:, pl.ds(16, 16)], dnl),
            (-1, -1, rsb.at[:, pl.ds(0, 16)], dnr),
        ]
    )
    halo_start(halo2)

    for q in range(4):
        a32[pl.ds(q * C, C), :] = upacc[:, q * C : (q + 1) * C]
        a32[pl.ds((4 + q) * C, C), :] = dtacc[:, q * C : (q + 1) * C].T
    for s in range(3):
        a32[pl.ds((8 + 4 * s) * C, 4 * C), :] = secacc[s]
    s1[...] = a32[...].astype(BF16)

    core_to, x_to = (lat + 1 - 2 * core, lon), (lax.rem(lat + 2, 4), lon)
    c1 = remote(s1.at[rows((1 - core) * 1280, 1280)], r1, take(1), core_to)
    c1.start()

    def sum_taps(r0, r1_):
        @pl.loop(r0, r1_)
        def _(r):
            @pl.loop(0, 4)
            def _(cb):
                d = ext2[rows(((r + 3) * EC + 3 + cb * 8) * G, 8 * G), :]
                for a in range(7):
                    for b in range(7):
                        x = ext[rows(((r + a) * EC + cb * 8 + b) * G, 8 * G), :]
                        tapacc[7 * a + b] += jnp.sum((x * d).reshape(16, 8, C), axis=0)

    tapacc[...] = jnp.zeros_like(tapacc)
    sum_taps(0, 2)

    c1.wait()
    s2f[...] = a32[rows(core * 1280, 1280), :] + r1[...].astype(F32)
    s2[...] = s2f[...].astype(BF16)
    c2 = remote(s2.at[rows((1 - xl) * 640, 640)], r2, take(1), x_to)
    c2.start()
    sum_taps(2, 4)
    c2.wait()
    s3[...] = (s2f[rows(xl * 640, 640), :] + r2[...].astype(F32)).astype(BF16)
    sem3 = take(NH - 1)
    for j in range(1, NH):
        h, to = hi_peer(j)
        remote(s3.at[rows(h * 80, 80)], r3.at[hi], sem3 + j - 1, to).start()
    r3[hi] = s3[rows(hi * 80, 80), :]
    sum_taps(4, 8)

    def tap_stage(buf, peers, me):
        sem = take(len(peers))

        def start(value):
            buf[me] = value
            for i, (_, to) in enumerate(peers):
                remote(buf.at[me], buf.at[me], sem + i, to).start()

        def finish():
            for i, (frm, to) in enumerate(peers):
                copy = remote(buf.at[me], buf.at[frm], sem + i, to)
                copy.wait_send()
                copy.wait_recv()
            out = buf[0]
            for i in range(1, buf.shape[0]):
                out = out + buf[i]
            return out

        return start, finish

    lat_peers = [(lax.rem(lat + 4 - j, 4), (lax.rem(lat + j, 4), lon)) for j in range(1, 4)]
    hi_peers = [(lax.rem(hi + NH - j, NH), hi_peer(j)[1]) for j in range(1, NH)]
    z_peers = [(lax.rem(z + NZ - j, NZ), z_peer(j)[1]) for j in range(1, NZ)]
    tl_start, tl_finish = tap_stage(tl, lat_peers, lat)
    th_start, th_finish = tap_stage(th, hi_peers, hi)
    tz_start, tz_finish = tap_stage(tz, z_peers, z)
    tl_start(jnp.concatenate([jnp.sum(tapacc[...], axis=1), jnp.zeros((15, C), F32)], axis=0))

    halo_wait(halo2)

    @pl.when(south)
    def _():
        drs[...] = jnp.zeros_like(drs)
        dsl[...] = jnp.zeros_like(dsl)
        dsr[...] = jnp.zeros_like(dsr)

    @pl.when(north)
    def _():
        drn[...] = jnp.zeros_like(drn)
        dnl[...] = jnp.zeros_like(dnl)
        dnr[...] = jnp.zeros_like(dnr)

    @pl.loop(0, RR)
    def _(r):
        for j in range(3):
            ext2[rows(((r + 3) * EC + j) * G, G), :] = dcl[r, j].astype(F32)
            ext2[rows(((r + 3) * EC + 3 + CC + j) * G, G), :] = dcr[r, j].astype(F32)

    fg1, fg2, fg3 = fold_exchange(fg, hr1, hs2, hr2, CC)

    @pl.when(north)
    def _():
        for i in range(3):
            for cut, at in ((0, 0), (8, 8), (16, 16), (24, 24), (30, 30)):
                zbuf[i, pl.ds(at, 8), :] = ext2[pl.ds(((8 + i) * EC + cut) * G + 15, 8, stride=G), :]
        for k in range(1, 4):
            total_ = None
            for a in range(k + 3, 7):
                for b in range(7):
                    term = zbuf[k - a + 5, pl.ds(6 - b, CC), :] * wb[7 * a + b][0:1]
                    total_ = term if total_ is None else total_ + term
            fg[k - 1] = total_.astype(BF16)
        fg1()

    for k in range(6):
        low = k < 3
        r = k + 5 if low else k - 3
        edge, el, er = (drs, dsl, dsr) if low else (drn, dnl, dnr)
        i = k if low else k - 3
        line = 7 if low else 24
        for c in range(EC):
            sh[pl.ds(c * 32 + 8, G), :] = ext2[pl.ds(((r + 3) * EC + c) * G, G), :]
        sh[pl.ds(3 * 32 + line, CC, stride=32), :] = edge[i].astype(F32)
        lft, rgt = el[i].astype(F32), er[i].astype(F32)
        for j in range(3):
            sh[pl.ds(j * 32 + line, 1), :] = lft[13 + j : 14 + j]
            sh[pl.ds((CC + 3 + j) * 32 + line, 1), :] = rgt[j : j + 1]
        to = k if low else k + 8
        for c in range(EC):
            ext2[pl.ds((to * EC + c) * G, G), :] = sh[pl.ds(c * 32 + (7 if low else 9), G), :]

    def grad_rows(r0, r1_):
        @pl.loop(r0, r1_)
        def _(r):
            @pl.loop(0, 4)
            def _(cb):
                v = conv(ext2, r, cb, True)
                v = v + direct[rows((r * CC + cb * 8) * G, 8 * G), :].astype(F32).reshape(8, G, C)
                for j in range(8):
                    obuf[pl.ds(r * CC + cb * 8 + j, G, stride=RR * CC), :] = v[j]

    for j in range(1, NH):
        h = lax.rem(hi + NH - j, NH)
        copy = remote(s3.at[pl.ds(0, 80)], r3.at[h], sem3 + j - 1, hi_peer(j)[1])
        copy.wait_send()
        copy.wait_recv()
    part = r3[0].astype(F32)
    for i in range(1, NH):
        part = part + r3[i].astype(F32)
    r4[z] = part.astype(BF16)
    sem4 = take(NZ - 1)
    for j in range(1, NZ):
        remote(r4.at[z], r4.at[z], sem4 + j - 1, z_peer(j)[1]).start()
    grad_rows(0, 2)

    th_start(tl_finish())
    pl.when(north)(fg2)
    for j in range(1, NZ):
        t = lax.rem(z + NZ - j, NZ)
        copy = remote(r4.at[z], r4.at[t], sem4 + j - 1, z_peer(j)[1])
        copy.wait_send()
        copy.wait_recv()
    part = r4[0].astype(F32)
    for i in range(1, NZ):
        part = part + r4[i].astype(F32)
    g3[hi] = part.astype(BF16)
    sem5 = take(NH - 1)
    for j in range(1, NH):
        remote(g3.at[hi], g3.at[hi], sem5 + j - 1, hi_peer(j)[1]).start()
    grad_rows(2, 4)

    tz_start(th_finish())
    for j in range(1, NH):
        h = lax.rem(hi + NH - j, NH)
        copy = remote(g3.at[hi], g3.at[h], sem5 + j - 1, hi_peer(j)[1])
        copy.wait_send()
        copy.wait_recv()
    x6 = remote(g3, g2, take(1), x_to)
    x7 = remote(g3, g1a, take(1), core_to)
    x8 = remote(g2, g1b, take(1), core_to)
    x6.start()
    x7.start()
    grad_rows(4, 6)
    x6.wait_recv()
    x8.start()
    gtaps[...] = tz_finish()[:49] * factor
    grad_rows(6, 8)

    @pl.when(north)
    def _():
        off = fg3()
        for k in range(1, 4):
            for i in range(CC):
                at = pl.ds((128 - k) * CC + i, 1)
                obuf[at, :] += fcat[k - 1, pl.ds(off + CC - 1 - i, 1), :]

    @pl.loop(0, 128)
    def _(i):
        gfield[i] = obuf[rows(i * CC, CC), :].astype(BF16)

    x6.wait_send()
    x7.wait()
    x8.wait()

    def place(c_, x_, v):
        a32[rows((c_ * 2 + x_) * 640, 640), :] = v.reshape(640, C).astype(F32) * factor

    place(core, xl, g3[...])
    place(core, 1 - xl, g2[...])
    place(1 - core, xl, g1a[...])
    place(1 - core, 1 - xl, g1b[...])
    for q in range(4):
        gup[:, q * C : (q + 1) * C] = a32[pl.ds(q * C, C), :]
        gdown[pl.ds(q * C, C), :] = a32[pl.ds((4 + q) * C, C), :]
    for s in range(3):
        gsec[s] = a32[pl.ds((8 + 4 * s) * C, 4 * C), :]


def on_device(field, land, mirror, depth_weight, norm_gain, up_weight, up_bias, down_proj, layer_scale, section_gain, section_weight, section_bias, cotangent):
    factor = 1.0 / math.sqrt(512 * 2048 / 64.0)
    land_t = land.astype(F32).reshape(G, RR * CC)
    cot_t = jnp.transpose(cotangent, (1, 0, 2)).reshape(4 * G, C)
    vm = pl.BlockSpec(memory_space=pltpu.VMEM)
    n = RR * CC * G

    def f(*shape):
        return pltpu.VMEM(shape, F32)

    def h(*shape):
        return pltpu.VMEM(shape, BF16)

    sems = 96
    scratch = dict(
        fbuf=f(134 * PITCH, C),
        ext=f(ER * EC * G, C),
        ext2=f(ER * EC * G, C),
        obuf=f(n, C),
        sh=f(EC * 32, C),
        wb=f(49, G, C),
        hat=f(n, C),
        rstd=f(n, C),
        normed=h(n, C),
        act=h(n, 512),
        slope=h(n, 512),
        landb=f(n, C),
        lev0=h(n, C),
        lev1=h(n // 4, C),
        lev2=h(n // 16, C),
        hat1=f(n, C),
        rstd1=f(n, C),
        hat2=f(n // 4, C),
        rstd2=f(n // 4, C),
        hat3=f(n // 16, C),
        rstd3=f(n // 16, C),
        p1=h(n // 4, 512),
        p2=h(n // 16, 512),
        p3=h(n // 64, 512),
        back1=h(n // 4, C),
        back2=h(n // 16, C),
        direct=h(n, C),
        dgb=h(RR, CC, G, C),
        upacc=f(C, 512),
        dtacc=f(C, 512),
        secacc=f(3, 512, C),
        tapacc=f(49, 8, C),
        a32=f(2560, C),
        s1=h(2560, C),
        r1=h(1280, C),
        s2f=f(1280, C),
        s2=h(1280, C),
        r2=h(640, C),
        s3=h(640, C),
        r3=h(NH, 80, C),
        r4=h(NZ, 80, C),
        g3=h(NH, 80, C),
        g2=h(NH, 80, C),
        g1a=h(NH, 80, C),
        g1b=h(NH, 80, C),
        tl=f(4, 64, C),
        th=f(NH, 64, C),
        tz=f(NZ, 64, C),
        stl=h(3, 128, C),
        str_=h(3, 128, C),
        cl=h(3, 128, C),
        cr=h(3, 128, C),
        rs=h(3, CC, C),
        rn=h(3, CC, C),
        csl=h(3, 16, C),
        csr=h(3, 16, C),
        cnl=h(3, 16, C),
        cnr=h(3, 16, C),
        dcl=h(RR, 3, G, C),
        dcr=h(RR, 3, G, C),
        rst=h(3, CC, C),
        rsb=h(3, CC, C),
        drs=h(3, CC, C),
        drn=h(3, CC, C),
        dsl=h(3, 16, C),
        dsr=h(3, 16, C),
        dnl=h(3, 16, C),
        dnr=h(3, 16, C),
        fr1=h(NH, 3, CC, C),
        fs2=h(NZ - 1, 3, CC, C),
        fr2=h(NZ, 3, CC, C),
        fcat=f(3, 3 * CC, C),
        zbuf=f(3, 40, C),
        fg=h(3, CC, C),
        hr1=h(NH, 3, CC, C),
        hs2=h(NZ - 1, 3, CC, C),
        hr2=h(NZ, 3, CC, C),
        ssem=pltpu.SemaphoreType.DMA((sems,)),
        rsem=pltpu.SemaphoreType.DMA((sems,)),
    )
    bott, gfield, gtaps, gup, gdown, gsec = pl.pallas_call(
        functools.partial(kernel, factor),
        out_shape=(
            jax.ShapeDtypeStruct((4 * G, C), BF16),
            jax.ShapeDtypeStruct((128, CC, C), BF16),
            jax.ShapeDtypeStruct((49, C), F32),
            jax.ShapeDtypeStruct((C, 512), F32),
            jax.ShapeDtypeStruct((512, C), F32),
            jax.ShapeDtypeStruct((3, 512, C), F32),
        ),
        in_specs=[pl.BlockSpec(memory_space=pltpu.SMEM)] + [vm] * 12,
        out_specs=(vm,) * 6,
        scratch_shapes=list(scratch.values()),
        compiler_params=pltpu.CompilerParams(
            collective_id=0, has_side_effects=True, vmem_limit_bytes=67043328
        ),
    )(
        mirror,
        field,
        land_t,
        depth_weight,
        norm_gain.reshape(1, C),
        up_weight,
        up_bias.reshape(1, 512),
        down_proj,
        layer_scale.reshape(1, C),
        section_gain,
        section_weight,
        section_bias,
        cot_t,
    )
    bott = jnp.transpose(bott.reshape(4, G, C), (1, 0, 2))
    return bott, gfield, gtaps, gup, gdown, gsec


def solution(mesh):
    cell = P("lat", "lon", None)
    in_specs = (cell, P("lat", "lon")) + (P(),) * 10 + (cell,)
    out_specs = (cell, cell, P(), P(), P(), P())
    return jax.shard_map(
        on_device, mesh=mesh, in_specs=in_specs, out_specs=out_specs, check_vma=False
    )
```

```python
import functools
import math

import jax
import jax.numpy as jnp
from jax import lax
from jax.experimental import pallas as pl
from jax.experimental.pallas import tpu as pltpu
from jax.sharding import PartitionSpec as P

MESH = pl.DeviceIdType.MESH
F32 = jnp.float32
BF16 = jnp.bfloat16
epsilon = 1e-06

G = 16
RR = 8
CC = 32
C = 128
PITCH = 48
EC = CC + 6
ER = RR + 6
NZ = 8
NH = 8
M = 512
CHUNKS = RR * CC * G // M
POS = M // G


def mean_mx(values):
    ones = jnp.full((C, C), 1.0 / C, BF16)
    return dot(values.astype(BF16), ones, 1, 0)


def norm_parts(values, exact=False):
    mean = mean_mx(values) if exact else jnp.mean(values, axis=-1, keepdims=True)
    center = values - mean
    rstd = lax.rsqrt(mean_mx(center * center) + epsilon)
    return center * rstd, rstd


def norm_back(grad_hat, normed_hat, rstd):
    return rstd * (grad_hat - mean_mx(grad_hat) - normed_hat * mean_mx(grad_hat * normed_hat))


def gelu_parts(h):
    h = h.astype(BF16)
    e = jnp.exp2(h * h * jnp.asarray(-0.7213475204444817, BF16))
    cdf = jnp.asarray(0.5, BF16) + jnp.asarray(0.5, BF16) * lax.erf(h * jnp.asarray(0.7071067811865476, BF16))
    return h * cdf, cdf + h * (e * jnp.asarray(0.3989422804014327, BF16))


def tree(terms):
    while len(terms) > 1:
        terms = [a + b for a, b in zip(terms[::2], terms[1::2])] + terms[len(terms) & ~1 :]
    return terms[0]


def dot(a, b, ca, cb):
    return lax.dot_general(a, b, (((ca,), (cb,)), ((), ())), preferred_element_type=F32)


def rows(start, size, align=16):
    return pl.ds(pl.multiple_of(start, align), size)


def kernel(
    factor,
    mirror,
    field,
    land,
    taps_in,
    gain_in,
    up,
    bias_in,
    down,
    scale_in,
    sgain_in,
    sw,
    sbias_in,
    cot,
    bott,
    gfield,
    gtaps,
    gup,
    gdown,
    gsec,
    fbuf,
    d32,
    obuf,
    sh,
    hat,
    rstd,
    landb,
    hat1,
    rstd1,
    hat2,
    rstd2,
    hat3,
    rstd3,
    dgb,
    upacc,
    dtacc,
    secacc,
    tapacc,
    a32,
    s1,
    r1,
    s2f,
    s2,
    r2,
    s3,
    r3,
    r4,
    g3,
    g2,
    g1a,
    g1b,
    tl,
    th,
    tz,
    stl,
    str_,
    cl,
    cr,
    rs,
    rn,
    csl,
    csr,
    cnl,
    cnr,
    dcl,
    dcr,
    rst,
    rsb,
    drs,
    drn,
    dsl,
    dsr,
    dnl,
    dnr,
    fr1,
    fs2,
    fr2,
    fcat,
    zbuf,
    fg,
    hr1,
    hs2,
    hr2,
    ssem,
    rsem,
    ext,
    ext2,
    wb,
    normed,
    act,
    slope,
    lev0,
    lev1,
    lev2,
    p1,
    p2,
    p3,
    back1,
    back2,
    direct,
):
    lat = lax.axis_index("lat")
    lon = lax.axis_index("lon")
    hi, z = lon // NZ, lax.rem(lon, NZ)
    core, xl = lax.rem(lat, 2), lat // 2
    right, left = lax.rem(lon + 1, NH * NZ), lax.rem(lon + NH * NZ - 1, NH * NZ)
    north, south = lat == 3, lat == 0

    counter = [0]

    def take(n):
        counter[0] += n
        return counter[0] - n

    def remote(src, dst, sem, to):
        return pltpu.make_async_remote_copy(
            src_ref=src,
            dst_ref=dst,
            send_sem=ssem.at[sem],
            recv_sem=rsem.at[sem],
            device_id=to,
            device_id_type=MESH,
        )

    def hi_peer(j):
        h = lax.rem(hi + j, NH)
        return h, (lat, h * NZ + z)

    def z_peer(j):
        t = lax.rem(z + j, NZ)
        return t, (lat, hi * NZ + t)

    barrier = pltpu.get_barrier_semaphore()

    def greet(to):
        pl.semaphore_signal(barrier, inc=1, device_id=to, device_id_type=MESH)

    greet((lat, left))
    greet((lat, right))
    for dl in (-1, 1):

        @pl.when((lat + dl >= 0) & (lat + dl < 4))
        def _():
            greet((lat + dl, left))
            greet((lat + dl, right))

    for j in range(1, 4):
        greet((lax.rem(lat + j, 4), lon))
    for j in range(1, NH):
        greet(hi_peer(j)[1])
    for j in range(1, NZ):
        greet(z_peer(j)[1])

    @pl.loop(0, 128)
    def _(i):
        fbuf[rows((i + 3) * PITCH + 8, CC, 8), :] = field[i].astype(F32)

    for j in range(3):
        stl[j] = fbuf[pl.ds(3 * PITCH + 8 + j, 128, stride=PITCH), :].astype(BF16)
        str_[j] = fbuf[pl.ds(3 * PITCH + 8 + CC - 3 + j, 128, stride=PITCH), :].astype(BF16)

    waits = 2 + 3 + (NH - 1) + (NZ - 1)
    pl.semaphore_wait(barrier, waits + jnp.where(south | north, 2, 4))

    def halo_copies(pieces):
        made = []
        for dl, dn, src, dst in pieces:
            sem = take(1)
            to_lon = right if dn == 1 else left if dn == -1 else lon
            copy = remote(src, dst, sem, (lat + dl, to_lon))
            made.append((dl, copy))
        return made

    def when_lat(dl, ok, fn):
        if dl == 0:
            fn()
        else:
            pl.when(ok)(fn)

    def halo_start(made):
        for dl, copy in made:
            when_lat(dl, (lat + dl >= 0) & (lat + dl < 4), copy.start)

    def halo_wait(made):
        for dl, copy in made:
            when_lat(dl, (lat + dl >= 0) & (lat + dl < 4), copy.wait_send)
            when_lat(dl, (lat - dl >= 0) & (lat - dl < 4), copy.wait_recv)

    halo = halo_copies(
        [
            (0, -1, stl, cr),
            (0, 1, str_, cl),
            (1, 0, field.at[pl.ds(125, 3)], rs),
            (-1, 0, field.at[pl.ds(0, 3)], rn),
            (1, 1, str_.at[:, pl.ds(112, 16)], csl),
            (1, -1, stl.at[:, pl.ds(112, 16)], csr),
            (-1, 1, str_.at[:, pl.ds(0, 16)], cnl),
            (-1, -1, stl.at[:, pl.ds(0, 16)], cnr),
        ]
    )
    halo_start(halo)

    shift = mirror[0]
    total = NH * NZ * CC

    def first_block(dev, width):
        base = lax.rem(shift - CC * dev - (width - 1) + (3 if width > CC else 0) + 2 * total, total)
        return base // CC, lax.rem(base, CC)

    def fold_exchange(src, buf1, stage2, buf2, width):
        sem1, sem2 = take(NH - 1), take(NZ - 1)

        def first():
            for j in range(1, NH):
                remote(src, buf1.at[hi], sem1 + j - 1, hi_peer(j)[1]).start()
            buf1[hi] = src[...]

        def held(dev):
            q = first_block(dev, width)[0]
            block = lax.rem(q + lax.rem(z + NH * NZ - q, NZ), NH * NZ)
            return block // NZ

        def second():
            for j in range(1, NH):
                h = lax.rem(hi + NH - j, NH)
                copy = remote(src, buf1.at[h], sem1 + j - 1, hi_peer(j)[1])
                copy.wait_send()
                copy.wait_recv()
            for j in range(1, NZ):
                t, to = z_peer(j)
                stage2[j - 1] = buf1[held(hi * NZ + t)]
                remote(stage2.at[j - 1], buf2.at[z], sem2 + j - 1, to).start()
            buf2[z] = buf1[held(lon)]

        def last():
            for j in range(1, NZ):
                t = lax.rem(z + NZ - j, NZ)
                copy = remote(stage2.at[j - 1], buf2.at[t], sem2 + j - 1, z_peer(j)[1])
                copy.wait_send()
                copy.wait_recv()
            q, off = first_block(lon, width)
            for m in range(3 if width > CC else 2):
                fcat[:, pl.ds(m * CC, CC), :] = buf2[lax.rem(q + m, NZ)].astype(F32)
            return off

        return first, second, last

    fold1, fold2, fold3 = fold_exchange(field.at[pl.ds(125, 3)], fr1, fs2, fr2, CC + 6)
    pl.when(north)(fold1)

    tapf = taps_in[...].astype(F32)
    for t in range(49):
        wb[t] = jnp.broadcast_to(tapf[t : t + 1], (G, C)).astype(BF16)
    gain = gain_in[...].astype(F32)
    bias = bias_in[...].astype(F32)
    scale = scale_in[...].astype(F32)

    @pl.loop(0, CHUNKS)
    def _(k):
        turned = pltpu.roll(land[...], lax.rem(256 - k * POS, 256), 1)
        for j in range(POS):
            landb[rows((k * POS + j) * G, G), :] = jnp.broadcast_to(turned[:, j : j + 1], (G, C))

    def gather_rows(r0, r1, c0, c1):
        @pl.loop(r0, r1)
        def _(r):
            for c in range(c0, c1):
                ext[rows((r * EC + c) * G, G), :] = fbuf[
                    pl.ds(r * PITCH + 5 + c, G, stride=RR * PITCH), :
                ].astype(BF16)

    halo_wait(halo)
    for j in range(3):
        fbuf[pl.ds(3 * PITCH + 5 + j, 128, stride=PITCH), :] = cl[j].astype(F32)
        fbuf[pl.ds(3 * PITCH + 8 + CC + j, 128, stride=PITCH), :] = cr[j].astype(F32)

    @pl.when(south)
    def _():
        fbuf[pl.ds(0, 3 * PITCH), :] = jnp.zeros((3 * PITCH, C), F32)

    @pl.when(jnp.logical_not(south))
    def _():
        for k in range(3):
            fbuf[pl.ds(k * PITCH + 8, CC), :] = rs[k].astype(F32)
            for j in range(3):
                fbuf[pl.ds(k * PITCH + 5 + j, 1), :] = csl[j].astype(F32)[13 + k : 14 + k]
                fbuf[pl.ds(k * PITCH + 8 + CC + j, 1), :] = csr[j].astype(F32)[13 + k : 14 + k]

    @pl.when(jnp.logical_not(north))
    def _():
        for k in range(3):
            fbuf[pl.ds((131 + k) * PITCH + 8, CC), :] = rn[k].astype(F32)
            for j in range(3):
                fbuf[pl.ds((131 + k) * PITCH + 5 + j, 1), :] = cnl[j].astype(F32)[k : k + 1]
                fbuf[pl.ds((131 + k) * PITCH + 8 + CC + j, 1), :] = cnr[j].astype(F32)[k : k + 1]

    gather_rows(0, 11, 0, EC)
    pl.when(north)(fold2)

    def conv(src, r, cb, flip):
        total_ = None
        for a in range(7):
            terms = []
            for b in range(7):
                t = 48 - (7 * a + b) if flip else 7 * a + b
                x = src[rows(((r + a) * EC + cb * 8 + b) * G, 8 * G), :].reshape(8, G, C)
                terms.append(x * wb[t][None])
            term = tree(terms).astype(F32)
            total_ = term if total_ is None else total_ + term
        return total_

    def depth_rows(r0, r1):
        @pl.loop(r0, r1)
        def _(r):
            @pl.loop(0, 4)
            def _(cb):
                hat[rows((r * CC + cb * 8) * G, 8 * G), :] = conv(ext, r, cb, False).reshape(8 * G, C)

    depth_rows(0, 5)

    @pl.when(north)
    def _():
        off = fold3()
        for k in range(3):
            for i in range(EC):
                fbuf[pl.ds((131 + k) * PITCH + 5 + i, 1), :] = fcat[2 - k, pl.ds(off + EC - 1 - i, 1), :]

    gather_rows(11, 14, 0, EC)
    depth_rows(5, 8)

    @pl.loop(0, CHUNKS)
    def _(k):
        at = rows(k * M, M)
        r = k
        dh, ds = norm_parts(hat[at, :])
        hat[at, :] = dh
        rstd[at, :] = ds
        nm = (dh * gain).astype(BF16)
        normed[at, :] = nm
        active, slp = gelu_parts(dot(nm, up[...], 1, 0) + bias)
        act[at, :] = active
        slope[at, :] = slp
        mixed = dot(active, down[...], 1, 0)
        x = ext[rows(((r + 3) * EC + 3) * G, M), :].astype(F32)
        lev0[at, :] = (landb[at, :] * (x + scale * mixed)).astype(BF16)

    def section(s, count, cols, src, hats, rstds, patches, put):
        sg = sgain_in[s : s + 1].astype(F32)
        sb = sbias_in[s : s + 1].astype(F32)
        n = cols * G
        half = cols // 2

        def step(i):
            parts = []
            for a in range(2):
                at = rows((2 * i + a) * n, n)
                h, rs_ = norm_parts(src[at, :].astype(F32), True)
                hats[at, :] = h
                rstds[at, :] = rs_
                sn = (h * sg).astype(BF16).reshape(half, 2, G, C)
                parts += [sn[:, b].reshape(half * G, C) for b in range(2)]
            p = jnp.concatenate(parts, axis=1)
            patches[rows(i * half * G, half * G), :] = p
            put(i, (dot(p, sw[s], 1, 0) + sb).astype(BF16))

        if count == 1:
            step(0)
        else:
            pl.loop(0, count)(step)

    def put1(i, v):
        lev1[rows(i * 256, 256), :] = v

    def put2(i, v):
        lev2[rows(i * 128, 128), :] = v

    def put3(i, v):
        bott[...] = v

    section(0, 4, 32, lev0, hat1, rstd1, p1, put1)
    section(1, 2, 16, lev1, hat2, rstd2, p2, put2)
    section(2, 1, 8, lev2, hat3, rstd3, p3, put3)

    def section_back(s, count, cols, src, hats, rstds, patches, put):
        sg = sgain_in[s : s + 1].astype(F32)
        n = cols * G
        half = cols // 2
        secacc[s] = jnp.zeros((C, 4 * C), F32)

        def step(i):
            at = rows(i * half * G, half * G)
            u = src[at, :]
            secacc[s] += dot(u, patches[at, :], 0, 0)
            spread = dot(u, sw[s], 1, 1)
            for a in range(2):
                at2 = rows((2 * i + a) * n, n)
                hh = hats[at2, :].reshape(half, 2, G, C)
                rr = rstds[at2, :].reshape(half, 2, G, C)
                outs = []
                for b in range(2):
                    q = 2 * a + b
                    g = spread[:, q * C : (q + 1) * C] * sg
                    back = norm_back(g, hh[:, b].reshape(half * G, C), rr[:, b].reshape(half * G, C))
                    outs.append(back.astype(BF16).reshape(half, G, C))
                put(at2, jnp.stack(outs, axis=1).reshape(n, C))

        if count == 1:
            step(0)
        else:
            pl.loop(0, count)(step)

    def putb2(at, v):
        back2[at, :] = v

    def putb1(at, v):
        back1[at, :] = v

    def putb0(at, v):
        direct[at, :] = (landb[at, :] * v.astype(F32)).astype(BF16)

    section_back(2, 1, 8, cot, hat3, rstd3, p3, putb2)
    section_back(1, 2, 16, back2, hat2, rstd2, p2, putb1)
    section_back(0, 4, 32, back1, hat1, rstd1, p1, putb0)

    upacc[...] = jnp.zeros_like(upacc)
    dtacc[...] = jnp.zeros_like(dtacc)

    @pl.loop(0, CHUNKS)
    def _(k):
        at = rows(k * M, M)
        r = k
        mg = (direct[at, :].astype(F32) * scale).astype(BF16)
        dtacc[...] += dot(mg, act[at, :], 0, 0)
        hg = (dot(mg, down[...], 1, 1) * slope[at, :].astype(F32)).astype(BF16)
        upacc[...] += dot(normed[at, :], hg, 0, 0)
        ng = dot(hg, up[...], 1, 1) * gain
        dg = norm_back(ng, hat[at, :], rstd[at, :]).astype(BF16)
        dgb[r] = dg.reshape(POS, G, C)
        ext2[rows(((r + 3) * EC + 3) * G, M), :] = dg
        d32[rows((r * EC + 3) * G, M), :] = dg.astype(F32)

    for i in range(3):
        rst[i] = d32[pl.ds(((5 + i) * EC + 3) * G + 15, CC, stride=G), :].astype(BF16)
        rsb[i] = d32[pl.ds((i * EC + 3) * G, CC, stride=G), :].astype(BF16)

    halo2 = halo_copies(
        [
            (0, -1, dgb.at[:, pl.ds(0, 3)], dcr),
            (0, 1, dgb.at[:, pl.ds(CC - 3, 3)], dcl),
            (1, 0, rst, drs),
            (-1, 0, rsb, drn),
            (1, 1, rst.at[:, pl.ds(16, 16)], dsl),
            (1, -1, rst.at[:, pl.ds(0, 16)], dsr),
            (-1, 1, rsb.at[:, pl.ds(16, 16)], dnl),
            (-1, -1, rsb.at[:, pl.ds(0, 16)], dnr),
        ]
    )
    halo_start(halo2)

    for q in range(4):
        a32[pl.ds(q * C, C), :] = upacc[:, q * C : (q + 1) * C]
        a32[pl.ds((4 + q) * C, C), :] = dtacc[:, q * C : (q + 1) * C].T
    for s in range(3):
        for q in range(4):
            a32[pl.ds((8 + 4 * s + q) * C, C), :] = secacc[s, :, q * C : (q + 1) * C].T
    s1[...] = a32[...].astype(BF16)

    core_to, x_to = (lat + 1 - 2 * core, lon), (lax.rem(lat + 2, 4), lon)
    c1 = remote(s1.at[rows((1 - core) * 1280, 1280)], r1, take(1), core_to)
    c1.start()

    def sum_taps(r0, r1_):
        @pl.loop(r0, r1_)
        def _(r):
            @pl.loop(0, 4)
            def _(cb):
                d = ext2[rows(((r + 3) * EC + 3 + cb * 8) * G, 8 * G), :].reshape(8, G, C)
                for a in range(7):
                    for b in range(7):
                        x = ext[rows(((r + a) * EC + cb * 8 + b) * G, 8 * G), :]
                        p = x.reshape(8, G, C) * d
                        t = tree([p[i] for i in range(8)]).astype(F32)
                        tapacc[7 * a + b] += t[:8] + t[8:]

    tapacc[...] = jnp.zeros_like(tapacc)
    sum_taps(0, 2)

    c1.wait()
    s2f[...] = a32[rows(core * 1280, 1280), :] + r1[...].astype(F32)
    s2[...] = s2f[...].astype(BF16)
    c2 = remote(s2.at[rows((1 - xl) * 640, 640)], r2, take(1), x_to)
    c2.start()
    sum_taps(2, 4)
    c2.wait()
    s3[...] = (s2f[rows(xl * 640, 640), :] + r2[...].astype(F32)).astype(BF16)
    sem3 = take(NH - 1)
    for j in range(1, NH):
        h, to = hi_peer(j)
        remote(s3.at[rows(h * 80, 80)], r3.at[hi], sem3 + j - 1, to).start()
    r3[hi] = s3[rows(hi * 80, 80), :]
    sum_taps(4, 8)

    def tap_stage(buf, peers, me):
        sem = take(len(peers))

        def start(value):
            buf[me] = value
            for i, (_, to) in enumerate(peers):
                remote(buf.at[me], buf.at[me], sem + i, to).start()

        def finish():
            for i, (frm, to) in enumerate(peers):
                copy = remote(buf.at[me], buf.at[frm], sem + i, to)
                copy.wait_send()
                copy.wait_recv()
            out = buf[0]
            for i in range(1, buf.shape[0]):
                out = out + buf[i]
            return out

        return start, finish

    lat_peers = [(lax.rem(lat + 4 - j, 4), (lax.rem(lat + j, 4), lon)) for j in range(1, 4)]
    hi_peers = [(lax.rem(hi + NH - j, NH), hi_peer(j)[1]) for j in range(1, NH)]
    z_peers = [(lax.rem(z + NZ - j, NZ), z_peer(j)[1]) for j in range(1, NZ)]
    tl_start, tl_finish = tap_stage(tl, lat_peers, lat)
    th_start, th_finish = tap_stage(th, hi_peers, hi)
    tz_start, tz_finish = tap_stage(tz, z_peers, z)
    tl_start(jnp.concatenate([jnp.sum(tapacc[...], axis=1), jnp.zeros((15, C), F32)], axis=0))

    halo_wait(halo2)

    @pl.when(south)
    def _():
        drs[...] = jnp.zeros_like(drs)
        dsl[...] = jnp.zeros_like(dsl)
        dsr[...] = jnp.zeros_like(dsr)

    @pl.when(north)
    def _():
        drn[...] = jnp.zeros_like(drn)
        dnl[...] = jnp.zeros_like(dnl)
        dnr[...] = jnp.zeros_like(dnr)

    @pl.loop(0, RR)
    def _(r):
        for j in range(3):
            ext2[rows(((r + 3) * EC + j) * G, G), :] = dcl[r, j]
            ext2[rows(((r + 3) * EC + 3 + CC + j) * G, G), :] = dcr[r, j]
            d32[rows((r * EC + j) * G, G), :] = dcl[r, j].astype(F32)
            d32[rows((r * EC + 3 + CC + j) * G, G), :] = dcr[r, j].astype(F32)

    fg1, fg2, fg3 = fold_exchange(fg, hr1, hs2, hr2, CC)

    @pl.when(north)
    def _():
        for i in range(3):
            for cut, at in ((0, 0), (8, 8), (16, 16), (24, 24), (30, 30)):
                zbuf[i, pl.ds(at, 8), :] = d32[pl.ds(((5 + i) * EC + cut) * G + 15, 8, stride=G), :]
        for k in range(1, 4):
            total_ = None
            for a in range(k + 3, 7):
                for b in range(7):
                    term = zbuf[k - a + 5, pl.ds(6 - b, CC), :] * tapf[7 * a + b : 7 * a + b + 1]
                    total_ = term if total_ is None else total_ + term
            fg[k - 1] = total_.astype(BF16)
        fg1()

    for k in range(6):
        low = k < 3
        r = k + 5 if low else k - 3
        edge, el, er = (drs, dsl, dsr) if low else (drn, dnl, dnr)
        i = k if low else k - 3
        line = 7 if low else 24
        for c in range(EC):
            sh[pl.ds(c * 32 + 8, G), :] = d32[pl.ds((r * EC + c) * G, G), :]
        sh[pl.ds(3 * 32 + line, CC, stride=32), :] = edge[i].astype(F32)
        lft, rgt = el[i].astype(F32), er[i].astype(F32)
        for j in range(3):
            sh[pl.ds(j * 32 + line, 1), :] = lft[13 + j : 14 + j]
            sh[pl.ds((CC + 3 + j) * 32 + line, 1), :] = rgt[j : j + 1]
        to = k if low else k + 8
        for c in range(EC):
            ext2[pl.ds((to * EC + c) * G, G), :] = sh[pl.ds(c * 32 + (7 if low else 9), G), :].astype(BF16)

    def grad_rows(r0, r1_):
        @pl.loop(r0, r1_)
        def _(r):
            @pl.loop(0, 4)
            def _(cb):
                v = conv(ext2, r, cb, True)
                v = v + direct[rows((r * CC + cb * 8) * G, 8 * G), :].astype(F32).reshape(8, G, C)
                for j in range(8):
                    obuf[pl.ds(r * CC + cb * 8 + j, G, stride=RR * CC), :] = v[j]

    for j in range(1, NH):
        h = lax.rem(hi + NH - j, NH)
        copy = remote(s3.at[pl.ds(0, 80)], r3.at[h], sem3 + j - 1, hi_peer(j)[1])
        copy.wait_send()
        copy.wait_recv()
    part = r3[0].astype(F32)
    for i in range(1, NH):
        part = part + r3[i].astype(F32)
    r4[z] = part.astype(BF16)
    sem4 = take(NZ - 1)
    for j in range(1, NZ):
        remote(r4.at[z], r4.at[z], sem4 + j - 1, z_peer(j)[1]).start()
    grad_rows(0, 2)

    th_start(tl_finish())
    pl.when(north)(fg2)
    for j in range(1, NZ):
        t = lax.rem(z + NZ - j, NZ)
        copy = remote(r4.at[z], r4.at[t], sem4 + j - 1, z_peer(j)[1])
        copy.wait_send()
        copy.wait_recv()
    part = r4[0].astype(F32)
    for i in range(1, NZ):
        part = part + r4[i].astype(F32)
    g3[hi] = part.astype(BF16)
    sem5 = take(NH - 1)
    for j in range(1, NH):
        remote(g3.at[hi], g3.at[hi], sem5 + j - 1, hi_peer(j)[1]).start()
    grad_rows(2, 4)

    tz_start(th_finish())
    for j in range(1, NH):
        h = lax.rem(hi + NH - j, NH)
        copy = remote(g3.at[hi], g3.at[h], sem5 + j - 1, hi_peer(j)[1])
        copy.wait_send()
        copy.wait_recv()
    x6 = remote(g3, g2, take(1), x_to)
    x7 = remote(g3, g1a, take(1), core_to)
    x8 = remote(g2, g1b, take(1), core_to)
    x6.start()
    x7.start()
    grad_rows(4, 6)
    x6.wait_recv()
    x8.start()
    gtaps[...] = tz_finish()[:49] * factor
    grad_rows(6, 8)

    @pl.when(north)
    def _():
        off = fg3()
        for k in range(1, 4):
            for i in range(CC):
                at = pl.ds((128 - k) * CC + i, 1)
                obuf[at, :] += fcat[k - 1, pl.ds(off + CC - 1 - i, 1), :]

    @pl.loop(0, 128)
    def _(i):
        gfield[i] = obuf[rows(i * CC, CC), :].astype(BF16)

    x6.wait_send()
    x7.wait()
    x8.wait()

    def place(c_, x_, v):
        a32[rows((c_ * 2 + x_) * 640, 640), :] = v.reshape(640, C).astype(F32) * factor

    place(core, xl, g3[...])
    place(core, 1 - xl, g2[...])
    place(1 - core, xl, g1a[...])
    place(1 - core, 1 - xl, g1b[...])
    for q in range(4):
        gup[:, q * C : (q + 1) * C] = a32[pl.ds(q * C, C), :]
        gdown[pl.ds(q * C, C), :] = a32[pl.ds((4 + q) * C, C), :]
    for s in range(3):
        gsec[s] = a32[pl.ds((8 + 4 * s) * C, 4 * C), :]


def on_device(field, land, mirror, depth_weight, norm_gain, up_weight, up_bias, down_proj, layer_scale, section_gain, section_weight, section_bias, cotangent):
    factor = 1.0 / math.sqrt(512 * 2048 / 64.0)
    land_t = land.astype(F32).reshape(G, RR * CC)
    cot_t = jnp.transpose(cotangent, (1, 0, 2)).reshape(4 * G, C)
    vm = pl.BlockSpec(memory_space=pltpu.VMEM)
    n = RR * CC * G

    def f(*shape):
        return pltpu.VMEM(shape, F32)

    def h(*shape):
        return pltpu.VMEM(shape, BF16)

    sems = 96
    scratch = dict(
        fbuf=f(134 * PITCH, C),
        d32=f(RR * EC * G, C),
        obuf=f(n, C),
        sh=f(EC * 32, C),
        hat=f(n, C),
        rstd=f(n, C),
        landb=f(n, C),
        hat1=f(n, C),
        rstd1=f(n, C),
        hat2=f(n // 4, C),
        rstd2=f(n // 4, C),
        hat3=f(n // 16, C),
        rstd3=f(n // 16, C),
        dgb=h(RR, CC, G, C),
        upacc=f(C, 512),
        dtacc=f(C, 512),
        secacc=f(3, C, 512),
        tapacc=f(49, 8, C),
        a32=f(2560, C),
        s1=h(2560, C),
        r1=h(1280, C),
        s2f=f(1280, C),
        s2=h(1280, C),
        r2=h(640, C),
        s3=h(640, C),
        r3=h(NH, 80, C),
        r4=h(NZ, 80, C),
        g3=h(NH, 80, C),
        g2=h(NH, 80, C),
        g1a=h(NH, 80, C),
        g1b=h(NH, 80, C),
        tl=f(4, 64, C),
        th=f(NH, 64, C),
        tz=f(NZ, 64, C),
        stl=h(3, 128, C),
        str_=h(3, 128, C),
        cl=h(3, 128, C),
        cr=h(3, 128, C),
        rs=h(3, CC, C),
        rn=h(3, CC, C),
        csl=h(3, 16, C),
        csr=h(3, 16, C),
        cnl=h(3, 16, C),
        cnr=h(3, 16, C),
        dcl=h(RR, 3, G, C),
        dcr=h(RR, 3, G, C),
        rst=h(3, CC, C),
        rsb=h(3, CC, C),
        drs=h(3, CC, C),
        drn=h(3, CC, C),
        dsl=h(3, 16, C),
        dsr=h(3, 16, C),
        dnl=h(3, 16, C),
        dnr=h(3, 16, C),
        fr1=h(NH, 3, CC, C),
        fs2=h(NZ - 1, 3, CC, C),
        fr2=h(NZ, 3, CC, C),
        fcat=f(3, 3 * CC, C),
        zbuf=f(3, 40, C),
        fg=h(3, CC, C),
        hr1=h(NH, 3, CC, C),
        hs2=h(NZ - 1, 3, CC, C),
        hr2=h(NZ, 3, CC, C),
        ssem=pltpu.SemaphoreType.DMA((sems,)),
        rsem=pltpu.SemaphoreType.DMA((sems,)),
    )
    scoped = dict(
        ext=h(ER * EC * G, C),
        ext2=h(ER * EC * G, C),
        wb=h(49, G, C),
        normed=h(n, C),
        act=h(n, 512),
        slope=h(n, 512),
        lev0=h(n, C),
        lev1=h(n // 4, C),
        lev2=h(n // 16, C),
        p1=h(n // 4, 512),
        p2=h(n // 16, 512),
        p3=h(n // 64, 512),
        back1=h(n // 4, C),
        back2=h(n // 16, C),
        direct=h(n, C),
    )

    def whole(*refs):
        pl.run_scoped(functools.partial(kernel, factor, *refs), **scoped)

    bott, gfield, gtaps, gup, gdown, gsec = pl.pallas_call(
        whole,
        out_shape=(
            jax.ShapeDtypeStruct((4 * G, C), BF16),
            jax.ShapeDtypeStruct((128, CC, C), BF16),
            jax.ShapeDtypeStruct((49, C), F32),
            jax.ShapeDtypeStruct((C, 512), F32),
            jax.ShapeDtypeStruct((512, C), F32),
            jax.ShapeDtypeStruct((3, 512, C), F32),
        ),
        in_specs=[pl.BlockSpec(memory_space=pltpu.SMEM)] + [vm] * 12,
        out_specs=(vm,) * 6,
        scratch_shapes=list(scratch.values()),
        compiler_params=pltpu.CompilerParams(
            collective_id=0, has_side_effects=True, vmem_limit_bytes=67043328
        ),
    )(
        mirror,
        field,
        land_t,
        depth_weight,
        norm_gain.reshape(1, C),
        up_weight,
        up_bias.reshape(1, 512),
        down_proj,
        layer_scale.reshape(1, C),
        section_gain,
        section_weight,
        section_bias,
        cot_t,
    )
    bott = jnp.transpose(bott.reshape(4, G, C), (1, 0, 2))
    return bott, gfield, gtaps, gup, gdown, gsec


def solution(mesh):
    cell = P("lat", "lon", None)
    in_specs = (cell, P("lat", "lon")) + (P(),) * 10 + (cell,)
    out_specs = (cell, cell, P(), P(), P(), P())
    return jax.shard_map(
        on_device, mesh=mesh, in_specs=in_specs, out_specs=out_specs, check_vma=False
    )
```

```python
import functools
import math

import jax
import jax.numpy as jnp
from jax import lax
from jax.experimental import pallas as pl
from jax.experimental.pallas import tpu as pltpu
from jax.sharding import PartitionSpec as P

MESH = pl.DeviceIdType.MESH
F32 = jnp.float32
BF16 = jnp.bfloat16
epsilon = 1e-06

G = 16
RR = 8
CC = 32
C = 128
PITCH = 48
EC = CC + 6
ER = RR + 6
NZ = 8
NH = 8
M = 512
CHUNKS = RR * CC * G // M
POS = M // G


def mean_mx(values):
    ones = jnp.full((C, C), 1.0 / C, BF16)
    return dot(values.astype(BF16), ones, 1, 0)


def norm_parts(values, exact=False):
    mean = mean_mx(values) if exact else jnp.mean(values, axis=-1, keepdims=True)
    center = values - mean
    rstd = lax.rsqrt(mean_mx(center * center) + epsilon)
    return center * rstd, rstd


def norm_back(grad_hat, normed_hat, rstd):
    return rstd * (grad_hat - mean_mx(grad_hat) - normed_hat * mean_mx(grad_hat * normed_hat))


def gelu_parts(h):
    h = h.astype(BF16)
    e = jnp.exp2(h * h * jnp.asarray(-0.7213475204444817, BF16))
    cdf = jnp.asarray(0.5, BF16) + jnp.asarray(0.5, BF16) * lax.erf(h * jnp.asarray(0.7071067811865476, BF16))
    return h * cdf, cdf + h * (e * jnp.asarray(0.3989422804014327, BF16))


def tree(terms):
    while len(terms) > 1:
        terms = [a + b for a, b in zip(terms[::2], terms[1::2])] + terms[len(terms) & ~1 :]
    return terms[0]


def dot(a, b, ca, cb):
    return lax.dot_general(a, b, (((ca,), (cb,)), ((), ())), preferred_element_type=F32)


def rows(start, size, align=16):
    return pl.ds(pl.multiple_of(start, align), size)


def kernel(
    factor,
    mirror,
    x_field,
    x_land,
    x_taps_in,
    x_gain_in,
    x_up,
    x_bias_in,
    x_down,
    x_scale_in,
    x_sgain_in,
    x_sw,
    x_sbias_in,
    x_cot,
    bott,
    gfield,
    gtaps,
    gup,
    gdown,
    gsec,
    field,
    land,
    taps_in,
    gain_in,
    up,
    bias_in,
    down,
    scale_in,
    sgain_in,
    sw,
    sbias_in,
    cot,
    lsem,
    fbuf,
    d32,
    obuf,
    sh,
    hat,
    rstd,
    landb,
    hat1,
    rstd1,
    hat2,
    rstd2,
    hat3,
    rstd3,
    dgb,
    upacc,
    dtacc,
    secacc,
    tapacc,
    lt,
    cb32,
    cotb,
    asec,
    aden,
    sec_s1,
    sec_r1,
    sec_s2f,
    sec_s2,
    sec_r2,
    sec_s3,
    sec_r3,
    sec_r4,
    sec_g3,
    sec_g2,
    sec_g1a,
    sec_g1b,
    den_s1,
    den_r1,
    den_s2f,
    den_s2,
    den_r2,
    den_s3,
    den_r3,
    den_r4,
    den_g3,
    den_g2,
    den_g1a,
    den_g1b,
    tl,
    th,
    tz,
    stl,
    str_,
    cl,
    cr,
    rs,
    rn,
    csl,
    csr,
    cnl,
    cnr,
    dcl,
    dcr,
    rst,
    rsb,
    drs,
    drn,
    dsl,
    dsr,
    dnl,
    dnr,
    fr1,
    fs2,
    fr2,
    fcat,
    zbuf,
    fg,
    hr1,
    hs2,
    hr2,
    ssem,
    rsem,
    ext,
    ext2,
    wb,
    normed,
    act,
    slope,
    lev0,
    lev1,
    lev2,
    p1,
    p2,
    p3,
    back1,
    back2,
    direct,
):
    loads = [
        pltpu.make_async_copy(a, b, lsem.at[i])
        for i, (a, b) in enumerate(
            (
                (x_field, field),
                (x_land, land),
                (x_taps_in, taps_in),
                (x_gain_in, gain_in),
                (x_up, up),
                (x_bias_in, bias_in),
                (x_down, down),
                (x_scale_in, scale_in),
                (x_sgain_in, sgain_in),
                (x_sw, sw),
                (x_sbias_in, sbias_in),
                (x_cot, cot),
            )
        )
    ]
    for copy in loads:
        copy.start()

    lat = lax.axis_index("lat")
    lon = lax.axis_index("lon")
    hi, z = lon // NZ, lax.rem(lon, NZ)
    core, xl = lax.rem(lat, 2), lat // 2
    right, left = lax.rem(lon + 1, NH * NZ), lax.rem(lon + NH * NZ - 1, NH * NZ)
    north, south = lat == 3, lat == 0

    counter = [0]

    def take(n):
        counter[0] += n
        return counter[0] - n

    def remote(src, dst, sem, to):
        return pltpu.make_async_remote_copy(
            src_ref=src,
            dst_ref=dst,
            send_sem=ssem.at[sem],
            recv_sem=rsem.at[sem],
            device_id=to,
            device_id_type=MESH,
        )

    def hi_peer(j):
        h = lax.rem(hi + j, NH)
        return h, (lat, h * NZ + z)

    def z_peer(j):
        t = lax.rem(z + j, NZ)
        return t, (lat, hi * NZ + t)

    barrier = pltpu.get_barrier_semaphore()

    def greet(to):
        pl.semaphore_signal(barrier, inc=1, device_id=to, device_id_type=MESH)

    greet((lat, left))
    greet((lat, right))
    for dl in (-1, 1):

        @pl.when((lat + dl >= 0) & (lat + dl < 4))
        def _():
            greet((lat + dl, left))
            greet((lat + dl, right))

    for j in range(1, 4):
        greet((lax.rem(lat + j, 4), lon))
    for j in range(1, NH):
        greet(hi_peer(j)[1])
    for j in range(1, NZ):
        greet(z_peer(j)[1])

    loads[0].wait()

    @pl.loop(0, 128)
    def _(i):
        fbuf[rows((i + 3) * PITCH + 8, CC, 8), :] = field[i].astype(F32)

    for j in range(3):
        stl[j] = fbuf[pl.ds(3 * PITCH + 8 + j, 128, stride=PITCH), :].astype(BF16)
        str_[j] = fbuf[pl.ds(3 * PITCH + 8 + CC - 3 + j, 128, stride=PITCH), :].astype(BF16)

    waits = 2 + 3 + (NH - 1) + (NZ - 1)
    pl.semaphore_wait(barrier, waits + jnp.where(south | north, 2, 4))

    def halo_copies(pieces):
        made = []
        for dl, dn, src, dst in pieces:
            sem = take(1)
            to_lon = right if dn == 1 else left if dn == -1 else lon
            copy = remote(src, dst, sem, (lat + dl, to_lon))
            made.append((dl, copy))
        return made

    def when_lat(dl, ok, fn):
        if dl == 0:
            fn()
        else:
            pl.when(ok)(fn)

    def halo_start(made):
        for dl, copy in made:
            when_lat(dl, (lat + dl >= 0) & (lat + dl < 4), copy.start)

    def halo_wait(made):
        for dl, copy in made:
            when_lat(dl, (lat + dl >= 0) & (lat + dl < 4), copy.wait_send)
            when_lat(dl, (lat - dl >= 0) & (lat - dl < 4), copy.wait_recv)

    halo = halo_copies(
        [
            (0, -1, stl, cr),
            (0, 1, str_, cl),
            (1, 0, field.at[pl.ds(125, 3)], rs),
            (-1, 0, field.at[pl.ds(0, 3)], rn),
            (1, 1, str_.at[:, pl.ds(112, 16)], csl),
            (1, -1, stl.at[:, pl.ds(112, 16)], csr),
            (-1, 1, str_.at[:, pl.ds(0, 16)], cnl),
            (-1, -1, stl.at[:, pl.ds(0, 16)], cnr),
        ]
    )
    halo_start(halo)

    shift = mirror[0]
    total = NH * NZ * CC

    def first_block(dev, width):
        base = lax.rem(shift - CC * dev - (width - 1) + (3 if width > CC else 0) + 2 * total, total)
        return base // CC, lax.rem(base, CC)

    def fold_exchange(src, buf1, stage2, buf2, width):
        sem1, sem2 = take(NH - 1), take(NZ - 1)

        def first():
            for j in range(1, NH):
                remote(src, buf1.at[hi], sem1 + j - 1, hi_peer(j)[1]).start()
            buf1[hi] = src[...]

        def held(dev):
            q = first_block(dev, width)[0]
            block = lax.rem(q + lax.rem(z + NH * NZ - q, NZ), NH * NZ)
            return block // NZ

        def second():
            for j in range(1, NH):
                h = lax.rem(hi + NH - j, NH)
                copy = remote(src, buf1.at[h], sem1 + j - 1, hi_peer(j)[1])
                copy.wait_send()
                copy.wait_recv()
            for j in range(1, NZ):
                t, to = z_peer(j)
                stage2[j - 1] = buf1[held(hi * NZ + t)]
                remote(stage2.at[j - 1], buf2.at[z], sem2 + j - 1, to).start()
            buf2[z] = buf1[held(lon)]

        def last():
            for j in range(1, NZ):
                t = lax.rem(z + NZ - j, NZ)
                copy = remote(stage2.at[j - 1], buf2.at[t], sem2 + j - 1, z_peer(j)[1])
                copy.wait_send()
                copy.wait_recv()
            q, off = first_block(lon, width)
            for m in range(3 if width > CC else 2):
                fcat[:, pl.ds(m * CC, CC), :] = buf2[lax.rem(q + m, NZ)].astype(F32)
            return off

        return first, second, last

    fold1, fold2, fold3 = fold_exchange(field.at[pl.ds(125, 3)], fr1, fs2, fr2, CC + 6)
    pl.when(north)(fold1)

    for copy in loads[1:]:
        copy.wait()

    tapf = taps_in[...].astype(F32)
    for t in range(49):
        wb[t] = jnp.broadcast_to(tapf[t : t + 1], (G, C)).astype(BF16)
    gain = gain_in[...].astype(F32)
    bias = bias_in[...].astype(F32).reshape(1, 512)
    scale = scale_in[...].astype(F32)

    lt[...] = jnp.concatenate([land[...].astype(F32), jnp.zeros((C - CC, C), F32)], axis=0).T

    @pl.loop(0, RR)
    def _(r):
        v = lt[pl.ds(r, G, stride=RR), :]
        for c in range(CC):
            landb[rows((r * CC + c) * G, G), :] = jnp.broadcast_to(v[:, c : c + 1], (G, C))

    for g in range(G):
        cb32[pl.ds(g, 4, stride=G), :] = cot[g].astype(F32)
    cotb[...] = cb32[...].astype(BF16)

    def gather_rows(r0, r1, c0, c1):
        @pl.loop(r0, r1)
        def _(r):
            for c in range(c0, c1):
                ext[rows((r * EC + c) * G, G), :] = fbuf[
                    pl.ds(r * PITCH + 5 + c, G, stride=RR * PITCH), :
                ].astype(BF16)

    halo_wait(halo)
    for j in range(3):
        fbuf[pl.ds(3 * PITCH + 5 + j, 128, stride=PITCH), :] = cl[j].astype(F32)
        fbuf[pl.ds(3 * PITCH + 8 + CC + j, 128, stride=PITCH), :] = cr[j].astype(F32)

    @pl.when(south)
    def _():
        fbuf[pl.ds(0, 3 * PITCH), :] = jnp.zeros((3 * PITCH, C), F32)

    @pl.when(jnp.logical_not(south))
    def _():
        for k in range(3):
            fbuf[pl.ds(k * PITCH + 8, CC), :] = rs[k].astype(F32)
            for j in range(3):
                fbuf[pl.ds(k * PITCH + 5 + j, 1), :] = csl[j].astype(F32)[13 + k : 14 + k]
                fbuf[pl.ds(k * PITCH + 8 + CC + j, 1), :] = csr[j].astype(F32)[13 + k : 14 + k]

    @pl.when(jnp.logical_not(north))
    def _():
        for k in range(3):
            fbuf[pl.ds((131 + k) * PITCH + 8, CC), :] = rn[k].astype(F32)
            for j in range(3):
                fbuf[pl.ds((131 + k) * PITCH + 5 + j, 1), :] = cnl[j].astype(F32)[k : k + 1]
                fbuf[pl.ds((131 + k) * PITCH + 8 + CC + j, 1), :] = cnr[j].astype(F32)[k : k + 1]

    gather_rows(0, 11, 0, EC)
    pl.when(north)(fold2)

    def last_rows():
        @pl.when(north)
        def _():
            off = fold3()
            for k in range(3):
                for i in range(EC):
                    fbuf[pl.ds((131 + k) * PITCH + 5 + i, 1), :] = fcat[2 - k, pl.ds(off + EC - 1 - i, 1), :]

        gather_rows(11, 14, 0, EC)

    def conv(src, r, cb, flip):
        total_ = None
        for a in range(7):
            terms = []
            for b in range(7):
                t = 48 - (7 * a + b) if flip else 7 * a + b
                x = src[rows(((r + a) * EC + cb * 8 + b) * G, 8 * G), :].reshape(8, G, C)
                terms.append(x * wb[t][None])
            term = tree(terms).astype(F32)
            total_ = term if total_ is None else total_ + term
        return total_

    @pl.loop(0, RR)
    def _(r):
        pl.when(r == 5)(last_rows)

        @pl.loop(0, 4)
        def _(cb):
            hat[rows((r * CC + cb * 8) * G, 8 * G), :] = conv(ext, r, cb, False).reshape(8 * G, C)

    @pl.loop(0, CHUNKS)
    def _(k):
        at = rows(k * M, M)
        r = k
        dh, ds = norm_parts(hat[at, :])
        hat[at, :] = dh
        rstd[at, :] = ds
        nm = (dh * gain).astype(BF16)
        normed[at, :] = nm
        active, slp = gelu_parts(dot(nm, up[...], 1, 0) + bias)
        act[at, :] = active
        slope[at, :] = slp
        mixed = dot(active, down[...], 1, 0)
        x = ext[rows(((r + 3) * EC + 3) * G, M), :].astype(F32)
        lev0[at, :] = (landb[at, :] * (x + scale * mixed)).astype(BF16)

    def section(s, count, cols, src, hats, rstds, patches, put):
        sg = sgain_in[s : s + 1].astype(F32)
        sb = sbias_in[s : s + 1].astype(F32)
        n = cols * G
        half = cols // 2

        def step(i):
            parts = []
            for a in range(2):
                at = rows((2 * i + a) * n, n)
                h, rs_ = norm_parts(src[at, :].astype(F32), True)
                hats[at, :] = h
                rstds[at, :] = rs_
                sn = (h * sg).astype(BF16).reshape(half, 2, G, C)
                parts += [sn[:, b].reshape(half * G, C) for b in range(2)]
            p = jnp.concatenate(parts, axis=1)
            patches[rows(i * half * G, half * G), :] = p
            put(i, (dot(p, sw[s], 1, 0) + sb).astype(BF16))

        if count == 1:
            step(0)
        else:
            pl.loop(0, count)(step)

    def put1(i, v):
        lev1[rows(i * 256, 256), :] = v

    def put2(i, v):
        lev2[rows(i * 128, 128), :] = v

    def put3(i, v):
        v = v.astype(F32)
        for j in range(4):
            cb32[pl.ds(j, G, stride=4), :] = v[j * G : (j + 1) * G]
        for g in range(G):
            bott[g] = cb32[pl.ds(g * 4, 4), :].astype(BF16)

    section(0, 4, 32, lev0, hat1, rstd1, p1, put1)
    section(1, 2, 16, lev1, hat2, rstd2, p2, put2)
    section(2, 1, 8, lev2, hat3, rstd3, p3, put3)

    def section_back(s, count, cols, src, hats, rstds, patches, put):
        sg = sgain_in[s : s + 1].astype(F32)
        n = cols * G
        half = cols // 2
        secacc[s] = jnp.zeros((C, 4 * C), F32)

        def step(i):
            at = rows(i * half * G, half * G)
            u = src[at, :]
            secacc[s] += dot(u, patches[at, :], 0, 0)
            spread = dot(u, sw[s], 1, 1)
            for a in range(2):
                at2 = rows((2 * i + a) * n, n)
                hh = hats[at2, :].reshape(half, 2, G, C)
                rr = rstds[at2, :].reshape(half, 2, G, C)
                outs = []
                for b in range(2):
                    q = 2 * a + b
                    g = spread[:, q * C : (q + 1) * C] * sg
                    back = norm_back(g, hh[:, b].reshape(half * G, C), rr[:, b].reshape(half * G, C))
                    outs.append(back.astype(BF16).reshape(half, G, C))
                put(at2, jnp.stack(outs, axis=1).reshape(n, C))

        if count == 1:
            step(0)
        else:
            pl.loop(0, count)(step)

    def putb2(at, v):
        back2[at, :] = v

    def putb1(at, v):
        back1[at, :] = v

    def putb0(at, v):
        direct[at, :] = (landb[at, :] * v.astype(F32)).astype(BF16)

    section_back(2, 1, 8, cotb, hat3, rstd3, p3, putb2)
    section_back(1, 2, 16, back2, hat2, rstd2, p2, putb1)
    section_back(0, 4, 32, back1, hat1, rstd1, p1, putb0)

    bsec = dict(s1=sec_s1, r1=sec_r1, s2f=sec_s2f, s2=sec_s2, r2=sec_r2, s3=sec_s3, r3=sec_r3, r4=sec_r4, g3=sec_g3, g2=sec_g2, g1a=sec_g1a, g1b=sec_g1b)
    bden = dict(s1=den_s1, r1=den_r1, s2f=den_s2f, s2=den_s2, r2=den_r2, s3=den_s3, r3=den_r3, r4=den_r4, g3=den_g3, g2=den_g2, g1a=den_g1a, g1b=den_g1b)
    core_to, x_to = (lat + 1 - 2 * core, lon), (lax.rem(lat + 2, 4), lon)
    far_to = (lax.rem(lat + 3 - 2 * core, 4), lon)

    def reduction(size, full, b):
        half, quarter, piece = size // 2, size // 4, size // 32
        c1 = remote(b["s1"].at[rows((1 - core) * half, half)], b["r1"], take(1), core_to)
        c2 = remote(b["s2"].at[rows((1 - xl) * quarter, quarter)], b["r2"], take(1), x_to)
        sem3, sem4, sem5 = take(NH - 1), take(NZ - 1), take(NH - 1)
        x6 = remote(b["g3"], b["g2"], take(1), x_to)
        x7 = remote(b["g3"], b["g1a"], take(1), core_to)
        x8 = remote(b["g3"], b["g1b"], take(1), far_to)

        def first():
            b["s1"][...] = full[...].astype(BF16)
            c1.start()

        def second():
            c1.wait()
            b["s2f"][...] = full[rows(core * half, half), :] + b["r1"][...].astype(F32)
            b["s2"][...] = b["s2f"][...].astype(BF16)
            c2.start()

        def third():
            c2.wait()
            b["s3"][...] = (b["s2f"][rows(xl * quarter, quarter), :] + b["r2"][...].astype(F32)).astype(BF16)
            for j in range(1, NH):
                h, to = hi_peer(j)
                remote(b["s3"].at[rows(h * piece, piece)], b["r3"].at[hi], sem3 + j - 1, to).start()
            b["r3"][hi] = b["s3"][rows(hi * piece, piece), :]

        def total8(buf):
            part = buf[0].astype(F32)
            for i in range(1, 8):
                part = part + buf[i].astype(F32)
            return part.astype(BF16)

        def fourth():
            for j in range(1, NH):
                h = lax.rem(hi + NH - j, NH)
                copy = remote(b["s3"].at[pl.ds(0, piece)], b["r3"].at[h], sem3 + j - 1, hi_peer(j)[1])
                copy.wait_send()
                copy.wait_recv()
            b["r4"][z] = total8(b["r3"])
            for j in range(1, NZ):
                remote(b["r4"].at[z], b["r4"].at[z], sem4 + j - 1, z_peer(j)[1]).start()

        def fifth():
            for j in range(1, NZ):
                t = lax.rem(z + NZ - j, NZ)
                copy = remote(b["r4"].at[z], b["r4"].at[t], sem4 + j - 1, z_peer(j)[1])
                copy.wait_send()
                copy.wait_recv()
            b["g3"][hi] = total8(b["r4"])
            for j in range(1, NH):
                remote(b["g3"].at[hi], b["g3"].at[hi], sem5 + j - 1, hi_peer(j)[1]).start()

        def sixth():
            for j in range(1, NH):
                h = lax.rem(hi + NH - j, NH)
                copy = remote(b["g3"].at[hi], b["g3"].at[h], sem5 + j - 1, hi_peer(j)[1])
                copy.wait_send()
                copy.wait_recv()
            x6.start()
            x7.start()
            x8.start()

        def last(out):
            def place(c_, x_, v):
                out[rows((c_ * 2 + x_) * quarter, quarter), :] = v.reshape(quarter, C).astype(F32) * factor

            place(core, xl, b["g3"][...])
            x7.wait()
            place(1 - core, xl, b["g1a"][...])
            x6.wait()
            place(core, 1 - xl, b["g2"][...])
            x8.wait()
            place(1 - core, 1 - xl, b["g1b"][...])

        return first, second, third, fourth, fifth, sixth, last

    rs1, rs2, rs3, rs4, rs5, rs6, rs7 = reduction(1536, asec, bsec)
    rd1, rd2, rd3, rd4, rd5, rd6, rd7 = reduction(1024, aden, bden)

    for s in range(3):
        for q in range(4):
            asec[pl.ds((4 * s + q) * C, C), :] = secacc[s, :, q * C : (q + 1) * C].T
    rs1()

    upacc[...] = jnp.zeros_like(upacc)
    dtacc[...] = jnp.zeros_like(dtacc)

    @pl.loop(0, CHUNKS)
    def _(k):
        at = rows(k * M, M)
        r = k
        mg = (direct[at, :].astype(F32) * scale).astype(BF16)
        dtacc[...] += dot(mg, act[at, :], 0, 0)
        hg = (dot(mg, down[...], 1, 1) * slope[at, :].astype(F32)).astype(BF16)
        upacc[...] += dot(normed[at, :], hg, 0, 0)
        ng = dot(hg, up[...], 1, 1) * gain
        dg = norm_back(ng, hat[at, :], rstd[at, :]).astype(BF16)
        dgb[r] = dg.reshape(POS, G, C)
        ext2[rows(((r + 3) * EC + 3) * G, M), :] = dg
        d32[rows((r * EC + 3) * G, M), :] = dg.astype(F32)
        pl.when(k == 1)(rs2)
        pl.when(k == 5)(rs3)

    for i in range(3):
        rst[i] = d32[pl.ds(((5 + i) * EC + 3) * G + 15, CC, stride=G), :].astype(BF16)
        rsb[i] = d32[pl.ds((i * EC + 3) * G, CC, stride=G), :].astype(BF16)

    halo2 = halo_copies(
        [
            (0, -1, dgb.at[:, pl.ds(0, 3)], dcr),
            (0, 1, dgb.at[:, pl.ds(CC - 3, 3)], dcl),
            (1, 0, rst, drs),
            (-1, 0, rsb, drn),
            (1, 1, rst.at[:, pl.ds(16, 16)], dsl),
            (1, -1, rst.at[:, pl.ds(0, 16)], dsr),
            (-1, 1, rsb.at[:, pl.ds(16, 16)], dnl),
            (-1, -1, rsb.at[:, pl.ds(0, 16)], dnr),
        ]
    )
    halo_start(halo2)

    for q in range(4):
        aden[pl.ds(q * C, C), :] = upacc[:, q * C : (q + 1) * C]
        aden[pl.ds((4 + q) * C, C), :] = dtacc[:, q * C : (q + 1) * C].T
    rd1()

    tapacc[...] = jnp.zeros_like(tapacc)

    @pl.loop(0, RR)
    def _(r):
        @pl.loop(0, 4)
        def _(cb):
            d = ext2[rows(((r + 3) * EC + 3 + cb * 8) * G, 8 * G), :].reshape(8, G, C)
            for a in range(7):
                for b in range(7):
                    x = ext[rows(((r + a) * EC + cb * 8 + b) * G, 8 * G), :]
                    p = x.reshape(8, G, C) * d
                    t = tree([p[i] for i in range(8)]).astype(F32)
                    tapacc[7 * a + b] += t[:8] + t[8:]

        pl.when(r == 1)(rs4)
        pl.when(r == 2)(rd2)
        pl.when(r == 6)(rd3)

    rs5()

    def tap_stage(buf, peers, me):
        sem = take(len(peers))

        def start(value):
            buf[me] = value.astype(BF16)
            for i, (_, to) in enumerate(peers):
                remote(buf.at[me], buf.at[me], sem + i, to).start()

        def finish():
            for i, (frm, to) in enumerate(peers):
                copy = remote(buf.at[me], buf.at[frm], sem + i, to)
                copy.wait_send()
                copy.wait_recv()
            out = buf[0].astype(F32)
            for i in range(1, buf.shape[0]):
                out = out + buf[i].astype(F32)
            return out

        return start, finish

    lat_peers = [(lax.rem(lat + 4 - j, 4), (lax.rem(lat + j, 4), lon)) for j in range(1, 4)]
    hi_peers = [(lax.rem(hi + NH - j, NH), hi_peer(j)[1]) for j in range(1, NH)]
    z_peers = [(lax.rem(z + NZ - j, NZ), z_peer(j)[1]) for j in range(1, NZ)]
    tl_start, tl_finish = tap_stage(tl, lat_peers, lat)
    th_start, th_finish = tap_stage(th, hi_peers, hi)
    tz_start, tz_finish = tap_stage(tz, z_peers, z)
    tl_start(jnp.concatenate([jnp.sum(tapacc[...], axis=1), jnp.zeros((15, C), F32)], axis=0))

    halo_wait(halo2)

    @pl.when(south)
    def _():
        drs[...] = jnp.zeros_like(drs)
        dsl[...] = jnp.zeros_like(dsl)
        dsr[...] = jnp.zeros_like(dsr)

    @pl.when(north)
    def _():
        drn[...] = jnp.zeros_like(drn)
        dnl[...] = jnp.zeros_like(dnl)
        dnr[...] = jnp.zeros_like(dnr)

    @pl.loop(0, RR)
    def _(r):
        for j in range(3):
            ext2[rows(((r + 3) * EC + j) * G, G), :] = dcl[r, j]
            ext2[rows(((r + 3) * EC + 3 + CC + j) * G, G), :] = dcr[r, j]
            d32[rows((r * EC + j) * G, G), :] = dcl[r, j].astype(F32)
            d32[rows((r * EC + 3 + CC + j) * G, G), :] = dcr[r, j].astype(F32)

    fg1, fg2, fg3 = fold_exchange(fg, hr1, hs2, hr2, CC)

    @pl.when(north)
    def _():
        for i in range(3):
            for cut, at in ((0, 0), (8, 8), (16, 16), (24, 24), (30, 30)):
                zbuf[i, pl.ds(at, 8), :] = d32[pl.ds(((5 + i) * EC + cut) * G + 15, 8, stride=G), :]
        for k in range(1, 4):
            total_ = None
            for a in range(k + 3, 7):
                for b in range(7):
                    term = zbuf[k - a + 5, pl.ds(6 - b, CC), :] * tapf[7 * a + b : 7 * a + b + 1]
                    total_ = term if total_ is None else total_ + term
            fg[k - 1] = total_.astype(BF16)
        fg1()

    for k in range(6):
        low = k < 3
        r = k + 5 if low else k - 3
        edge, el, er = (drs, dsl, dsr) if low else (drn, dnl, dnr)
        i = k if low else k - 3
        line = 7 if low else 24
        for c in range(EC):
            sh[pl.ds(c * 32 + 8, G), :] = d32[pl.ds((r * EC + c) * G, G), :]
        sh[pl.ds(3 * 32 + line, CC, stride=32), :] = edge[i].astype(F32)
        lft, rgt = el[i].astype(F32), er[i].astype(F32)
        for j in range(3):
            sh[pl.ds(j * 32 + line, 1), :] = lft[13 + j : 14 + j]
            sh[pl.ds((CC + 3 + j) * 32 + line, 1), :] = rgt[j : j + 1]
        to = k if low else k + 8
        for c in range(EC):
            ext2[pl.ds((to * EC + c) * G, G), :] = sh[pl.ds(c * 32 + (7 if low else 9), G), :].astype(BF16)

    @pl.loop(0, RR)
    def _(r):
        @pl.loop(0, 4)
        def _(cb):
            v = conv(ext2, r, cb, True)
            v = v + direct[rows((r * CC + cb * 8) * G, 8 * G), :].astype(F32).reshape(8, G, C)
            for j in range(8):
                obuf[pl.ds(r * CC + cb * 8 + j, G, stride=RR * CC), :] = v[j]

        @pl.when(r == 0)
        def _():
            rs6()
            rd4()

        @pl.when(r == 1)
        def _():
            th_start(tl_finish())
            pl.when(north)(fg2)

        pl.when(r == 3)(rd5)

        @pl.when(r == 5)
        def _():
            tz_start(th_finish())
            rd6()

        @pl.when(r == 6)
        def _():
            rs7(gsec)

    @pl.when(north)
    def _():
        off = fg3()
        for k in range(1, 4):
            for i in range(CC):
                at = pl.ds((128 - k) * CC + i, 1)
                obuf[at, :] += fcat[k - 1, pl.ds(off + CC - 1 - i, 1), :]

    @pl.loop(0, 128)
    def _(i):
        gfield[i] = obuf[rows(i * CC, CC), :].astype(BF16)

    rd7(aden)
    for q in range(4):
        gup[:, q * C : (q + 1) * C] = aden[pl.ds(q * C, C), :]
    gdown[...] = aden[pl.ds(4 * C, 4 * C), :]
    gtaps[...] = tz_finish()[:49] * factor


def on_device(field, land, mirror, depth_weight, norm_gain, up_weight, up_bias, down_proj, layer_scale, section_gain, section_weight, section_bias, cotangent):
    factor = 1.0 / math.sqrt(512 * 2048 / 64.0)
    vm = pl.BlockSpec(memory_space=pltpu.VMEM)
    n = RR * CC * G

    def f(*shape):
        return pltpu.VMEM(shape, F32)

    def h(*shape):
        return pltpu.VMEM(shape, BF16)

    sems = 128
    scratch = dict(
        field=h(128, CC, C),
        land=pltpu.VMEM((CC, 128), jnp.int32),
        taps_in=h(49, C),
        gain_in=h(1, C),
        up=h(C, 512),
        bias_in=h(512),
        down=h(512, C),
        scale_in=h(1, C),
        sgain_in=h(3, C),
        sw=h(3, 512, C),
        sbias_in=h(3, C),
        cot=h(G, 4, C),
        lsem=pltpu.SemaphoreType.DMA((12,)),
        fbuf=f(134 * PITCH, C),
        d32=f(RR * EC * G, C),
        obuf=f(n, C),
        sh=f(EC * 32, C),
        hat=f(n, C),
        rstd=f(n, C),
        landb=f(n, C),
        hat1=f(n, C),
        rstd1=f(n, C),
        hat2=f(n // 4, C),
        rstd2=f(n // 4, C),
        hat3=f(n // 16, C),
        rstd3=f(n // 16, C),
        dgb=h(RR, CC, G, C),
        upacc=f(C, 512),
        dtacc=f(C, 512),
        secacc=f(3, C, 512),
        tapacc=f(49, 8, C),
        lt=f(C, C),
        cb32=f(64, C),
        cotb=h(64, C),
        asec=f(1536, C),
        aden=f(1024, C),
        sec_s1=h(1536, C),
        sec_r1=h(768, C),
        sec_s2f=f(768, C),
        sec_s2=h(768, C),
        sec_r2=h(384, C),
        sec_s3=h(384, C),
        sec_r3=h(NH, 48, C),
        sec_r4=h(NZ, 48, C),
        sec_g3=h(NH, 48, C),
        sec_g2=h(NH, 48, C),
        sec_g1a=h(NH, 48, C),
        sec_g1b=h(NH, 48, C),
        den_s1=h(1024, C),
        den_r1=h(512, C),
        den_s2f=f(512, C),
        den_s2=h(512, C),
        den_r2=h(256, C),
        den_s3=h(256, C),
        den_r3=h(NH, 32, C),
        den_r4=h(NZ, 32, C),
        den_g3=h(NH, 32, C),
        den_g2=h(NH, 32, C),
        den_g1a=h(NH, 32, C),
        den_g1b=h(NH, 32, C),
        tl=h(4, 64, C),
        th=h(NH, 64, C),
        tz=h(NZ, 64, C),
        stl=h(3, 128, C),
        str_=h(3, 128, C),
        cl=h(3, 128, C),
        cr=h(3, 128, C),
        rs=h(3, CC, C),
        rn=h(3, CC, C),
        csl=h(3, 16, C),
        csr=h(3, 16, C),
        cnl=h(3, 16, C),
        cnr=h(3, 16, C),
        dcl=h(RR, 3, G, C),
        dcr=h(RR, 3, G, C),
        rst=h(3, CC, C),
        rsb=h(3, CC, C),
        drs=h(3, CC, C),
        drn=h(3, CC, C),
        dsl=h(3, 16, C),
        dsr=h(3, 16, C),
        dnl=h(3, 16, C),
        dnr=h(3, 16, C),
        fr1=h(NH, 3, CC, C),
        fs2=h(NZ - 1, 3, CC, C),
        fr2=h(NZ, 3, CC, C),
        fcat=f(3, 3 * CC, C),
        zbuf=f(3, 40, C),
        fg=h(3, CC, C),
        hr1=h(NH, 3, CC, C),
        hs2=h(NZ - 1, 3, CC, C),
        hr2=h(NZ, 3, CC, C),
        ssem=pltpu.SemaphoreType.DMA((sems,)),
        rsem=pltpu.SemaphoreType.DMA((sems,)),
    )
    scoped = dict(
        ext=h(ER * EC * G, C),
        ext2=h(ER * EC * G, C),
        wb=h(49, G, C),
        normed=h(n, C),
        act=h(n, 512),
        slope=h(n, 512),
        lev0=h(n, C),
        lev1=h(n // 4, C),
        lev2=h(n // 16, C),
        p1=h(n // 4, 512),
        p2=h(n // 16, 512),
        p3=h(n // 64, 512),
        back1=h(n // 4, C),
        back2=h(n // 16, C),
        direct=h(n, C),
    )

    def whole(*refs):
        pl.run_scoped(functools.partial(kernel, factor, *refs), **scoped)

    bott, gfield, gtaps, gup, gdown, gsec = pl.pallas_call(
        whole,
        out_shape=(
            jax.ShapeDtypeStruct((G, 4, C), BF16),
            jax.ShapeDtypeStruct((128, CC, C), BF16),
            jax.ShapeDtypeStruct((49, C), F32),
            jax.ShapeDtypeStruct((C, 512), F32),
            jax.ShapeDtypeStruct((512, C), F32),
            jax.ShapeDtypeStruct((1536, C), F32),
        ),
        in_specs=[pl.BlockSpec(memory_space=pltpu.SMEM)] + [pl.BlockSpec(memory_space=pltpu.HBM)] * 12,
        out_specs=(vm,) * 6,
        scratch_shapes=list(scratch.values()),
        compiler_params=pltpu.CompilerParams(
            collective_id=0, has_side_effects=True, vmem_limit_bytes=50 * 1024 * 1024
        ),
    )(
        mirror,
        *(
            pltpu.with_memory_space_constraint(v, pltpu.HBM)
            for v in (
                field,
                land.T,
                depth_weight,
                norm_gain.reshape(1, C),
                up_weight,
                up_bias,
                down_proj,
                layer_scale.reshape(1, C),
                section_gain,
                section_weight,
                section_bias,
                cotangent,
            )
        ),
    )
    results = (bott, gfield, gtaps, gup, gdown, gsec)
    anywhere = pl.BlockSpec(memory_space=pl.ANY)

    def write(*refs):
        copies = [pltpu.make_async_copy(refs[i], refs[6 + i], refs[12].at[i]) for i in range(6)]
        for copy in copies:
            copy.start()
        for copy in copies:
            copy.wait()

    bott, gfield, gtaps, gup, gdown, gsec = pl.pallas_call(
        write,
        out_shape=tuple(jax.ShapeDtypeStruct(x.shape, x.dtype) for x in results),
        in_specs=[vm] * 6,
        out_specs=(anywhere,) * 6,
        scratch_shapes=[pltpu.SemaphoreType.DMA((6,))],
        compiler_params=pltpu.CompilerParams(vmem_limit_bytes=16 * 1024 * 1024),
    )(*results)
    return bott, gfield, gtaps, gup, gdown, gsec.reshape(3, 512, C)


def solution(mesh):
    cell = P("lat", "lon", None)
    in_specs = (cell, P("lat", "lon")) + (P(),) * 10 + (cell,)
    out_specs = (cell, cell, P(), P(), P(), P())
    return jax.shard_map(
        on_device, mesh=mesh, in_specs=in_specs, out_specs=out_specs, check_vma=False
    )
```

```python
import functools
import math

import jax
import jax.numpy as jnp
from jax import lax
from jax.experimental import pallas as pl
from jax.experimental.pallas import tpu as pltpu
from jax.sharding import PartitionSpec as P

MESH = pl.DeviceIdType.MESH
F32 = jnp.float32
BF16 = jnp.bfloat16
epsilon = 1e-06

G = 16
RR = 8
CC = 32
C = 128
PITCH = 48
EC = CC + 6
ER = RR + 6
NZ = 8
NH = 8
M = 512
CHUNKS = RR * CC * G // M
POS = M // G


def mean_mx(values):
    ones = jnp.full((C, C), 1.0 / C, BF16)
    return dot(values.astype(BF16), ones, 1, 0)


def norm_parts(values, exact=False):
    mean = mean_mx(values) if exact else jnp.mean(values, axis=-1, keepdims=True)
    center = values - mean
    rstd = lax.rsqrt(jnp.mean(center * center, axis=-1, keepdims=True) + epsilon)
    return center * rstd, rstd


def norm_back(grad_hat, normed_hat, rstd):
    second = jnp.mean(grad_hat * normed_hat, axis=-1, keepdims=True)
    return rstd * (grad_hat - mean_mx(grad_hat) - normed_hat * second)


def norm_back_wide(grad_hat, normed_hat, rstd):
    pair = jnp.concatenate([grad_hat.astype(BF16), (grad_hat * normed_hat).astype(BF16)], axis=1)
    ones, zeros = jnp.full((C, C), 1.0 / C, BF16), jnp.zeros((C, C), BF16)
    both = jnp.concatenate(
        [jnp.concatenate([ones, zeros], axis=1), jnp.concatenate([zeros, ones], axis=1)], axis=0
    )
    means = dot(pair, both, 1, 0)
    return rstd * (grad_hat - means[:, :C] - normed_hat * means[:, C:])


def gelu_parts(h):
    h = h.astype(BF16)
    e = jnp.exp2(h * h * jnp.asarray(-0.7213475204444817, BF16))
    cdf = jnp.asarray(0.5, BF16) + jnp.asarray(0.5, BF16) * lax.erf(h * jnp.asarray(0.7071067811865476, BF16))
    return h * cdf, cdf + h * (e * jnp.asarray(0.3989422804014327, BF16))


def tree(terms):
    while len(terms) > 1:
        terms = [a + b for a, b in zip(terms[::2], terms[1::2])] + terms[len(terms) & ~1 :]
    return terms[0]


def dot(a, b, ca, cb):
    return lax.dot_general(a, b, (((ca,), (cb,)), ((), ())), preferred_element_type=F32)


def rows(start, size, align=16):
    return pl.ds(pl.multiple_of(start, align), size)


def kernel(
    factor,
    mirror,
    x_field,
    x_land,
    x_taps_in,
    x_gain_in,
    x_up,
    x_bias_in,
    x_down,
    x_scale_in,
    x_sgain_in,
    x_sw,
    x_sbias_in,
    x_cot,
    bott,
    gfield,
    gtaps,
    gup,
    gdown,
    gsec,
    field,
    land,
    taps_in,
    gain_in,
    up,
    bias_in,
    down,
    scale_in,
    sgain_in,
    sw,
    sbias_in,
    cot,
    lsem,
    fbuf,
    d32,
    obuf,
    sh,
    hat,
    rstd,
    landb,
    hat1,
    rstd1,
    hat2,
    rstd2,
    hat3,
    rstd3,
    dgb,
    upacc,
    dtacc,
    secacc,
    tapacc,
    lt,
    cb32,
    cotb,
    asec,
    aden,
    sec_s1,
    sec_r1,
    sec_s2f,
    sec_s2,
    sec_r2,
    sec_s3,
    sec_r3,
    sec_r4,
    sec_g3,
    sec_g2,
    sec_g1a,
    sec_g1b,
    den_s1,
    den_r1,
    den_s2f,
    den_s2,
    den_r2,
    den_s3,
    den_r3,
    den_r4,
    den_g3,
    den_g2,
    den_g1a,
    den_g1b,
    tl,
    th,
    tz,
    stl,
    str_,
    cl,
    cr,
    rs,
    rn,
    csl,
    csr,
    cnl,
    cnr,
    dcl,
    dcr,
    rst,
    rsb,
    drs,
    drn,
    dsl,
    dsr,
    dnl,
    dnr,
    fr1,
    fs2,
    fr2,
    fcat,
    zbuf,
    fg,
    hr1,
    hs2,
    hr2,
    ssem,
    rsem,
    ext,
    ext2,
    wb,
    normed,
    act,
    slope,
    lev0,
    lev1,
    lev2,
    p1,
    p2,
    p3,
    back1,
    back2,
    direct,
):
    loads = [
        pltpu.make_async_copy(a, b, lsem.at[i])
        for i, (a, b) in enumerate(
            (
                (x_field, field),
                (x_land, land),
                (x_taps_in, taps_in),
                (x_gain_in, gain_in),
                (x_up, up),
                (x_bias_in, bias_in),
                (x_down, down),
                (x_scale_in, scale_in),
                (x_sgain_in, sgain_in),
                (x_sw, sw),
                (x_sbias_in, sbias_in),
                (x_cot, cot),
            )
        )
    ]
    for copy in loads:
        copy.start()

    lat = lax.axis_index("lat")
    lon = lax.axis_index("lon")
    hi, z = lon // NZ, lax.rem(lon, NZ)
    core, xl = lax.rem(lat, 2), lat // 2
    right, left = lax.rem(lon + 1, NH * NZ), lax.rem(lon + NH * NZ - 1, NH * NZ)
    north, south = lat == 3, lat == 0

    counter = [0]

    def take(n):
        counter[0] += n
        return counter[0] - n

    def remote(src, dst, sem, to):
        return pltpu.make_async_remote_copy(
            src_ref=src,
            dst_ref=dst,
            send_sem=ssem.at[sem],
            recv_sem=rsem.at[sem],
            device_id=to,
            device_id_type=MESH,
        )

    def hi_peer(j):
        h = lax.rem(hi + j, NH)
        return h, (lat, h * NZ + z)

    def z_peer(j):
        t = lax.rem(z + j, NZ)
        return t, (lat, hi * NZ + t)

    barrier = pltpu.get_barrier_semaphore()

    def greet(to):
        pl.semaphore_signal(barrier, inc=1, device_id=to, device_id_type=MESH)

    greet((lat, left))
    greet((lat, right))
    for dl in (-1, 1):

        @pl.when((lat + dl >= 0) & (lat + dl < 4))
        def _():
            greet((lat + dl, left))
            greet((lat + dl, right))

    for j in range(1, 4):
        greet((lax.rem(lat + j, 4), lon))
    for j in range(1, NH):
        greet(hi_peer(j)[1])
    for j in range(1, NZ):
        greet(z_peer(j)[1])

    loads[0].wait()

    @pl.loop(0, 128)
    def _(i):
        fbuf[rows((i + 3) * PITCH + 8, CC, 8), :] = field[i].astype(F32)

    for j in range(3):
        stl[j] = fbuf[pl.ds(3 * PITCH + 8 + j, 128, stride=PITCH), :].astype(BF16)
        str_[j] = fbuf[pl.ds(3 * PITCH + 8 + CC - 3 + j, 128, stride=PITCH), :].astype(BF16)

    waits = 2 + 3 + (NH - 1) + (NZ - 1)
    pl.semaphore_wait(barrier, waits + jnp.where(south | north, 2, 4))

    def halo_copies(pieces):
        made = []
        for dl, dn, src, dst in pieces:
            sem = take(1)
            to_lon = right if dn == 1 else left if dn == -1 else lon
            copy = remote(src, dst, sem, (lat + dl, to_lon))
            made.append((dl, copy))
        return made

    def when_lat(dl, ok, fn):
        if dl == 0:
            fn()
        else:
            pl.when(ok)(fn)

    def halo_start(made):
        for dl, copy in made:
            when_lat(dl, (lat + dl >= 0) & (lat + dl < 4), copy.start)

    def halo_wait(made):
        for dl, copy in made:
            when_lat(dl, (lat + dl >= 0) & (lat + dl < 4), copy.wait_send)
            when_lat(dl, (lat - dl >= 0) & (lat - dl < 4), copy.wait_recv)

    halo = halo_copies(
        [
            (0, -1, stl, cr),
            (0, 1, str_, cl),
            (1, 0, field.at[pl.ds(125, 3)], rs),
            (-1, 0, field.at[pl.ds(0, 3)], rn),
            (1, 1, str_.at[:, pl.ds(112, 16)], csl),
            (1, -1, stl.at[:, pl.ds(112, 16)], csr),
            (-1, 1, str_.at[:, pl.ds(0, 16)], cnl),
            (-1, -1, stl.at[:, pl.ds(0, 16)], cnr),
        ]
    )
    halo_start(halo)

    shift = mirror[0]
    total = NH * NZ * CC

    def first_block(dev, width):
        base = lax.rem(shift - CC * dev - (width - 1) + (3 if width > CC else 0) + 2 * total, total)
        return base // CC, lax.rem(base, CC)

    def fold_exchange(src, buf1, stage2, buf2, width):
        sem1, sem2 = take(NH - 1), take(NZ - 1)

        def first():
            for j in range(1, NH):
                remote(src, buf1.at[hi], sem1 + j - 1, hi_peer(j)[1]).start()
            buf1[hi] = src[...]

        def held(dev):
            q = first_block(dev, width)[0]
            block = lax.rem(q + lax.rem(z + NH * NZ - q, NZ), NH * NZ)
            return block // NZ

        def second():
            for j in range(1, NH):
                h = lax.rem(hi + NH - j, NH)
                copy = remote(src, buf1.at[h], sem1 + j - 1, hi_peer(j)[1])
                copy.wait_send()
                copy.wait_recv()
            for j in range(1, NZ):
                t, to = z_peer(j)
                stage2[j - 1] = buf1[held(hi * NZ + t)]
                remote(stage2.at[j - 1], buf2.at[z], sem2 + j - 1, to).start()
            buf2[z] = buf1[held(lon)]

        def last():
            for j in range(1, NZ):
                t = lax.rem(z + NZ - j, NZ)
                copy = remote(stage2.at[j - 1], buf2.at[t], sem2 + j - 1, z_peer(j)[1])
                copy.wait_send()
                copy.wait_recv()
            q, off = first_block(lon, width)
            for m in range(3 if width > CC else 2):
                fcat[:, pl.ds(m * CC, CC), :] = buf2[lax.rem(q + m, NZ)].astype(F32)
            return off

        return first, second, last

    fold1, fold2, fold3 = fold_exchange(field.at[pl.ds(125, 3)], fr1, fs2, fr2, CC + 6)
    pl.when(north)(fold1)

    for copy in loads[1:]:
        copy.wait()

    tapf = taps_in[...].astype(F32)
    for t in range(49):
        wb[t] = jnp.broadcast_to(tapf[t : t + 1], (G, C)).astype(BF16)
    gain = gain_in[...].astype(F32)
    bias = bias_in[...].astype(F32).reshape(1, 512)
    scale = scale_in[...].astype(F32)

    lt[...] = jnp.concatenate([land[...].astype(F32), jnp.zeros((C - CC, C), F32)], axis=0).T

    @pl.loop(0, RR)
    def _(r):
        v = lt[pl.ds(r, G, stride=RR), :]
        for c in range(CC):
            landb[rows((r * CC + c) * G, G), :] = jnp.broadcast_to(v[:, c : c + 1], (G, C))

    for g in range(G):
        cb32[pl.ds(g, 4, stride=G), :] = cot[g].astype(F32)
    cotb[...] = cb32[...].astype(BF16)

    def gather_rows(r0, r1, c0, c1):
        @pl.loop(r0, r1)
        def _(r):
            for c in range(c0, c1):
                ext[rows((r * EC + c) * G, G), :] = fbuf[
                    pl.ds(r * PITCH + 5 + c, G, stride=RR * PITCH), :
                ].astype(BF16)

    halo_wait(halo)
    for j in range(3):
        fbuf[pl.ds(3 * PITCH + 5 + j, 128, stride=PITCH), :] = cl[j].astype(F32)
        fbuf[pl.ds(3 * PITCH + 8 + CC + j, 128, stride=PITCH), :] = cr[j].astype(F32)

    @pl.when(south)
    def _():
        fbuf[pl.ds(0, 3 * PITCH), :] = jnp.zeros((3 * PITCH, C), F32)

    @pl.when(jnp.logical_not(south))
    def _():
        for k in range(3):
            fbuf[pl.ds(k * PITCH + 8, CC), :] = rs[k].astype(F32)
            for j in range(3):
                fbuf[pl.ds(k * PITCH + 5 + j, 1), :] = csl[j].astype(F32)[13 + k : 14 + k]
                fbuf[pl.ds(k * PITCH + 8 + CC + j, 1), :] = csr[j].astype(F32)[13 + k : 14 + k]

    @pl.when(jnp.logical_not(north))
    def _():
        for k in range(3):
            fbuf[pl.ds((131 + k) * PITCH + 8, CC), :] = rn[k].astype(F32)
            for j in range(3):
                fbuf[pl.ds((131 + k) * PITCH + 5 + j, 1), :] = cnl[j].astype(F32)[k : k + 1]
                fbuf[pl.ds((131 + k) * PITCH + 8 + CC + j, 1), :] = cnr[j].astype(F32)[k : k + 1]

    gather_rows(0, 11, 0, EC)
    pl.when(north)(fold2)

    def last_rows():
        @pl.when(north)
        def _():
            off = fold3()
            for k in range(3):
                for i in range(EC):
                    fbuf[pl.ds((131 + k) * PITCH + 5 + i, 1), :] = fcat[2 - k, pl.ds(off + EC - 1 - i, 1), :]

        gather_rows(11, 14, 0, EC)

    def conv(src, r, cb, flip):
        outs = []
        for c in range(8):
            total_ = None
            for group in ((0, 1), (2, 3), (4, 5, 6)):
                terms = []
                for a in group:
                    line = []
                    for b in range(7):
                        t = 48 - (7 * a + b) if flip else 7 * a + b
                        x = src[rows(((r + a) * EC + cb * 8 + c + b) * G, G), :].reshape(1, G, C)
                        line.append(x * wb[t][None])
                    terms.append(tree(line))
                term = tree(terms).astype(F32)
                total_ = term if total_ is None else total_ + term
            outs.append(total_)
        return jnp.concatenate(outs, axis=0)

    @pl.loop(0, RR)
    def _(r):
        pl.when(r == 5)(last_rows)

        @pl.loop(0, 4)
        def _(cb):
            hat[rows((r * CC + cb * 8) * G, 8 * G), :] = conv(ext, r, cb, False).reshape(8 * G, C)

    def forward1(k):
        at = rows(k * M, M)
        dh, ds = norm_parts(hat[at, :])
        hat[at, :] = dh
        rstd[at, :] = jnp.broadcast_to(ds, dh.shape)
        nm = (dh * gain).astype(BF16)
        normed[at, :] = nm
        active, slp = gelu_parts(dot(nm, up[...], 1, 0) + bias)
        act[at, :] = active
        slope[at, :] = slp
        return active

    def forward2(k, active):
        at = rows(k * M, M)
        mixed = dot(active, down[...], 1, 0)
        x = ext[rows(((k + 3) * EC + 3) * G, M), :].astype(F32)
        lev0[at, :] = (landb[at, :] * (x + scale * mixed)).astype(BF16)

    @pl.loop(0, CHUNKS)
    def _(k):
        forward2(k, forward1(k))

    def section(s, count, cols, src, hats, rstds, patches, put):
        sg = sgain_in[s : s + 1].astype(F32)
        sb = sbias_in[s : s + 1].astype(F32)
        n = cols * G
        half = cols // 2

        def step(i):
            parts = []
            for a in range(2):
                at = rows((2 * i + a) * n, n)
                h, rs_ = norm_parts(src[at, :].astype(F32), True)
                hats[at, :] = h
                rstds[at, :] = jnp.broadcast_to(rs_, h.shape)
                sn = (h * sg).astype(BF16).reshape(half, 2, G, C)
                parts += [sn[:, b].reshape(half * G, C) for b in range(2)]
            p = jnp.concatenate(parts, axis=1)
            patches[rows(i * half * G, half * G), :] = p
            put(i, (dot(p, sw[s], 1, 0) + sb).astype(BF16))

        if count == 1:
            step(0)
        else:
            pl.loop(0, count)(step)

    def put1(i, v):
        lev1[rows(i * 256, 256), :] = v

    def put2(i, v):
        lev2[rows(i * 128, 128), :] = v

    def put3(i, v):
        v = v.astype(F32)
        for j in range(4):
            cb32[pl.ds(j, G, stride=4), :] = v[j * G : (j + 1) * G]
        for g in range(G):
            bott[g] = cb32[pl.ds(g * 4, 4), :].astype(BF16)

    section(0, 4, 32, lev0, hat1, rstd1, p1, put1)
    section(1, 2, 16, lev1, hat2, rstd2, p2, put2)
    section(2, 1, 8, lev2, hat3, rstd3, p3, put3)

    def section_back(s, count, cols, src, hats, rstds, patches, put):
        sg = sgain_in[s : s + 1].astype(F32)
        n = cols * G
        half = cols // 2
        secacc[s] = jnp.zeros((C, 4 * C), F32)

        def step(i):
            at = rows(i * half * G, half * G)
            u = src[at, :]
            secacc[s] += dot(u, patches[at, :], 0, 0)
            spread = dot(u, sw[s], 1, 1)
            for a in range(2):
                at2 = rows((2 * i + a) * n, n)
                hh = hats[at2, :].reshape(half, 2, G, C)
                rr = rstds[at2, :].reshape(half, 2, G, C)
                outs = []
                for b in range(2):
                    q = 2 * a + b
                    g = spread[:, q * C : (q + 1) * C] * sg
                    back = norm_back(g, hh[:, b].reshape(half * G, C), rr[:, b].reshape(half * G, C))
                    outs.append(back.astype(BF16).reshape(half, G, C))
                put(at2, jnp.stack(outs, axis=1).reshape(n, C))

        if count == 1:
            step(0)
        else:
            pl.loop(0, count)(step)

    def putb2(at, v):
        back2[at, :] = v

    def putb1(at, v):
        back1[at, :] = v

    def putb0(at, v):
        direct[at, :] = (landb[at, :] * v.astype(F32)).astype(BF16)

    section_back(2, 1, 8, cotb, hat3, rstd3, p3, putb2)
    section_back(1, 2, 16, back2, hat2, rstd2, p2, putb1)
    section_back(0, 4, 32, back1, hat1, rstd1, p1, putb0)

    bsec = dict(s1=sec_s1, r1=sec_r1, s2f=sec_s2f, s2=sec_s2, r2=sec_r2, s3=sec_s3, r3=sec_r3, r4=sec_r4, g3=sec_g3, g2=sec_g2, g1a=sec_g1a, g1b=sec_g1b)
    bden = dict(s1=den_s1, r1=den_r1, s2f=den_s2f, s2=den_s2, r2=den_r2, s3=den_s3, r3=den_r3, r4=den_r4, g3=den_g3, g2=den_g2, g1a=den_g1a, g1b=den_g1b)
    core_to, x_to = (lat + 1 - 2 * core, lon), (lax.rem(lat + 2, 4), lon)
    far_to = (lax.rem(lat + 3 - 2 * core, 4), lon)

    def reduction(size, full, b):
        half, quarter, piece = size // 2, size // 4, size // 32
        c1 = remote(b["s1"].at[rows((1 - core) * half, half)], b["r1"], take(1), core_to)
        c2 = remote(b["s2"].at[rows((1 - xl) * quarter, quarter)], b["r2"], take(1), x_to)
        sem3, sem4, sem5 = take(NH - 1), take(NZ - 1), take(NH - 1)
        x6 = remote(b["g3"], b["g2"], take(1), x_to)
        x7 = remote(b["g3"], b["g1a"], take(1), core_to)
        x8 = remote(b["g3"], b["g1b"], take(1), far_to)

        def first():
            b["s1"][...] = full[...].astype(BF16)
            c1.start()

        def second():
            c1.wait()
            b["s2f"][...] = full[rows(core * half, half), :] + b["r1"][...].astype(F32)
            b["s2"][...] = b["s2f"][...].astype(BF16)
            c2.start()

        def third():
            c2.wait()
            b["s3"][...] = (b["s2f"][rows(xl * quarter, quarter), :] + b["r2"][...].astype(F32)).astype(BF16)
            for j in range(1, NH):
                h, to = hi_peer(j)
                remote(b["s3"].at[rows(h * piece, piece)], b["r3"].at[hi], sem3 + j - 1, to).start()
            b["r3"][hi] = b["s3"][rows(hi * piece, piece), :]

        def total8(buf):
            part = buf[0].astype(F32)
            for i in range(1, 8):
                part = part + buf[i].astype(F32)
            return part.astype(BF16)

        def fourth():
            for j in range(1, NH):
                h = lax.rem(hi + NH - j, NH)
                copy = remote(b["s3"].at[pl.ds(0, piece)], b["r3"].at[h], sem3 + j - 1, hi_peer(j)[1])
                copy.wait_send()
                copy.wait_recv()
            b["r4"][z] = total8(b["r3"])
            for j in range(1, NZ):
                remote(b["r4"].at[z], b["r4"].at[z], sem4 + j - 1, z_peer(j)[1]).start()

        def fifth():
            for j in range(1, NZ):
                t = lax.rem(z + NZ - j, NZ)
                copy = remote(b["r4"].at[z], b["r4"].at[t], sem4 + j - 1, z_peer(j)[1])
                copy.wait_send()
                copy.wait_recv()
            b["g3"][hi] = total8(b["r4"])
            for j in range(1, NH):
                remote(b["g3"].at[hi], b["g3"].at[hi], sem5 + j - 1, hi_peer(j)[1]).start()

        def sixth():
            for j in range(1, NH):
                h = lax.rem(hi + NH - j, NH)
                copy = remote(b["g3"].at[hi], b["g3"].at[h], sem5 + j - 1, hi_peer(j)[1])
                copy.wait_send()
                copy.wait_recv()
            x6.start()
            x7.start()
            x8.start()

        def last(out):
            def place(c_, x_, v):
                out[rows((c_ * 2 + x_) * quarter, quarter), :] = v.reshape(quarter, C).astype(F32) * factor

            place(core, xl, b["g3"][...])
            x7.wait()
            place(1 - core, xl, b["g1a"][...])
            x6.wait()
            place(core, 1 - xl, b["g2"][...])
            x8.wait()
            place(1 - core, 1 - xl, b["g1b"][...])

        return first, second, third, fourth, fifth, sixth, last

    rs1, rs2, rs3, rs4, rs5, rs6, rs7 = reduction(1536, asec, bsec)
    rd1, rd2, rd3, rd4, rd5, rd6, rd7 = reduction(1024, aden, bden)

    for s in range(3):
        for q in range(4):
            asec[pl.ds((4 * s + q) * C, C), :] = secacc[s, :, q * C : (q + 1) * C].T
    rs1()

    upacc[...] = jnp.zeros_like(upacc)
    dtacc[...] = jnp.zeros_like(dtacc)

    def backward1(k):
        at = rows(k * M, M)
        mg = (direct[at, :].astype(F32) * scale).astype(BF16)
        dtacc[...] += dot(mg, act[at, :], 0, 0)
        return (dot(mg, down[...], 1, 1) * slope[at, :].astype(F32)).astype(BF16)

    def backward2(k, hg):
        at = rows(k * M, M)
        upacc[...] += dot(normed[at, :], hg, 0, 0)
        ng = dot(hg, up[...], 1, 1) * gain
        dg = norm_back_wide(ng, hat[at, :], rstd[at, :]).astype(BF16)
        dgb[k] = dg.reshape(POS, G, C)
        ext2[rows(((k + 3) * EC + 3) * G, M), :] = dg
        d32[rows((k * EC + 3) * G, M), :] = dg.astype(F32)

    @pl.loop(0, CHUNKS)
    def _(k):
        backward2(k, backward1(k))
        pl.when(k == 1)(rs2)
        pl.when(k == 5)(rs3)

    for i in range(3):
        rst[i] = d32[pl.ds(((5 + i) * EC + 3) * G + 15, CC, stride=G), :].astype(BF16)
        rsb[i] = d32[pl.ds((i * EC + 3) * G, CC, stride=G), :].astype(BF16)

    halo2 = halo_copies(
        [
            (0, -1, dgb.at[:, pl.ds(0, 3)], dcr),
            (0, 1, dgb.at[:, pl.ds(CC - 3, 3)], dcl),
            (1, 0, rst, drs),
            (-1, 0, rsb, drn),
            (1, 1, rst.at[:, pl.ds(16, 16)], dsl),
            (1, -1, rst.at[:, pl.ds(0, 16)], dsr),
            (-1, 1, rsb.at[:, pl.ds(16, 16)], dnl),
            (-1, -1, rsb.at[:, pl.ds(0, 16)], dnr),
        ]
    )
    halo_start(halo2)

    for q in range(4):
        aden[pl.ds(q * C, C), :] = upacc[:, q * C : (q + 1) * C]
        aden[pl.ds((4 + q) * C, C), :] = dtacc[:, q * C : (q + 1) * C].T
    rd1()

    tapacc[...] = jnp.zeros_like(tapacc)

    @pl.loop(0, RR)
    def _(r):
        @pl.loop(0, 4)
        def _(cb):
            d = ext2[rows(((r + 3) * EC + 3 + cb * 8) * G, 8 * G), :].reshape(8, G, C)
            for a in range(7):
                for b in range(7):
                    x = ext[rows(((r + a) * EC + cb * 8 + b) * G, 8 * G), :]
                    p = x.reshape(8, G, C) * d
                    t = tree([p[i] for i in range(8)]).astype(F32)
                    tapacc[7 * a + b] += t[:8] + t[8:]

        pl.when(r == 1)(rs4)
        pl.when(r == 2)(rd2)
        pl.when(r == 6)(rd3)

    rs5()

    def tap_stage(buf, peers, me):
        sem = take(len(peers))

        def start(value):
            buf[me] = value.astype(BF16)
            for i, (_, to) in enumerate(peers):
                remote(buf.at[me], buf.at[me], sem + i, to).start()

        def finish():
            for i, (frm, to) in enumerate(peers):
                copy = remote(buf.at[me], buf.at[frm], sem + i, to)
                copy.wait_send()
                copy.wait_recv()
            out = buf[0].astype(F32)
            for i in range(1, buf.shape[0]):
                out = out + buf[i].astype(F32)
            return out

        return start, finish

    lat_peers = [(lax.rem(lat + 4 - j, 4), (lax.rem(lat + j, 4), lon)) for j in range(1, 4)]
    hi_peers = [(lax.rem(hi + NH - j, NH), hi_peer(j)[1]) for j in range(1, NH)]
    z_peers = [(lax.rem(z + NZ - j, NZ), z_peer(j)[1]) for j in range(1, NZ)]
    tl_start, tl_finish = tap_stage(tl, lat_peers, lat)
    th_start, th_finish = tap_stage(th, hi_peers, hi)
    tz_start, tz_finish = tap_stage(tz, z_peers, z)
    tl_start(jnp.concatenate([jnp.sum(tapacc[...], axis=1), jnp.zeros((15, C), F32)], axis=0))

    halo_wait(halo2)

    @pl.when(south)
    def _():
        drs[...] = jnp.zeros_like(drs)
        dsl[...] = jnp.zeros_like(dsl)
        dsr[...] = jnp.zeros_like(dsr)

    @pl.when(north)
    def _():
        drn[...] = jnp.zeros_like(drn)
        dnl[...] = jnp.zeros_like(dnl)
        dnr[...] = jnp.zeros_like(dnr)

    @pl.loop(0, RR)
    def _(r):
        for j in range(3):
            ext2[rows(((r + 3) * EC + j) * G, G), :] = dcl[r, j]
            ext2[rows(((r + 3) * EC + 3 + CC + j) * G, G), :] = dcr[r, j]
            d32[rows((r * EC + j) * G, G), :] = dcl[r, j].astype(F32)
            d32[rows((r * EC + 3 + CC + j) * G, G), :] = dcr[r, j].astype(F32)

    fg1, fg2, fg3 = fold_exchange(fg, hr1, hs2, hr2, CC)

    @pl.when(north)
    def _():
        for i in range(3):
            for cut, at in ((0, 0), (8, 8), (16, 16), (24, 24), (30, 30)):
                zbuf[i, pl.ds(at, 8), :] = d32[pl.ds(((5 + i) * EC + cut) * G + 15, 8, stride=G), :]
        for k in range(1, 4):
            total_ = None
            for a in range(k + 3, 7):
                for b in range(7):
                    term = zbuf[k - a + 5, pl.ds(6 - b, CC), :] * tapf[7 * a + b : 7 * a + b + 1]
                    total_ = term if total_ is None else total_ + term
            fg[k - 1] = total_.astype(BF16)
        fg1()

    for k in range(6):
        low = k < 3
        r = k + 5 if low else k - 3
        edge, el, er = (drs, dsl, dsr) if low else (drn, dnl, dnr)
        i = k if low else k - 3
        line = 7 if low else 24
        for c in range(EC):
            sh[pl.ds(c * 32 + 8, G), :] = d32[pl.ds((r * EC + c) * G, G), :]
        sh[pl.ds(3 * 32 + line, CC, stride=32), :] = edge[i].astype(F32)
        lft, rgt = el[i].astype(F32), er[i].astype(F32)
        for j in range(3):
            sh[pl.ds(j * 32 + line, 1), :] = lft[13 + j : 14 + j]
            sh[pl.ds((CC + 3 + j) * 32 + line, 1), :] = rgt[j : j + 1]
        to = k if low else k + 8
        for c in range(EC):
            ext2[pl.ds((to * EC + c) * G, G), :] = sh[pl.ds(c * 32 + (7 if low else 9), G), :].astype(BF16)

    @pl.loop(0, RR)
    def _(r):
        @pl.loop(0, 4)
        def _(cb):
            v = conv(ext2, r, cb, True)
            v = v + direct[rows((r * CC + cb * 8) * G, 8 * G), :].astype(F32).reshape(8, G, C)
            for j in range(8):
                obuf[pl.ds(r * CC + cb * 8 + j, G, stride=RR * CC), :] = v[j]

        @pl.when(r == 0)
        def _():
            rs6()
            rd4()

        @pl.when(r == 1)
        def _():
            th_start(tl_finish())
            pl.when(north)(fg2)

        pl.when(r == 3)(rd5)

        @pl.when(r == 5)
        def _():
            tz_start(th_finish())
            rd6()

        @pl.when(r == 6)
        def _():
            rs7(gsec)

    @pl.when(north)
    def _():
        off = fg3()
        for k in range(1, 4):
            for i in range(CC):
                at = pl.ds((128 - k) * CC + i, 1)
                obuf[at, :] += fcat[k - 1, pl.ds(off + CC - 1 - i, 1), :]

    @pl.loop(0, 128)
    def _(i):
        gfield[i] = obuf[rows(i * CC, CC), :].astype(BF16)

    rd7(aden)
    for q in range(4):
        gup[:, q * C : (q + 1) * C] = aden[pl.ds(q * C, C), :]
    gdown[...] = aden[pl.ds(4 * C, 4 * C), :]
    gtaps[...] = tz_finish()[:49] * factor


def on_device(field, land, mirror, depth_weight, norm_gain, up_weight, up_bias, down_proj, layer_scale, section_gain, section_weight, section_bias, cotangent):
    factor = 1.0 / math.sqrt(512 * 2048 / 64.0)
    vm = pl.BlockSpec(memory_space=pltpu.VMEM)
    n = RR * CC * G

    def f(*shape):
        return pltpu.VMEM(shape, F32)

    def h(*shape):
        return pltpu.VMEM(shape, BF16)

    sems = 128
    scratch = dict(
        field=h(128, CC, C),
        land=pltpu.VMEM((CC, 128), jnp.int32),
        taps_in=h(49, C),
        gain_in=h(1, C),
        up=h(C, 512),
        bias_in=h(512),
        down=h(512, C),
        scale_in=h(1, C),
        sgain_in=h(3, C),
        sw=h(3, 512, C),
        sbias_in=h(3, C),
        cot=h(G, 4, C),
        lsem=pltpu.SemaphoreType.DMA((12,)),
        fbuf=f(134 * PITCH, C),
        d32=f(RR * EC * G, C),
        obuf=f(n, C),
        sh=f(EC * 32, C),
        hat=f(n, C),
        rstd=f(n, C),
        landb=f(n, C),
        hat1=f(n, C),
        rstd1=f(n, C),
        hat2=f(n // 4, C),
        rstd2=f(n // 4, C),
        hat3=f(n // 16, C),
        rstd3=f(n // 16, C),
        dgb=h(RR, CC, G, C),
        upacc=f(C, 512),
        dtacc=f(C, 512),
        secacc=f(3, C, 512),
        tapacc=f(49, 8, C),
        lt=f(C, C),
        cb32=f(64, C),
        cotb=h(64, C),
        asec=f(1536, C),
        aden=f(1024, C),
        sec_s1=h(1536, C),
        sec_r1=h(768, C),
        sec_s2f=f(768, C),
        sec_s2=h(768, C),
        sec_r2=h(384, C),
        sec_s3=h(384, C),
        sec_r3=h(NH, 48, C),
        sec_r4=h(NZ, 48, C),
        sec_g3=h(NH, 48, C),
        sec_g2=h(NH, 48, C),
        sec_g1a=h(NH, 48, C),
        sec_g1b=h(NH, 48, C),
        den_s1=h(1024, C),
        den_r1=h(512, C),
        den_s2f=f(512, C),
        den_s2=h(512, C),
        den_r2=h(256, C),
        den_s3=h(256, C),
        den_r3=h(NH, 32, C),
        den_r4=h(NZ, 32, C),
        den_g3=h(NH, 32, C),
        den_g2=h(NH, 32, C),
        den_g1a=h(NH, 32, C),
        den_g1b=h(NH, 32, C),
        tl=h(4, 64, C),
        th=h(NH, 64, C),
        tz=h(NZ, 64, C),
        stl=h(3, 128, C),
        str_=h(3, 128, C),
        cl=h(3, 128, C),
        cr=h(3, 128, C),
        rs=h(3, CC, C),
        rn=h(3, CC, C),
        csl=h(3, 16, C),
        csr=h(3, 16, C),
        cnl=h(3, 16, C),
        cnr=h(3, 16, C),
        dcl=h(RR, 3, G, C),
        dcr=h(RR, 3, G, C),
        rst=h(3, CC, C),
        rsb=h(3, CC, C),
        drs=h(3, CC, C),
        drn=h(3, CC, C),
        dsl=h(3, 16, C),
        dsr=h(3, 16, C),
        dnl=h(3, 16, C),
        dnr=h(3, 16, C),
        fr1=h(NH, 3, CC, C),
        fs2=h(NZ - 1, 3, CC, C),
        fr2=h(NZ, 3, CC, C),
        fcat=f(3, 3 * CC, C),
        zbuf=f(3, 40, C),
        fg=h(3, CC, C),
        hr1=h(NH, 3, CC, C),
        hs2=h(NZ - 1, 3, CC, C),
        hr2=h(NZ, 3, CC, C),
        ssem=pltpu.SemaphoreType.DMA((sems,)),
        rsem=pltpu.SemaphoreType.DMA((sems,)),
    )
    scoped = dict(
        ext=h(ER * EC * G, C),
        ext2=h(ER * EC * G, C),
        wb=h(49, G, C),
        normed=h(n, C),
        act=h(n, 512),
        slope=h(n, 512),
        lev0=h(n, C),
        lev1=h(n // 4, C),
        lev2=h(n // 16, C),
        p1=h(n // 4, 512),
        p2=h(n // 16, 512),
        p3=h(n // 64, 512),
        back1=h(n // 4, C),
        back2=h(n // 16, C),
        direct=h(n, C),
    )

    def whole(*refs):
        pl.run_scoped(functools.partial(kernel, factor, *refs), **scoped)

    bott, gfield, gtaps, gup, gdown, gsec = pl.pallas_call(
        whole,
        out_shape=(
            jax.ShapeDtypeStruct((G, 4, C), BF16),
            jax.ShapeDtypeStruct((128, CC, C), BF16),
            jax.ShapeDtypeStruct((49, C), F32),
            jax.ShapeDtypeStruct((C, 512), F32),
            jax.ShapeDtypeStruct((512, C), F32),
            jax.ShapeDtypeStruct((1536, C), F32),
        ),
        in_specs=[pl.BlockSpec(memory_space=pltpu.SMEM)] + [pl.BlockSpec(memory_space=pltpu.HBM)] * 12,
        out_specs=(vm,) * 6,
        scratch_shapes=list(scratch.values()),
        compiler_params=pltpu.CompilerParams(
            collective_id=0, has_side_effects=True, vmem_limit_bytes=50 * 1024 * 1024
        ),
    )(
        mirror,
        *(
            pltpu.with_memory_space_constraint(v, pltpu.HBM)
            for v in (
                field,
                land.T,
                depth_weight,
                norm_gain.reshape(1, C),
                up_weight,
                up_bias,
                down_proj,
                layer_scale.reshape(1, C),
                section_gain,
                section_weight,
                section_bias,
                cotangent,
            )
        ),
    )
    results = (bott, gfield, gtaps, gup, gdown, gsec)
    anywhere = pl.BlockSpec(memory_space=pl.ANY)

    def write(*refs):
        copies = [pltpu.make_async_copy(refs[i], refs[6 + i], refs[12].at[i]) for i in range(6)]
        for copy in copies:
            copy.start()
        for copy in copies:
            copy.wait()

    bott, gfield, gtaps, gup, gdown, gsec = pl.pallas_call(
        write,
        out_shape=tuple(jax.ShapeDtypeStruct(x.shape, x.dtype) for x in results),
        in_specs=[vm] * 6,
        out_specs=(anywhere,) * 6,
        scratch_shapes=[pltpu.SemaphoreType.DMA((6,))],
        compiler_params=pltpu.CompilerParams(vmem_limit_bytes=16 * 1024 * 1024),
    )(*results)
    return bott, gfield, gtaps, gup, gdown, gsec.reshape(3, 512, C)


def solution(mesh):
    cell = P("lat", "lon", None)
    in_specs = (cell, P("lat", "lon")) + (P(),) * 10 + (cell,)
    out_specs = (cell, cell, P(), P(), P(), P())
    return jax.shard_map(
        on_device, mesh=mesh, in_specs=in_specs, out_specs=out_specs, check_vma=False
    )
```

```python
import functools
import math

import jax
import jax.numpy as jnp
from jax import lax
from jax.experimental import pallas as pl
from jax.experimental.pallas import tpu as pltpu
from jax.sharding import PartitionSpec as P

MESH = pl.DeviceIdType.MESH
F32 = jnp.float32
BF16 = jnp.bfloat16
epsilon = 1e-06

G = 16
RR = 8
CC = 32
C = 128
PITCH = 48
EC = CC + 6
ER = RR + 6
NZ = 8
NH = 8
M = 512
CHUNKS = RR * CC * G // M
POS = M // G


def mean_mx(values):
    ones = jnp.full((C, C), 1.0 / C, BF16)
    return dot(values.astype(BF16), ones, 1, 0)


def norm_parts(values, exact=False):
    mean = mean_mx(values) if exact else jnp.mean(values, axis=-1, keepdims=True)
    center = values - mean
    rstd = lax.rsqrt(jnp.mean(center * center, axis=-1, keepdims=True) + epsilon)
    return center * rstd, rstd


def norm_back(grad_hat, normed_hat, rstd):
    second = jnp.mean(grad_hat * normed_hat, axis=-1, keepdims=True)
    return rstd * (grad_hat - mean_mx(grad_hat) - normed_hat * second)


def norm_back_wide(grad_hat, normed_hat, rstd):
    pair = jnp.concatenate([grad_hat.astype(BF16), (grad_hat * normed_hat).astype(BF16)], axis=1)
    ones, zeros = jnp.full((C, C), 1.0 / C, BF16), jnp.zeros((C, C), BF16)
    both = jnp.concatenate(
        [jnp.concatenate([ones, zeros], axis=1), jnp.concatenate([zeros, ones], axis=1)], axis=0
    )
    means = dot(pair, both, 1, 0)
    return rstd * (grad_hat - means[:, :C] - normed_hat * means[:, C:])


def gelu_parts(h):
    h = h.astype(BF16)
    e = jnp.exp2(h * h * jnp.asarray(-0.7213475204444817, BF16))
    cdf = jnp.asarray(0.5, BF16) + jnp.asarray(0.5, BF16) * lax.erf(h * jnp.asarray(0.7071067811865476, BF16))
    return h * cdf, cdf + h * (e * jnp.asarray(0.3989422804014327, BF16))


def tree(terms):
    while len(terms) > 1:
        terms = [a + b for a, b in zip(terms[::2], terms[1::2])] + terms[len(terms) & ~1 :]
    return terms[0]


def dot(a, b, ca, cb):
    return lax.dot_general(a, b, (((ca,), (cb,)), ((), ())), preferred_element_type=F32)


def rows(start, size, align=16):
    return pl.ds(pl.multiple_of(start, align), size)


def kernel(
    factor,
    mirror,
    x_field,
    x_land,
    x_taps_in,
    x_gain_in,
    x_up,
    x_bias_in,
    x_down,
    x_scale_in,
    x_sgain_in,
    x_sw,
    x_sbias_in,
    x_cot,
    bott,
    gfield,
    gtaps,
    gup,
    gdown,
    gsec,
    field,
    land,
    taps_in,
    gain_in,
    up,
    bias_in,
    down,
    scale_in,
    sgain_in,
    sw,
    sbias_in,
    cot,
    lsem,
    fbuf,
    d32,
    obuf,
    sh,
    hat,
    rstd,
    landb,
    hat1,
    rstd1,
    hat2,
    rstd2,
    hat3,
    rstd3,
    dgb,
    upacc,
    dtacc,
    secacc,
    tapacc,
    lt,
    cb32,
    cotb,
    asec,
    aden,
    sec_s1,
    sec_rq,
    sec_s3,
    sec_r3,
    sec_r4,
    sec_g3,
    sec_ga,
    den_s1,
    den_rq,
    den_s3,
    den_r3,
    den_r4,
    den_g3,
    den_ga,
    tl,
    th,
    tz,
    stl,
    str_,
    cl,
    cr,
    rs,
    rn,
    csl,
    csr,
    cnl,
    cnr,
    dcl,
    dcr,
    rst,
    rsb,
    drs,
    drn,
    dsl,
    dsr,
    dnl,
    dnr,
    fr1,
    fs2,
    fr2,
    fcat,
    zbuf,
    fg,
    hr1,
    hs2,
    hr2,
    ssem,
    rsem,
    ext,
    ext2,
    wb,
    normed,
    act,
    slope,
    lev0,
    lev1,
    lev2,
    p1,
    p2,
    p3,
    back1,
    back2,
    direct,
):
    loads = [
        pltpu.make_async_copy(a, b, lsem.at[i])
        for i, (a, b) in enumerate(
            (
                (x_field, field),
                (x_land, land),
                (x_taps_in, taps_in),
                (x_gain_in, gain_in),
                (x_up, up),
                (x_bias_in, bias_in),
                (x_down, down),
                (x_scale_in, scale_in),
                (x_sgain_in, sgain_in),
                (x_sw, sw),
                (x_sbias_in, sbias_in),
                (x_cot, cot),
            )
        )
    ]
    for copy in loads:
        copy.start()

    lat = lax.axis_index("lat")
    lon = lax.axis_index("lon")
    hi, z = lon // NZ, lax.rem(lon, NZ)
    core, xl = lax.rem(lat, 2), lat // 2
    right, left = lax.rem(lon + 1, NH * NZ), lax.rem(lon + NH * NZ - 1, NH * NZ)
    north, south = lat == 3, lat == 0

    counter = [0]

    def take(n):
        counter[0] += n
        return counter[0] - n

    def remote(src, dst, sem, to):
        return pltpu.make_async_remote_copy(
            src_ref=src,
            dst_ref=dst,
            send_sem=ssem.at[sem],
            recv_sem=rsem.at[sem],
            device_id=to,
            device_id_type=MESH,
        )

    def hi_peer(j):
        h = lax.rem(hi + j, NH)
        return h, (lat, h * NZ + z)

    def z_peer(j):
        t = lax.rem(z + j, NZ)
        return t, (lat, hi * NZ + t)

    barrier = pltpu.get_barrier_semaphore()

    def greet(to):
        pl.semaphore_signal(barrier, inc=1, device_id=to, device_id_type=MESH)

    greet((lat, left))
    greet((lat, right))
    for dl in (-1, 1):

        @pl.when((lat + dl >= 0) & (lat + dl < 4))
        def _():
            greet((lat + dl, left))
            greet((lat + dl, right))

    for j in range(1, 4):
        greet((lax.rem(lat + j, 4), lon))
    for j in range(1, NH):
        greet(hi_peer(j)[1])
    for j in range(1, NZ):
        greet(z_peer(j)[1])

    loads[0].wait()

    @pl.loop(0, 128)
    def _(i):
        fbuf[rows((i + 3) * PITCH + 8, CC, 8), :] = field[i].astype(F32)

    for j in range(3):
        stl[j] = fbuf[pl.ds(3 * PITCH + 8 + j, 128, stride=PITCH), :].astype(BF16)
        str_[j] = fbuf[pl.ds(3 * PITCH + 8 + CC - 3 + j, 128, stride=PITCH), :].astype(BF16)

    waits = 2 + 3 + (NH - 1) + (NZ - 1)
    pl.semaphore_wait(barrier, waits + jnp.where(south | north, 2, 4))

    def halo_copies(pieces):
        made = []
        for dl, dn, src, dst in pieces:
            sem = take(1)
            to_lon = right if dn == 1 else left if dn == -1 else lon
            copy = remote(src, dst, sem, (lat + dl, to_lon))
            made.append((dl, copy))
        return made

    def when_lat(dl, ok, fn):
        if dl == 0:
            fn()
        else:
            pl.when(ok)(fn)

    def halo_start(made):
        for dl, copy in made:
            when_lat(dl, (lat + dl >= 0) & (lat + dl < 4), copy.start)

    def halo_wait(made):
        for dl, copy in made:
            when_lat(dl, (lat + dl >= 0) & (lat + dl < 4), copy.wait_send)
            when_lat(dl, (lat - dl >= 0) & (lat - dl < 4), copy.wait_recv)

    halo = halo_copies(
        [
            (0, -1, stl, cr),
            (0, 1, str_, cl),
            (1, 0, field.at[pl.ds(125, 3)], rs),
            (-1, 0, field.at[pl.ds(0, 3)], rn),
            (1, 1, str_.at[:, pl.ds(112, 16)], csl),
            (1, -1, stl.at[:, pl.ds(112, 16)], csr),
            (-1, 1, str_.at[:, pl.ds(0, 16)], cnl),
            (-1, -1, stl.at[:, pl.ds(0, 16)], cnr),
        ]
    )
    halo_start(halo)

    shift = mirror[0]
    total = NH * NZ * CC

    def first_block(dev, width):
        base = lax.rem(shift - CC * dev - (width - 1) + (3 if width > CC else 0) + 2 * total, total)
        return base // CC, lax.rem(base, CC)

    def fold_exchange(src, buf1, stage2, buf2, width):
        sem1, sem2 = take(NH - 1), take(NZ - 1)

        def first():
            for j in range(1, NH):
                remote(src, buf1.at[hi], sem1 + j - 1, hi_peer(j)[1]).start()
            buf1[hi] = src[...]

        def held(dev):
            q = first_block(dev, width)[0]
            block = lax.rem(q + lax.rem(z + NH * NZ - q, NZ), NH * NZ)
            return block // NZ

        def second():
            for j in range(1, NH):
                h = lax.rem(hi + NH - j, NH)
                copy = remote(src, buf1.at[h], sem1 + j - 1, hi_peer(j)[1])
                copy.wait_send()
                copy.wait_recv()
            for j in range(1, NZ):
                t, to = z_peer(j)
                stage2[j - 1] = buf1[held(hi * NZ + t)]
                remote(stage2.at[j - 1], buf2.at[z], sem2 + j - 1, to).start()
            buf2[z] = buf1[held(lon)]

        def last():
            for j in range(1, NZ):
                t = lax.rem(z + NZ - j, NZ)
                copy = remote(stage2.at[j - 1], buf2.at[t], sem2 + j - 1, z_peer(j)[1])
                copy.wait_send()
                copy.wait_recv()
            q, off = first_block(lon, width)
            for m in range(3 if width > CC else 2):
                fcat[:, pl.ds(m * CC, CC), :] = buf2[lax.rem(q + m, NZ)].astype(F32)
            return off

        return first, second, last

    fold1, fold2, fold3 = fold_exchange(field.at[pl.ds(125, 3)], fr1, fs2, fr2, CC + 6)
    pl.when(north)(fold1)

    for copy in loads[1:]:
        copy.wait()

    tapf = taps_in[...].astype(F32)
    for t in range(49):
        wb[t] = jnp.broadcast_to(tapf[t : t + 1], (G, C)).astype(BF16)
    gain = gain_in[...].astype(F32)
    bias = bias_in[...].astype(F32).reshape(1, 512)
    scale = scale_in[...].astype(F32)

    lt[...] = jnp.concatenate([land[...].astype(F32), jnp.zeros((C - CC, C), F32)], axis=0).T

    @pl.loop(0, RR)
    def _(r):
        v = lt[pl.ds(r, G, stride=RR), :]
        for c in range(CC):
            landb[rows((r * CC + c) * G, G), :] = jnp.broadcast_to(v[:, c : c + 1], (G, C))

    for g in range(G):
        cb32[pl.ds(g, 4, stride=G), :] = cot[g].astype(F32)
    cotb[...] = cb32[...].astype(BF16)

    def gather_rows(r0, r1, c0, c1):
        @pl.loop(r0, r1)
        def _(r):
            for c in range(c0, c1):
                ext[rows((r * EC + c) * G, G), :] = fbuf[
                    pl.ds(r * PITCH + 5 + c, G, stride=RR * PITCH), :
                ].astype(BF16)

    gather_rows(3, 11, 3, 3 + CC)
    halo_wait(halo)
    for j in range(3):
        fbuf[pl.ds(3 * PITCH + 5 + j, 128, stride=PITCH), :] = cl[j].astype(F32)
        fbuf[pl.ds(3 * PITCH + 8 + CC + j, 128, stride=PITCH), :] = cr[j].astype(F32)

    @pl.when(south)
    def _():
        fbuf[pl.ds(0, 3 * PITCH), :] = jnp.zeros((3 * PITCH, C), F32)

    @pl.when(jnp.logical_not(south))
    def _():
        for k in range(3):
            fbuf[pl.ds(k * PITCH + 8, CC), :] = rs[k].astype(F32)
            for j in range(3):
                fbuf[pl.ds(k * PITCH + 5 + j, 1), :] = csl[j].astype(F32)[13 + k : 14 + k]
                fbuf[pl.ds(k * PITCH + 8 + CC + j, 1), :] = csr[j].astype(F32)[13 + k : 14 + k]

    @pl.when(jnp.logical_not(north))
    def _():
        for k in range(3):
            fbuf[pl.ds((131 + k) * PITCH + 8, CC), :] = rn[k].astype(F32)
            for j in range(3):
                fbuf[pl.ds((131 + k) * PITCH + 5 + j, 1), :] = cnl[j].astype(F32)[k : k + 1]
                fbuf[pl.ds((131 + k) * PITCH + 8 + CC + j, 1), :] = cnr[j].astype(F32)[k : k + 1]

    gather_rows(0, 3, 0, EC)
    gather_rows(3, 11, 0, 3)
    gather_rows(3, 11, 3 + CC, EC)
    pl.when(north)(fold2)

    def last_rows():
        @pl.when(north)
        def _():
            off = fold3()
            for k in range(3):
                for i in range(EC):
                    fbuf[pl.ds((131 + k) * PITCH + 5 + i, 1), :] = fcat[2 - k, pl.ds(off + EC - 1 - i, 1), :]

        gather_rows(11, 14, 0, EC)

    def conv(src, r, cb, flip):
        outs = []
        for c in range(8):
            total_ = None
            for group in ((0, 1), (2, 3), (4, 5, 6)):
                terms = []
                for a in group:
                    line = []
                    for b in range(7):
                        t = 48 - (7 * a + b) if flip else 7 * a + b
                        x = src[rows(((r + a) * EC + cb * 8 + c + b) * G, G), :].reshape(1, G, C)
                        line.append(x * wb[t][None])
                    terms.append(tree(line))
                term = tree(terms).astype(F32)
                total_ = term if total_ is None else total_ + term
            outs.append(total_)
        return jnp.concatenate(outs, axis=0)

    @pl.loop(0, RR)
    def _(r):
        pl.when(r == 5)(last_rows)

        @pl.loop(0, 4)
        def _(cb):
            hat[rows((r * CC + cb * 8) * G, 8 * G), :] = conv(ext, r, cb, False).reshape(8 * G, C)

    def forward1(k):
        at = rows(k * M, M)
        dh, ds = norm_parts(hat[at, :])
        hat[at, :] = dh
        rstd[at, :] = jnp.broadcast_to(ds, dh.shape)
        nm = (dh * gain).astype(BF16)
        normed[at, :] = nm
        active, slp = gelu_parts(dot(nm, up[...], 1, 0) + bias)
        act[at, :] = active
        slope[at, :] = slp
        return active

    def forward2(k, active):
        at = rows(k * M, M)
        mixed = dot(active, down[...], 1, 0)
        x = ext[rows(((k + 3) * EC + 3) * G, M), :].astype(F32)
        lev0[at, :] = (landb[at, :] * (x + scale * mixed)).astype(BF16)

    @pl.loop(0, CHUNKS)
    def _(k):
        forward2(k, forward1(k))

    def section(s, count, cols, src, hats, rstds, patches, put):
        sg = sgain_in[s : s + 1].astype(F32)
        sb = sbias_in[s : s + 1].astype(F32)
        n = cols * G
        half = cols // 2

        def step(i):
            parts = []
            for a in range(2):
                at = rows((2 * i + a) * n, n)
                h, rs_ = norm_parts(src[at, :].astype(F32), True)
                hats[at, :] = h
                rstds[at, :] = jnp.broadcast_to(rs_, h.shape)
                sn = (h * sg).astype(BF16).reshape(half, 2, G, C)
                parts += [sn[:, b].reshape(half * G, C) for b in range(2)]
            p = jnp.concatenate(parts, axis=1)
            patches[rows(i * half * G, half * G), :] = p
            put(i, (dot(p, sw[s], 1, 0) + sb).astype(BF16))

        if count == 1:
            step(0)
        else:
            pl.loop(0, count)(step)

    def put1(i, v):
        lev1[rows(i * 256, 256), :] = v

    def put2(i, v):
        lev2[rows(i * 128, 128), :] = v

    def put3(i, v):
        v = v.astype(F32)
        for j in range(4):
            cb32[pl.ds(j, G, stride=4), :] = v[j * G : (j + 1) * G]
        for g in range(G):
            bott[g] = cb32[pl.ds(g * 4, 4), :].astype(BF16)

    section(0, 4, 32, lev0, hat1, rstd1, p1, put1)
    section(1, 2, 16, lev1, hat2, rstd2, p2, put2)
    section(2, 1, 8, lev2, hat3, rstd3, p3, put3)

    def section_back(s, count, cols, src, hats, rstds, patches, put):
        sg = sgain_in[s : s + 1].astype(F32)
        n = cols * G
        half = cols // 2
        secacc[s] = jnp.zeros((C, 4 * C), F32)

        def step(i):
            at = rows(i * half * G, half * G)
            u = src[at, :]
            secacc[s] += dot(u, patches[at, :], 0, 0)
            spread = dot(u, sw[s], 1, 1)
            for a in range(2):
                at2 = rows((2 * i + a) * n, n)
                hh = hats[at2, :].reshape(half, 2, G, C)
                rr = rstds[at2, :].reshape(half, 2, G, C)
                outs = []
                for b in range(2):
                    q = 2 * a + b
                    g = spread[:, q * C : (q + 1) * C] * sg
                    back = norm_back(g, hh[:, b].reshape(half * G, C), rr[:, b].reshape(half * G, C))
                    outs.append(back.astype(BF16).reshape(half, G, C))
                put(at2, jnp.stack(outs, axis=1).reshape(n, C))

        if count == 1:
            step(0)
        else:
            pl.loop(0, count)(step)

    def putb2(at, v):
        back2[at, :] = v

    def putb1(at, v):
        back1[at, :] = v

    def putb0(at, v):
        direct[at, :] = (landb[at, :] * v.astype(F32)).astype(BF16)

    section_back(2, 1, 8, cotb, hat3, rstd3, p3, putb2)
    section_back(1, 2, 16, back2, hat2, rstd2, p2, putb1)
    section_back(0, 4, 32, back1, hat1, rstd1, p1, putb0)

    bsec = dict(s1=sec_s1, rq=sec_rq, s3=sec_s3, r3=sec_r3, r4=sec_r4, g3=sec_g3, ga=sec_ga)
    bden = dict(s1=den_s1, rq=den_rq, s3=den_s3, r3=den_r3, r4=den_r4, g3=den_g3, ga=den_ga)
    def reduction(size, full, b):
        quarter, piece = size // 4, size // 32
        sem1, sem6 = take(3), take(3)
        sem3, sem4, sem5 = take(NH - 1), take(NZ - 1), take(NH - 1)

        def lat_peer(j):
            to = lax.rem(lat + j, 4)
            return to, (to, lon)

        def first():
            b["s1"][...] = full[...].astype(BF16)
            for j in range(1, 4):
                t, to = lat_peer(j)
                remote(b["s1"].at[rows(t * quarter, quarter)], b["rq"].at[lat], sem1 + j - 1, to).start()

        def third():
            total_ = full[rows(lat * quarter, quarter), :]
            for j in range(1, 4):
                frm = lax.rem(lat + 4 - j, 4)
                copy = remote(b["s1"].at[pl.ds(0, quarter)], b["rq"].at[frm], sem1 + j - 1, lat_peer(j)[1])
                copy.wait_send()
                copy.wait_recv()
                total_ = total_ + b["rq"][frm].astype(F32)
            b["s3"][...] = total_.astype(BF16)
            for j in range(1, NH):
                h, to = hi_peer(j)
                remote(b["s3"].at[rows(h * piece, piece)], b["r3"].at[hi], sem3 + j - 1, to).start()
            b["r3"][hi] = b["s3"][rows(hi * piece, piece), :]

        def total8(buf):
            part = buf[0].astype(F32)
            for i in range(1, 8):
                part = part + buf[i].astype(F32)
            return part.astype(BF16)

        def fourth():
            for j in range(1, NH):
                h = lax.rem(hi + NH - j, NH)
                copy = remote(b["s3"].at[pl.ds(0, piece)], b["r3"].at[h], sem3 + j - 1, hi_peer(j)[1])
                copy.wait_send()
                copy.wait_recv()
            b["r4"][z] = total8(b["r3"])
            for j in range(1, NZ):
                remote(b["r4"].at[z], b["r4"].at[z], sem4 + j - 1, z_peer(j)[1]).start()

        def fifth():
            for j in range(1, NZ):
                t = lax.rem(z + NZ - j, NZ)
                copy = remote(b["r4"].at[z], b["r4"].at[t], sem4 + j - 1, z_peer(j)[1])
                copy.wait_send()
                copy.wait_recv()
            b["g3"][hi] = total8(b["r4"])
            for j in range(1, NH):
                remote(b["g3"].at[hi], b["g3"].at[hi], sem5 + j - 1, hi_peer(j)[1]).start()

        def sixth():
            for j in range(1, NH):
                h = lax.rem(hi + NH - j, NH)
                copy = remote(b["g3"].at[hi], b["g3"].at[h], sem5 + j - 1, hi_peer(j)[1])
                copy.wait_send()
                copy.wait_recv()
            for j in range(1, 4):
                remote(b["g3"], b["ga"].at[lat], sem6 + j - 1, lat_peer(j)[1]).start()

        def last(out):
            def place(t, v):
                out[rows(t * quarter, quarter), :] = v.reshape(quarter, C).astype(F32) * factor

            place(lat, b["g3"][...])
            for j in range(1, 4):
                frm = lax.rem(lat + 4 - j, 4)
                copy = remote(b["g3"], b["ga"].at[frm], sem6 + j - 1, lat_peer(j)[1])
                copy.wait_send()
                copy.wait_recv()
                place(frm, b["ga"][frm])

        return first, third, fourth, fifth, sixth, last

    rs1, rs3, rs4, rs5, rs6, rs7 = reduction(1536, asec, bsec)
    rd1, rd3, rd4, rd5, rd6, rd7 = reduction(1024, aden, bden)

    for s in range(3):
        for q in range(4):
            asec[pl.ds((4 * s + q) * C, C), :] = secacc[s, :, q * C : (q + 1) * C].T
    rs1()

    upacc[...] = jnp.zeros_like(upacc)
    dtacc[...] = jnp.zeros_like(dtacc)

    def backward1(k):
        at = rows(k * M, M)
        mg = (direct[at, :].astype(F32) * scale).astype(BF16)
        dtacc[...] += dot(mg, act[at, :], 0, 0)
        return (dot(mg, down[...], 1, 1) * slope[at, :].astype(F32)).astype(BF16)

    def backward2(k, hg):
        at = rows(k * M, M)
        upacc[...] += dot(normed[at, :], hg, 0, 0)
        ng = dot(hg, up[...], 1, 1) * gain
        dg = norm_back_wide(ng, hat[at, :], rstd[at, :]).astype(BF16)
        dgb[k] = dg.reshape(POS, G, C)
        ext2[rows(((k + 3) * EC + 3) * G, M), :] = dg
        d32[rows((k * EC + 3) * G, M), :] = dg.astype(F32)

    @pl.loop(0, CHUNKS)
    def _(k):
        backward2(k, backward1(k))
        pl.when(k == 4)(rs3)

    for i in range(3):
        rst[i] = d32[pl.ds(((5 + i) * EC + 3) * G + 15, CC, stride=G), :].astype(BF16)
        rsb[i] = d32[pl.ds((i * EC + 3) * G, CC, stride=G), :].astype(BF16)

    halo2 = halo_copies(
        [
            (0, -1, dgb.at[:, pl.ds(0, 3)], dcr),
            (0, 1, dgb.at[:, pl.ds(CC - 3, 3)], dcl),
            (1, 0, rst, drs),
            (-1, 0, rsb, drn),
            (1, 1, rst.at[:, pl.ds(16, 16)], dsl),
            (1, -1, rst.at[:, pl.ds(0, 16)], dsr),
            (-1, 1, rsb.at[:, pl.ds(16, 16)], dnl),
            (-1, -1, rsb.at[:, pl.ds(0, 16)], dnr),
        ]
    )
    halo_start(halo2)

    for q in range(4):
        aden[pl.ds(q * C, C), :] = upacc[:, q * C : (q + 1) * C]
        aden[pl.ds((4 + q) * C, C), :] = dtacc[:, q * C : (q + 1) * C].T
    rd1()

    tapacc[...] = jnp.zeros_like(tapacc)

    @pl.loop(0, RR)
    def _(r):
        @pl.loop(0, 4)
        def _(cb):
            d = ext2[rows(((r + 3) * EC + 3 + cb * 8) * G, 8 * G), :].reshape(8, G, C)
            for a in range(7):
                for b in range(7):
                    x = ext[rows(((r + a) * EC + cb * 8 + b) * G, 8 * G), :]
                    p = x.reshape(8, G, C) * d
                    t = tree([p[i] for i in range(8)]).astype(F32)
                    tapacc[7 * a + b] += t[:8] + t[8:]

        pl.when(r == 1)(rs4)
        pl.when(r == 4)(rd3)
        pl.when(r == 6)(rs5)

    def tap_stage(buf, peers, me):
        sem = take(len(peers))

        def start(value):
            buf[me] = value.astype(BF16)
            for i, (_, to) in enumerate(peers):
                remote(buf.at[me], buf.at[me], sem + i, to).start()

        def finish():
            for i, (frm, to) in enumerate(peers):
                copy = remote(buf.at[me], buf.at[frm], sem + i, to)
                copy.wait_send()
                copy.wait_recv()
            out = buf[0].astype(F32)
            for i in range(1, buf.shape[0]):
                out = out + buf[i].astype(F32)
            return out

        return start, finish

    lat_peers = [(lax.rem(lat + 4 - j, 4), (lax.rem(lat + j, 4), lon)) for j in range(1, 4)]
    hi_peers = [(lax.rem(hi + NH - j, NH), hi_peer(j)[1]) for j in range(1, NH)]
    z_peers = [(lax.rem(z + NZ - j, NZ), z_peer(j)[1]) for j in range(1, NZ)]
    tl_start, tl_finish = tap_stage(tl, lat_peers, lat)
    th_start, th_finish = tap_stage(th, hi_peers, hi)
    tz_start, tz_finish = tap_stage(tz, z_peers, z)
    tl_start(jnp.concatenate([jnp.sum(tapacc[...], axis=1), jnp.zeros((15, C), F32)], axis=0))

    halo_wait(halo2)

    @pl.when(south)
    def _():
        drs[...] = jnp.zeros_like(drs)
        dsl[...] = jnp.zeros_like(dsl)
        dsr[...] = jnp.zeros_like(dsr)

    @pl.when(north)
    def _():
        drn[...] = jnp.zeros_like(drn)
        dnl[...] = jnp.zeros_like(dnl)
        dnr[...] = jnp.zeros_like(dnr)

    @pl.loop(0, RR)
    def _(r):
        for j in range(3):
            ext2[rows(((r + 3) * EC + j) * G, G), :] = dcl[r, j]
            ext2[rows(((r + 3) * EC + 3 + CC + j) * G, G), :] = dcr[r, j]
            d32[rows((r * EC + j) * G, G), :] = dcl[r, j].astype(F32)
            d32[rows((r * EC + 3 + CC + j) * G, G), :] = dcr[r, j].astype(F32)

    fg1, fg2, fg3 = fold_exchange(fg, hr1, hs2, hr2, CC)

    @pl.when(north)
    def _():
        for i in range(3):
            for cut, at in ((0, 0), (8, 8), (16, 16), (24, 24), (30, 30)):
                zbuf[i, pl.ds(at, 8), :] = d32[pl.ds(((5 + i) * EC + cut) * G + 15, 8, stride=G), :]
        for k in range(1, 4):
            total_ = None
            for a in range(k + 3, 7):
                for b in range(7):
                    term = zbuf[k - a + 5, pl.ds(6 - b, CC), :] * tapf[7 * a + b : 7 * a + b + 1]
                    total_ = term if total_ is None else total_ + term
            fg[k - 1] = total_.astype(BF16)
        fg1()

    for k in range(6):
        low = k < 3
        r = k + 5 if low else k - 3
        edge, el, er = (drs, dsl, dsr) if low else (drn, dnl, dnr)
        i = k if low else k - 3
        line = 7 if low else 24
        for c in range(EC):
            sh[pl.ds(c * 32 + 8, G), :] = d32[pl.ds((r * EC + c) * G, G), :]
        sh[pl.ds(3 * 32 + line, CC, stride=32), :] = edge[i].astype(F32)
        lft, rgt = el[i].astype(F32), er[i].astype(F32)
        for j in range(3):
            sh[pl.ds(j * 32 + line, 1), :] = lft[13 + j : 14 + j]
            sh[pl.ds((CC + 3 + j) * 32 + line, 1), :] = rgt[j : j + 1]
        to = k if low else k + 8
        for c in range(EC):
            ext2[pl.ds((to * EC + c) * G, G), :] = sh[pl.ds(c * 32 + (7 if low else 9), G), :].astype(BF16)

    rd4()

    @pl.loop(0, RR)
    def _(r):
        @pl.loop(0, 4)
        def _(cb):
            v = conv(ext2, r, cb, True)
            v = v + direct[rows((r * CC + cb * 8) * G, 8 * G), :].astype(F32).reshape(8, G, C)
            for j in range(8):
                obuf[pl.ds(r * CC + cb * 8 + j, G, stride=RR * CC), :] = v[j]

        @pl.when(r == 1)
        def _():
            th_start(tl_finish())
            pl.when(north)(fg2)
            rs6()

        pl.when(r == 3)(rd5)

        @pl.when(r == 5)
        def _():
            tz_start(th_finish())
            rs7(gsec)

        pl.when(r == 6)(rd6)

    @pl.when(north)
    def _():
        off = fg3()
        for k in range(1, 4):
            for i in range(CC):
                at = pl.ds((128 - k) * CC + i, 1)
                obuf[at, :] += fcat[k - 1, pl.ds(off + CC - 1 - i, 1), :]

    @pl.loop(0, 128)
    def _(i):
        gfield[i] = obuf[rows(i * CC, CC), :].astype(BF16)

    rd7(aden)
    for q in range(4):
        gup[:, q * C : (q + 1) * C] = aden[pl.ds(q * C, C), :]
    gdown[...] = aden[pl.ds(4 * C, 4 * C), :]
    gtaps[...] = tz_finish()[:49] * factor


def on_device(field, land, mirror, depth_weight, norm_gain, up_weight, up_bias, down_proj, layer_scale, section_gain, section_weight, section_bias, cotangent):
    factor = 1.0 / math.sqrt(512 * 2048 / 64.0)
    vm = pl.BlockSpec(memory_space=pltpu.VMEM)
    n = RR * CC * G

    def f(*shape):
        return pltpu.VMEM(shape, F32)

    def h(*shape):
        return pltpu.VMEM(shape, BF16)

    sems = 128
    scratch = dict(
        field=h(128, CC, C),
        land=pltpu.VMEM((CC, 128), jnp.int32),
        taps_in=h(49, C),
        gain_in=h(1, C),
        up=h(C, 512),
        bias_in=h(512),
        down=h(512, C),
        scale_in=h(1, C),
        sgain_in=h(3, C),
        sw=h(3, 512, C),
        sbias_in=h(3, C),
        cot=h(G, 4, C),
        lsem=pltpu.SemaphoreType.DMA((12,)),
        fbuf=f(134 * PITCH, C),
        d32=f(RR * EC * G, C),
        obuf=f(n, C),
        sh=f(EC * 32, C),
        hat=f(n, C),
        rstd=f(n, C),
        landb=f(n, C),
        hat1=f(n, C),
        rstd1=f(n, C),
        hat2=f(n // 4, C),
        rstd2=f(n // 4, C),
        hat3=f(n // 16, C),
        rstd3=f(n // 16, C),
        dgb=h(RR, CC, G, C),
        upacc=f(C, 512),
        dtacc=f(C, 512),
        secacc=f(3, C, 512),
        tapacc=f(49, 8, C),
        lt=f(C, C),
        cb32=f(64, C),
        cotb=h(64, C),
        asec=f(1536, C),
        aden=f(1024, C),
        sec_s1=h(1536, C),
        sec_rq=h(4, 384, C),
        sec_s3=h(384, C),
        sec_r3=h(NH, 48, C),
        sec_r4=h(NZ, 48, C),
        sec_g3=h(NH, 48, C),
        sec_ga=h(4, NH, 48, C),
        den_s1=h(1024, C),
        den_rq=h(4, 256, C),
        den_s3=h(256, C),
        den_r3=h(NH, 32, C),
        den_r4=h(NZ, 32, C),
        den_g3=h(NH, 32, C),
        den_ga=h(4, NH, 32, C),
        tl=h(4, 64, C),
        th=h(NH, 64, C),
        tz=h(NZ, 64, C),
        stl=h(3, 128, C),
        str_=h(3, 128, C),
        cl=h(3, 128, C),
        cr=h(3, 128, C),
        rs=h(3, CC, C),
        rn=h(3, CC, C),
        csl=h(3, 16, C),
        csr=h(3, 16, C),
        cnl=h(3, 16, C),
        cnr=h(3, 16, C),
        dcl=h(RR, 3, G, C),
        dcr=h(RR, 3, G, C),
        rst=h(3, CC, C),
        rsb=h(3, CC, C),
        drs=h(3, CC, C),
        drn=h(3, CC, C),
        dsl=h(3, 16, C),
        dsr=h(3, 16, C),
        dnl=h(3, 16, C),
        dnr=h(3, 16, C),
        fr1=h(NH, 3, CC, C),
        fs2=h(NZ - 1, 3, CC, C),
        fr2=h(NZ, 3, CC, C),
        fcat=f(3, 3 * CC, C),
        zbuf=f(3, 40, C),
        fg=h(3, CC, C),
        hr1=h(NH, 3, CC, C),
        hs2=h(NZ - 1, 3, CC, C),
        hr2=h(NZ, 3, CC, C),
        ssem=pltpu.SemaphoreType.DMA((sems,)),
        rsem=pltpu.SemaphoreType.DMA((sems,)),
    )
    scoped = dict(
        ext=h(ER * EC * G, C),
        ext2=h(ER * EC * G, C),
        wb=h(49, G, C),
        normed=h(n, C),
        act=h(n, 512),
        slope=h(n, 512),
        lev0=h(n, C),
        lev1=h(n // 4, C),
        lev2=h(n // 16, C),
        p1=h(n // 4, 512),
        p2=h(n // 16, 512),
        p3=h(n // 64, 512),
        back1=h(n // 4, C),
        back2=h(n // 16, C),
        direct=h(n, C),
    )

    def whole(*refs):
        pl.run_scoped(functools.partial(kernel, factor, *refs), **scoped)

    bott, gfield, gtaps, gup, gdown, gsec = pl.pallas_call(
        whole,
        out_shape=(
            jax.ShapeDtypeStruct((G, 4, C), BF16),
            jax.ShapeDtypeStruct((128, CC, C), BF16),
            jax.ShapeDtypeStruct((49, C), F32),
            jax.ShapeDtypeStruct((C, 512), F32),
            jax.ShapeDtypeStruct((512, C), F32),
            jax.ShapeDtypeStruct((1536, C), F32),
        ),
        in_specs=[pl.BlockSpec(memory_space=pltpu.SMEM)] + [pl.BlockSpec(memory_space=pltpu.HBM)] * 12,
        out_specs=(vm,) * 6,
        scratch_shapes=list(scratch.values()),
        compiler_params=pltpu.CompilerParams(
            collective_id=0, has_side_effects=True, vmem_limit_bytes=50 * 1024 * 1024
        ),
    )(
        mirror,
        *(
            pltpu.with_memory_space_constraint(v, pltpu.HBM)
            for v in (
                field,
                land.T,
                depth_weight,
                norm_gain.reshape(1, C),
                up_weight,
                up_bias,
                down_proj,
                layer_scale.reshape(1, C),
                section_gain,
                section_weight,
                section_bias,
                cotangent,
            )
        ),
    )
    results = (bott, gfield, gtaps, gup, gdown, gsec)
    anywhere = pl.BlockSpec(memory_space=pl.ANY)

    def write(*refs):
        copies = [pltpu.make_async_copy(refs[i], refs[6 + i], refs[12].at[i]) for i in range(6)]
        for copy in copies:
            copy.start()
        for copy in copies:
            copy.wait()

    bott, gfield, gtaps, gup, gdown, gsec = pl.pallas_call(
        write,
        out_shape=tuple(jax.ShapeDtypeStruct(x.shape, x.dtype) for x in results),
        in_specs=[vm] * 6,
        out_specs=(anywhere,) * 6,
        scratch_shapes=[pltpu.SemaphoreType.DMA((6,))],
        compiler_params=pltpu.CompilerParams(vmem_limit_bytes=16 * 1024 * 1024),
    )(*results)
    return bott, gfield, gtaps, gup, gdown, gsec.reshape(3, 512, C)


def solution(mesh):
    cell = P("lat", "lon", None)
    in_specs = (cell, P("lat", "lon")) + (P(),) * 10 + (cell,)
    out_specs = (cell, cell, P(), P(), P(), P())
    return jax.shard_map(
        on_device, mesh=mesh, in_specs=in_specs, out_specs=out_specs, check_vma=False
    )
```

```python
import functools
import math

import jax
import jax.numpy as jnp
from jax import lax
from jax.experimental import pallas as pl
from jax.experimental.pallas import tpu as pltpu
from jax.sharding import PartitionSpec as P

MESH = pl.DeviceIdType.MESH
F32 = jnp.float32
BF16 = jnp.bfloat16
epsilon = 1e-06

G = 16
RR = 8
CC = 32
C = 128
PITCH = 48
EC = CC + 6
ER = RR + 6
NZ = 8
NH = 8
M = 1024
CHUNKS = RR * CC * G // M
POS = M // G


def mean_mx(values):
    ones = jnp.full((C, C), 1.0 / C, BF16)
    return dot(values.astype(BF16), ones, 1, 0)


def norm_parts(values, exact=False):
    mean = mean_mx(values) if exact else jnp.mean(values, axis=-1, keepdims=True)
    center = values - mean
    rstd = lax.rsqrt(jnp.mean(center * center, axis=-1, keepdims=True) + epsilon)
    return center * rstd, rstd


def norm_back(grad_hat, normed_hat, rstd):
    second = jnp.mean(grad_hat * normed_hat, axis=-1, keepdims=True)
    return rstd * (grad_hat - mean_mx(grad_hat) - normed_hat * second)


def norm_back_wide(grad_hat, normed_hat, rstd):
    pair = jnp.concatenate([grad_hat.astype(BF16), (grad_hat * normed_hat).astype(BF16)], axis=1)
    ones, zeros = jnp.full((C, C), 1.0 / C, BF16), jnp.zeros((C, C), BF16)
    both = jnp.concatenate(
        [jnp.concatenate([ones, zeros], axis=1), jnp.concatenate([zeros, ones], axis=1)], axis=0
    )
    means = dot(pair, both, 1, 0)
    return rstd * (grad_hat - means[:, :C] - normed_hat * means[:, C:])


def gelu_parts(h):
    h = h.astype(BF16)
    e = jnp.exp2(h * h * jnp.asarray(-0.7213475204444817, BF16))
    cdf = jnp.asarray(0.5, BF16) + jnp.asarray(0.5, BF16) * lax.erf(h * jnp.asarray(0.7071067811865476, BF16))
    return h * cdf, cdf + h * (e * jnp.asarray(0.3989422804014327, BF16))


def tree(terms):
    while len(terms) > 1:
        terms = [a + b for a, b in zip(terms[::2], terms[1::2])] + terms[len(terms) & ~1 :]
    return terms[0]


def dot(a, b, ca, cb):
    return lax.dot_general(a, b, (((ca,), (cb,)), ((), ())), preferred_element_type=F32)


def rows(start, size, align=16):
    return pl.ds(pl.multiple_of(start, align), size)


def kernel(
    factor,
    mirror,
    x_field,
    x_land,
    x_taps_in,
    x_gain_in,
    x_up,
    x_bias_in,
    x_down,
    x_scale_in,
    x_sgain_in,
    x_sw,
    x_sbias_in,
    x_cot,
    bott,
    gfield,
    gtaps,
    gup,
    gdown,
    gsec,
    field,
    land,
    taps_in,
    gain_in,
    up,
    bias_in,
    down,
    scale_in,
    sgain_in,
    sw,
    sbias_in,
    cot,
    lsem,
    fbuf,
    d32,
    obuf,
    sh,
    hat,
    rstd,
    landb,
    hat1,
    rstd1,
    hat2,
    rstd2,
    hat3,
    rstd3,
    dgb,
    upacc,
    dtacc,
    secacc,
    tapacc,
    lt,
    cb32,
    cotb,
    asec,
    aden,
    sec_s1,
    sec_rq,
    sec_s3,
    sec_r3,
    sec_r4,
    sec_g3,
    sec_ga,
    den_s1,
    den_rq,
    den_s3,
    den_r3,
    den_r4,
    den_g3,
    den_ga,
    tl,
    th,
    tz,
    stl,
    str_,
    cl,
    cr,
    rs,
    rn,
    csl,
    csr,
    cnl,
    cnr,
    dcl,
    dcr,
    rst,
    rsb,
    drs,
    drn,
    dsl,
    dsr,
    dnl,
    dnr,
    fr1,
    fs2,
    fr2,
    fcat,
    zbuf,
    fg,
    hr1,
    hs2,
    hr2,
    ssem,
    rsem,
    ext,
    ext2,
    wb,
    normed,
    act,
    slope,
    lev0,
    lev1,
    lev2,
    p1,
    p2,
    p3,
    back1,
    back2,
    direct,
):
    loads = [
        pltpu.make_async_copy(a, b, lsem.at[i])
        for i, (a, b) in enumerate(
            (
                (x_field, field),
                (x_land, land),
                (x_taps_in, taps_in),
                (x_gain_in, gain_in),
                (x_up, up),
                (x_bias_in, bias_in),
                (x_down, down),
                (x_scale_in, scale_in),
                (x_sgain_in, sgain_in),
                (x_sw, sw),
                (x_sbias_in, sbias_in),
                (x_cot, cot),
            )
        )
    ]
    for copy in loads:
        copy.start()

    lat = lax.axis_index("lat")
    lon = lax.axis_index("lon")
    hi, z = lon // NZ, lax.rem(lon, NZ)
    core, xl = lax.rem(lat, 2), lat // 2
    right, left = lax.rem(lon + 1, NH * NZ), lax.rem(lon + NH * NZ - 1, NH * NZ)
    north, south = lat == 3, lat == 0

    counter = [0]

    def take(n):
        counter[0] += n
        return counter[0] - n

    def remote(src, dst, sem, to):
        return pltpu.make_async_remote_copy(
            src_ref=src,
            dst_ref=dst,
            send_sem=ssem.at[sem],
            recv_sem=rsem.at[sem],
            device_id=to,
            device_id_type=MESH,
        )

    def hi_peer(j):
        h = lax.rem(hi + j, NH)
        return h, (lat, h * NZ + z)

    def z_peer(j):
        t = lax.rem(z + j, NZ)
        return t, (lat, hi * NZ + t)

    barrier = pltpu.get_barrier_semaphore()

    def greet(to):
        pl.semaphore_signal(barrier, inc=1, device_id=to, device_id_type=MESH)

    greet((lat, left))
    greet((lat, right))
    for dl in (-1, 1):

        @pl.when((lat + dl >= 0) & (lat + dl < 4))
        def _():
            greet((lat + dl, left))
            greet((lat + dl, right))

    for j in range(1, 4):
        greet((lax.rem(lat + j, 4), lon))
    for j in range(1, NH):
        greet(hi_peer(j)[1])
    for j in range(1, NZ):
        greet(z_peer(j)[1])

    loads[0].wait()

    @pl.loop(0, 128)
    def _(i):
        fbuf[rows((i + 3) * PITCH + 8, CC, 8), :] = field[i].astype(F32)

    for j in range(3):
        stl[j] = fbuf[pl.ds(3 * PITCH + 8 + j, 128, stride=PITCH), :].astype(BF16)
        str_[j] = fbuf[pl.ds(3 * PITCH + 8 + CC - 3 + j, 128, stride=PITCH), :].astype(BF16)

    waits = 2 + 3 + (NH - 1) + (NZ - 1)
    pl.semaphore_wait(barrier, waits + jnp.where(south | north, 2, 4))

    def halo_copies(pieces):
        made = []
        for dl, dn, src, dst in pieces:
            sem = take(1)
            to_lon = right if dn == 1 else left if dn == -1 else lon
            copy = remote(src, dst, sem, (lat + dl, to_lon))
            made.append((dl, copy))
        return made

    def when_lat(dl, ok, fn):
        if dl == 0:
            fn()
        else:
            pl.when(ok)(fn)

    def halo_start(made):
        for dl, copy in made:
            when_lat(dl, (lat + dl >= 0) & (lat + dl < 4), copy.start)

    def halo_wait(made):
        for dl, copy in made:
            when_lat(dl, (lat + dl >= 0) & (lat + dl < 4), copy.wait_send)
            when_lat(dl, (lat - dl >= 0) & (lat - dl < 4), copy.wait_recv)

    halo = halo_copies(
        [
            (0, -1, stl, cr),
            (0, 1, str_, cl),
            (1, 0, field.at[pl.ds(125, 3)], rs),
            (-1, 0, field.at[pl.ds(0, 3)], rn),
            (1, 1, str_.at[:, pl.ds(112, 16)], csl),
            (1, -1, stl.at[:, pl.ds(112, 16)], csr),
            (-1, 1, str_.at[:, pl.ds(0, 16)], cnl),
            (-1, -1, stl.at[:, pl.ds(0, 16)], cnr),
        ]
    )
    halo_start(halo)

    shift = mirror[0]
    total = NH * NZ * CC

    def first_block(dev, width):
        base = lax.rem(shift - CC * dev - (width - 1) + (3 if width > CC else 0) + 2 * total, total)
        return base // CC, lax.rem(base, CC)

    def fold_exchange(src, buf1, stage2, buf2, width):
        sem1, sem2 = take(NH - 1), take(NZ - 1)

        def first():
            for j in range(1, NH):
                remote(src, buf1.at[hi], sem1 + j - 1, hi_peer(j)[1]).start()
            buf1[hi] = src[...]

        def held(dev):
            q = first_block(dev, width)[0]
            block = lax.rem(q + lax.rem(z + NH * NZ - q, NZ), NH * NZ)
            return block // NZ

        def second():
            for j in range(1, NH):
                h = lax.rem(hi + NH - j, NH)
                copy = remote(src, buf1.at[h], sem1 + j - 1, hi_peer(j)[1])
                copy.wait_send()
                copy.wait_recv()
            for j in range(1, NZ):
                t, to = z_peer(j)
                stage2[j - 1] = buf1[held(hi * NZ + t)]
                remote(stage2.at[j - 1], buf2.at[z], sem2 + j - 1, to).start()
            buf2[z] = buf1[held(lon)]

        def last():
            for j in range(1, NZ):
                t = lax.rem(z + NZ - j, NZ)
                copy = remote(stage2.at[j - 1], buf2.at[t], sem2 + j - 1, z_peer(j)[1])
                copy.wait_send()
                copy.wait_recv()
            q, off = first_block(lon, width)
            for m in range(3 if width > CC else 2):
                fcat[:, pl.ds(m * CC, CC), :] = buf2[lax.rem(q + m, NZ)].astype(F32)
            return off

        return first, second, last

    fold1, fold2, fold3 = fold_exchange(field.at[pl.ds(125, 3)], fr1, fs2, fr2, CC + 6)
    pl.when(north)(fold1)

    for copy in loads[1:]:
        copy.wait()

    tapf = taps_in[...].astype(F32)
    for t in range(49):
        wb[t] = jnp.broadcast_to(tapf[t : t + 1], (G, C)).astype(BF16)
    gain = gain_in[...].astype(F32)
    bias = bias_in[...].astype(F32).reshape(1, 512)
    scale = scale_in[...].astype(F32)

    lt[...] = jnp.concatenate([land[...].astype(F32), jnp.zeros((C - CC, C), F32)], axis=0).T

    @pl.loop(0, RR)
    def _(r):
        v = lt[pl.ds(r, G, stride=RR), :]
        for c in range(CC):
            landb[rows((r * CC + c) * G, G), :] = jnp.broadcast_to(v[:, c : c + 1], (G, C))

    for g in range(G):
        cb32[pl.ds(g, 4, stride=G), :] = cot[g].astype(F32)
    cotb[...] = cb32[...].astype(BF16)

    def gather_rows(r0, r1, c0, c1):
        @pl.loop(r0, r1)
        def _(r):
            for c in range(c0, c1):
                ext[rows((r * EC + c) * G, G), :] = fbuf[
                    pl.ds(r * PITCH + 5 + c, G, stride=RR * PITCH), :
                ].astype(BF16)

    gather_rows(3, 11, 3, 3 + CC)
    halo_wait(halo)
    for j in range(3):
        fbuf[pl.ds(3 * PITCH + 5 + j, 128, stride=PITCH), :] = cl[j].astype(F32)
        fbuf[pl.ds(3 * PITCH + 8 + CC + j, 128, stride=PITCH), :] = cr[j].astype(F32)

    @pl.when(south)
    def _():
        fbuf[pl.ds(0, 3 * PITCH), :] = jnp.zeros((3 * PITCH, C), F32)

    @pl.when(jnp.logical_not(south))
    def _():
        for k in range(3):
            fbuf[pl.ds(k * PITCH + 8, CC), :] = rs[k].astype(F32)
            for j in range(3):
                fbuf[pl.ds(k * PITCH + 5 + j, 1), :] = csl[j].astype(F32)[13 + k : 14 + k]
                fbuf[pl.ds(k * PITCH + 8 + CC + j, 1), :] = csr[j].astype(F32)[13 + k : 14 + k]

    @pl.when(jnp.logical_not(north))
    def _():
        for k in range(3):
            fbuf[pl.ds((131 + k) * PITCH + 8, CC), :] = rn[k].astype(F32)
            for j in range(3):
                fbuf[pl.ds((131 + k) * PITCH + 5 + j, 1), :] = cnl[j].astype(F32)[k : k + 1]
                fbuf[pl.ds((131 + k) * PITCH + 8 + CC + j, 1), :] = cnr[j].astype(F32)[k : k + 1]

    gather_rows(0, 3, 0, EC)
    gather_rows(3, 11, 0, 3)
    gather_rows(3, 11, 3 + CC, EC)
    pl.when(north)(fold2)

    def last_rows():
        @pl.when(north)
        def _():
            off = fold3()
            for k in range(3):
                for i in range(EC):
                    fbuf[pl.ds((131 + k) * PITCH + 5 + i, 1), :] = fcat[2 - k, pl.ds(off + EC - 1 - i, 1), :]

        gather_rows(11, 14, 0, EC)

    def conv(src, r, cb, flip):
        outs = []
        for c in range(8):
            total_ = None
            for group in ((0, 1), (2, 3), (4, 5, 6)):
                terms = []
                for a in group:
                    line = []
                    for b in range(7):
                        t = 48 - (7 * a + b) if flip else 7 * a + b
                        x = src[rows(((r + a) * EC + cb * 8 + c + b) * G, G), :].reshape(1, G, C)
                        line.append(x * wb[t][None])
                    terms.append(tree(line))
                term = tree(terms).astype(F32)
                total_ = term if total_ is None else total_ + term
            outs.append(total_)
        return jnp.concatenate(outs, axis=0)

    @pl.loop(0, RR)
    def _(r):
        pl.when(r == 5)(last_rows)

        @pl.loop(0, 4)
        def _(cb):
            hat[rows((r * CC + cb * 8) * G, 8 * G), :] = conv(ext, r, cb, False).reshape(8 * G, C)

    def forward1(k):
        at = rows(k * M, M)
        dh, ds = norm_parts(hat[at, :])
        hat[at, :] = dh
        rstd[at, :] = jnp.broadcast_to(ds, dh.shape)
        nm = (dh * gain).astype(BF16)
        normed[at, :] = nm
        active, slp = gelu_parts(dot(nm, up[...], 1, 0) + bias)
        act[at, :] = active
        slope[at, :] = slp
        return active

    def forward2(k, active):
        at = rows(k * M, M)
        mixed = dot(active, down[...], 1, 0)
        x = jnp.concatenate([ext[rows(((2 * k + 3 + i) * EC + 3) * G, M // 2), :].astype(F32) for i in range(2)], axis=0)
        lev0[at, :] = (landb[at, :] * (x + scale * mixed)).astype(BF16)

    @pl.loop(0, CHUNKS)
    def _(k):
        forward2(k, forward1(k))

    def section(s, count, cols, src, hats, rstds, patches, put):
        sg = sgain_in[s : s + 1].astype(F32)
        sb = sbias_in[s : s + 1].astype(F32)
        n = cols * G
        half = cols // 2

        def step(i):
            parts = []
            for a in range(2):
                at = rows((2 * i + a) * n, n)
                h, rs_ = norm_parts(src[at, :].astype(F32), True)
                hats[at, :] = h
                rstds[at, :] = jnp.broadcast_to(rs_, h.shape)
                sn = (h * sg).astype(BF16).reshape(half, 2, G, C)
                parts += [sn[:, b].reshape(half * G, C) for b in range(2)]
            p = jnp.concatenate(parts, axis=1)
            patches[rows(i * half * G, half * G), :] = p
            put(i, (dot(p, sw[s], 1, 0) + sb).astype(BF16))

        if count == 1:
            step(0)
        else:
            pl.loop(0, count)(step)

    def put1(i, v):
        lev1[rows(i * 256, 256), :] = v

    def put2(i, v):
        lev2[rows(i * 128, 128), :] = v

    def put3(i, v):
        v = v.astype(F32)
        for j in range(4):
            cb32[pl.ds(j, G, stride=4), :] = v[j * G : (j + 1) * G]
        for g in range(G):
            bott[g] = cb32[pl.ds(g * 4, 4), :].astype(BF16)

    section(0, 4, 32, lev0, hat1, rstd1, p1, put1)
    section(1, 2, 16, lev1, hat2, rstd2, p2, put2)
    section(2, 1, 8, lev2, hat3, rstd3, p3, put3)

    def section_back(s, count, cols, src, hats, rstds, patches, put):
        sg = sgain_in[s : s + 1].astype(F32)
        n = cols * G
        half = cols // 2
        secacc[s] = jnp.zeros((C, 4 * C), F32)

        def step(i):
            at = rows(i * half * G, half * G)
            u = src[at, :]
            secacc[s] += dot(u, patches[at, :], 0, 0)
            spread = dot(u, sw[s], 1, 1)
            for a in range(2):
                at2 = rows((2 * i + a) * n, n)
                hh = hats[at2, :].reshape(half, 2, G, C)
                rr = rstds[at2, :].reshape(half, 2, G, C)
                outs = []
                for b in range(2):
                    q = 2 * a + b
                    g = spread[:, q * C : (q + 1) * C] * sg
                    back = norm_back(g, hh[:, b].reshape(half * G, C), rr[:, b].reshape(half * G, C))
                    outs.append(back.astype(BF16).reshape(half, G, C))
                put(at2, jnp.stack(outs, axis=1).reshape(n, C))

        if count == 1:
            step(0)
        else:
            pl.loop(0, count)(step)

    def putb2(at, v):
        back2[at, :] = v

    def putb1(at, v):
        back1[at, :] = v

    def putb0(at, v):
        direct[at, :] = (landb[at, :] * v.astype(F32)).astype(BF16)

    section_back(2, 1, 8, cotb, hat3, rstd3, p3, putb2)
    section_back(1, 2, 16, back2, hat2, rstd2, p2, putb1)
    section_back(0, 4, 32, back1, hat1, rstd1, p1, putb0)

    bsec = dict(s1=sec_s1, rq=sec_rq, s3=sec_s3, r3=sec_r3, r4=sec_r4, g3=sec_g3, ga=sec_ga)
    bden = dict(s1=den_s1, rq=den_rq, s3=den_s3, r3=den_r3, r4=den_r4, g3=den_g3, ga=den_ga)
    def reduction(size, full, b):
        quarter, piece = size // 4, size // 32
        sem1, sem6 = take(3), take(3)
        sem3, sem4, sem5 = take(NH - 1), take(NZ - 1), take(NH - 1)

        def lat_peer(j):
            to = lax.rem(lat + j, 4)
            return to, (to, lon)

        def first():
            b["s1"][...] = full[...].astype(BF16)
            for j in range(1, 4):
                t, to = lat_peer(j)
                remote(b["s1"].at[rows(t * quarter, quarter)], b["rq"].at[lat], sem1 + j - 1, to).start()

        def third():
            total_ = full[rows(lat * quarter, quarter), :]
            for j in range(1, 4):
                frm = lax.rem(lat + 4 - j, 4)
                copy = remote(b["s1"].at[pl.ds(0, quarter)], b["rq"].at[frm], sem1 + j - 1, lat_peer(j)[1])
                copy.wait_send()
                copy.wait_recv()
                total_ = total_ + b["rq"][frm].astype(F32)
            b["s3"][...] = total_.astype(BF16)
            for j in range(1, NH):
                h, to = hi_peer(j)
                remote(b["s3"].at[rows(h * piece, piece)], b["r3"].at[hi], sem3 + j - 1, to).start()
            b["r3"][hi] = b["s3"][rows(hi * piece, piece), :]

        def total8(buf):
            part = buf[0].astype(F32)
            for i in range(1, 8):
                part = part + buf[i].astype(F32)
            return part.astype(BF16)

        def fourth():
            for j in range(1, NH):
                h = lax.rem(hi + NH - j, NH)
                copy = remote(b["s3"].at[pl.ds(0, piece)], b["r3"].at[h], sem3 + j - 1, hi_peer(j)[1])
                copy.wait_send()
                copy.wait_recv()
            b["r4"][z] = total8(b["r3"])
            for j in range(1, NZ):
                remote(b["r4"].at[z], b["r4"].at[z], sem4 + j - 1, z_peer(j)[1]).start()

        def fifth():
            for j in range(1, NZ):
                t = lax.rem(z + NZ - j, NZ)
                copy = remote(b["r4"].at[z], b["r4"].at[t], sem4 + j - 1, z_peer(j)[1])
                copy.wait_send()
                copy.wait_recv()
            b["g3"][hi] = total8(b["r4"])
            for j in range(1, NH):
                remote(b["g3"].at[hi], b["g3"].at[hi], sem5 + j - 1, hi_peer(j)[1]).start()

        def sixth():
            for j in range(1, NH):
                h = lax.rem(hi + NH - j, NH)
                copy = remote(b["g3"].at[hi], b["g3"].at[h], sem5 + j - 1, hi_peer(j)[1])
                copy.wait_send()
                copy.wait_recv()
            for j in range(1, 4):
                remote(b["g3"], b["ga"].at[lat], sem6 + j - 1, lat_peer(j)[1]).start()

        def last(out):
            def place(t, v):
                out[rows(t * quarter, quarter), :] = v.reshape(quarter, C).astype(F32) * factor

            place(lat, b["g3"][...])
            for j in range(1, 4):
                frm = lax.rem(lat + 4 - j, 4)
                copy = remote(b["g3"], b["ga"].at[frm], sem6 + j - 1, lat_peer(j)[1])
                copy.wait_send()
                copy.wait_recv()
                place(frm, b["ga"][frm])

        return first, third, fourth, fifth, sixth, last

    rs1, rs3, rs4, rs5, rs6, rs7 = reduction(1536, asec, bsec)
    rd1, rd3, rd4, rd5, rd6, rd7 = reduction(1024, aden, bden)

    for s in range(3):
        for q in range(4):
            asec[pl.ds((4 * s + q) * C, C), :] = secacc[s, :, q * C : (q + 1) * C].T
    rs1()

    upacc[...] = jnp.zeros_like(upacc)
    dtacc[...] = jnp.zeros_like(dtacc)

    def backward1(k):
        at = rows(k * M, M)
        mg = (direct[at, :].astype(F32) * scale).astype(BF16)
        dtacc[...] += dot(mg, act[at, :], 0, 0)
        return (dot(mg, down[...], 1, 1) * slope[at, :].astype(F32)).astype(BF16)

    def backward2(k, hg):
        at = rows(k * M, M)
        upacc[...] += dot(normed[at, :], hg, 0, 0)
        ng = dot(hg, up[...], 1, 1) * gain
        dg = norm_back_wide(ng, hat[at, :], rstd[at, :]).astype(BF16)
        for i in range(2):
            part = dg[i * M // 2 : (i + 1) * M // 2]
            dgb[2 * k + i] = part.reshape(POS // 2, G, C)
            ext2[rows(((2 * k + i + 3) * EC + 3) * G, M // 2), :] = part
            d32[rows(((2 * k + i) * EC + 3) * G, M // 2), :] = part.astype(F32)

    @pl.loop(0, CHUNKS)
    def _(k):
        backward2(k, backward1(k))
        pl.when(k == 2)(rs3)

    for i in range(3):
        rst[i] = d32[pl.ds(((5 + i) * EC + 3) * G + 15, CC, stride=G), :].astype(BF16)
        rsb[i] = d32[pl.ds((i * EC + 3) * G, CC, stride=G), :].astype(BF16)

    halo2 = halo_copies(
        [
            (0, -1, dgb.at[:, pl.ds(0, 3)], dcr),
            (0, 1, dgb.at[:, pl.ds(CC - 3, 3)], dcl),
            (1, 0, rst, drs),
            (-1, 0, rsb, drn),
            (1, 1, rst.at[:, pl.ds(16, 16)], dsl),
            (1, -1, rst.at[:, pl.ds(0, 16)], dsr),
            (-1, 1, rsb.at[:, pl.ds(16, 16)], dnl),
            (-1, -1, rsb.at[:, pl.ds(0, 16)], dnr),
        ]
    )
    halo_start(halo2)

    for q in range(4):
        aden[pl.ds(q * C, C), :] = upacc[:, q * C : (q + 1) * C]
        aden[pl.ds((4 + q) * C, C), :] = dtacc[:, q * C : (q + 1) * C].T
    rd1()

    tapacc[...] = jnp.zeros_like(tapacc)

    @pl.loop(0, RR)
    def _(r):
        @pl.loop(0, 4)
        def _(cb):
            d = ext2[rows(((r + 3) * EC + 3 + cb * 8) * G, 8 * G), :].reshape(8, G, C)
            for a in range(7):
                for b in range(7):
                    x = ext[rows(((r + a) * EC + cb * 8 + b) * G, 8 * G), :]
                    p = x.reshape(8, G, C) * d
                    t = tree([p[i] for i in range(8)]).astype(F32)
                    tapacc[7 * a + b] += t[:8] + t[8:]

        pl.when(r == 1)(rs4)
        pl.when(r == 4)(rd3)
        pl.when(r == 6)(rs5)

    def tap_stage(buf, peers, me):
        sem = take(len(peers))

        def start(value):
            buf[me] = value.astype(BF16)
            for i, (_, to) in enumerate(peers):
                remote(buf.at[me], buf.at[me], sem + i, to).start()

        def finish():
            for i, (frm, to) in enumerate(peers):
                copy = remote(buf.at[me], buf.at[frm], sem + i, to)
                copy.wait_send()
                copy.wait_recv()
            out = buf[0].astype(F32)
            for i in range(1, buf.shape[0]):
                out = out + buf[i].astype(F32)
            return out

        return start, finish

    lat_peers = [(lax.rem(lat + 4 - j, 4), (lax.rem(lat + j, 4), lon)) for j in range(1, 4)]
    hi_peers = [(lax.rem(hi + NH - j, NH), hi_peer(j)[1]) for j in range(1, NH)]
    z_peers = [(lax.rem(z + NZ - j, NZ), z_peer(j)[1]) for j in range(1, NZ)]
    tl_start, tl_finish = tap_stage(tl, lat_peers, lat)
    th_start, th_finish = tap_stage(th, hi_peers, hi)
    tz_start, tz_finish = tap_stage(tz, z_peers, z)
    tl_start(jnp.concatenate([jnp.sum(tapacc[...], axis=1), jnp.zeros((15, C), F32)], axis=0))

    halo_wait(halo2)

    @pl.when(south)
    def _():
        drs[...] = jnp.zeros_like(drs)
        dsl[...] = jnp.zeros_like(dsl)
        dsr[...] = jnp.zeros_like(dsr)

    @pl.when(north)
    def _():
        drn[...] = jnp.zeros_like(drn)
        dnl[...] = jnp.zeros_like(dnl)
        dnr[...] = jnp.zeros_like(dnr)

    @pl.loop(0, RR)
    def _(r):
        for j in range(3):
            ext2[rows(((r + 3) * EC + j) * G, G), :] = dcl[r, j]
            ext2[rows(((r + 3) * EC + 3 + CC + j) * G, G), :] = dcr[r, j]
            d32[rows((r * EC + j) * G, G), :] = dcl[r, j].astype(F32)
            d32[rows((r * EC + 3 + CC + j) * G, G), :] = dcr[r, j].astype(F32)

    fg1, fg2, fg3 = fold_exchange(fg, hr1, hs2, hr2, CC)

    @pl.when(north)
    def _():
        for i in range(3):
            for cut, at in ((0, 0), (8, 8), (16, 16), (24, 24), (30, 30)):
                zbuf[i, pl.ds(at, 8), :] = d32[pl.ds(((5 + i) * EC + cut) * G + 15, 8, stride=G), :]
        for k in range(1, 4):
            total_ = None
            for a in range(k + 3, 7):
                for b in range(7):
                    term = zbuf[k - a + 5, pl.ds(6 - b, CC), :] * tapf[7 * a + b : 7 * a + b + 1]
                    total_ = term if total_ is None else total_ + term
            fg[k - 1] = total_.astype(BF16)
        fg1()

    for k in range(6):
        low = k < 3
        r = k + 5 if low else k - 3
        edge, el, er = (drs, dsl, dsr) if low else (drn, dnl, dnr)
        i = k if low else k - 3
        line = 7 if low else 24
        for c in range(EC):
            sh[pl.ds(c * 32 + 8, G), :] = d32[pl.ds((r * EC + c) * G, G), :]
        sh[pl.ds(3 * 32 + line, CC, stride=32), :] = edge[i].astype(F32)
        lft, rgt = el[i].astype(F32), er[i].astype(F32)
        for j in range(3):
            sh[pl.ds(j * 32 + line, 1), :] = lft[13 + j : 14 + j]
            sh[pl.ds((CC + 3 + j) * 32 + line, 1), :] = rgt[j : j + 1]
        to = k if low else k + 8
        for c in range(EC):
            ext2[pl.ds((to * EC + c) * G, G), :] = sh[pl.ds(c * 32 + (7 if low else 9), G), :].astype(BF16)

    rd4()

    @pl.loop(0, RR)
    def _(r):
        @pl.loop(0, 4)
        def _(cb):
            v = conv(ext2, r, cb, True)
            v = v + direct[rows((r * CC + cb * 8) * G, 8 * G), :].astype(F32).reshape(8, G, C)
            for j in range(8):
                obuf[pl.ds(r * CC + cb * 8 + j, G, stride=RR * CC), :] = v[j]

        @pl.when(r == 1)
        def _():
            th_start(tl_finish())
            pl.when(north)(fg2)
            rs6()

        pl.when(r == 3)(rd5)

        @pl.when(r == 5)
        def _():
            tz_start(th_finish())
            rs7(gsec)

        pl.when(r == 6)(rd6)

    @pl.when(north)
    def _():
        off = fg3()
        for k in range(1, 4):
            for i in range(CC):
                at = pl.ds((128 - k) * CC + i, 1)
                obuf[at, :] += fcat[k - 1, pl.ds(off + CC - 1 - i, 1), :]

    @pl.loop(0, 128)
    def _(i):
        gfield[i] = obuf[rows(i * CC, CC), :].astype(BF16)

    rd7(aden)
    for q in range(4):
        gup[:, q * C : (q + 1) * C] = aden[pl.ds(q * C, C), :]
    gdown[...] = aden[pl.ds(4 * C, 4 * C), :]
    gtaps[...] = tz_finish()[:49] * factor


def on_device(field, land, mirror, depth_weight, norm_gain, up_weight, up_bias, down_proj, layer_scale, section_gain, section_weight, section_bias, cotangent):
    factor = 1.0 / math.sqrt(512 * 2048 / 64.0)
    vm = pl.BlockSpec(memory_space=pltpu.VMEM)
    n = RR * CC * G

    def f(*shape):
        return pltpu.VMEM(shape, F32)

    def h(*shape):
        return pltpu.VMEM(shape, BF16)

    sems = 128
    scratch = dict(
        field=h(128, CC, C),
        land=pltpu.VMEM((CC, 128), jnp.int32),
        taps_in=h(49, C),
        gain_in=h(1, C),
        up=h(C, 512),
        bias_in=h(512),
        down=h(512, C),
        scale_in=h(1, C),
        sgain_in=h(3, C),
        sw=h(3, 512, C),
        sbias_in=h(3, C),
        cot=h(G, 4, C),
        lsem=pltpu.SemaphoreType.DMA((12,)),
        fbuf=f(134 * PITCH, C),
        d32=f(RR * EC * G, C),
        obuf=f(n, C),
        sh=f(EC * 32, C),
        hat=f(n, C),
        rstd=f(n, C),
        landb=f(n, C),
        hat1=f(n, C),
        rstd1=f(n, C),
        hat2=f(n // 4, C),
        rstd2=f(n // 4, C),
        hat3=f(n // 16, C),
        rstd3=f(n // 16, C),
        dgb=h(RR, CC, G, C),
        upacc=f(C, 512),
        dtacc=f(C, 512),
        secacc=f(3, C, 512),
        tapacc=f(49, 8, C),
        lt=f(C, C),
        cb32=f(64, C),
        cotb=h(64, C),
        asec=f(1536, C),
        aden=f(1024, C),
        sec_s1=h(1536, C),
        sec_rq=h(4, 384, C),
        sec_s3=h(384, C),
        sec_r3=h(NH, 48, C),
        sec_r4=h(NZ, 48, C),
        sec_g3=h(NH, 48, C),
        sec_ga=h(4, NH, 48, C),
        den_s1=h(1024, C),
        den_rq=h(4, 256, C),
        den_s3=h(256, C),
        den_r3=h(NH, 32, C),
        den_r4=h(NZ, 32, C),
        den_g3=h(NH, 32, C),
        den_ga=h(4, NH, 32, C),
        tl=h(4, 64, C),
        th=h(NH, 64, C),
        tz=h(NZ, 64, C),
        stl=h(3, 128, C),
        str_=h(3, 128, C),
        cl=h(3, 128, C),
        cr=h(3, 128, C),
        rs=h(3, CC, C),
        rn=h(3, CC, C),
        csl=h(3, 16, C),
        csr=h(3, 16, C),
        cnl=h(3, 16, C),
        cnr=h(3, 16, C),
        dcl=h(RR, 3, G, C),
        dcr=h(RR, 3, G, C),
        rst=h(3, CC, C),
        rsb=h(3, CC, C),
        drs=h(3, CC, C),
        drn=h(3, CC, C),
        dsl=h(3, 16, C),
        dsr=h(3, 16, C),
        dnl=h(3, 16, C),
        dnr=h(3, 16, C),
        fr1=h(NH, 3, CC, C),
        fs2=h(NZ - 1, 3, CC, C),
        fr2=h(NZ, 3, CC, C),
        fcat=f(3, 3 * CC, C),
        zbuf=f(3, 40, C),
        fg=h(3, CC, C),
        hr1=h(NH, 3, CC, C),
        hs2=h(NZ - 1, 3, CC, C),
        hr2=h(NZ, 3, CC, C),
        ssem=pltpu.SemaphoreType.DMA((sems,)),
        rsem=pltpu.SemaphoreType.DMA((sems,)),
    )
    scoped = dict(
        ext=h(ER * EC * G, C),
        ext2=h(ER * EC * G, C),
        wb=h(49, G, C),
        normed=h(n, C),
        act=h(n, 512),
        slope=h(n, 512),
        lev0=h(n, C),
        lev1=h(n // 4, C),
        lev2=h(n // 16, C),
        p1=h(n // 4, 512),
        p2=h(n // 16, 512),
        p3=h(n // 64, 512),
        back1=h(n // 4, C),
        back2=h(n // 16, C),
        direct=h(n, C),
    )

    def whole(*refs):
        pl.run_scoped(functools.partial(kernel, factor, *refs), **scoped)

    bott, gfield, gtaps, gup, gdown, gsec = pl.pallas_call(
        whole,
        out_shape=(
            jax.ShapeDtypeStruct((G, 4, C), BF16),
            jax.ShapeDtypeStruct((128, CC, C), BF16),
            jax.ShapeDtypeStruct((49, C), F32),
            jax.ShapeDtypeStruct((C, 512), F32),
            jax.ShapeDtypeStruct((512, C), F32),
            jax.ShapeDtypeStruct((1536, C), F32),
        ),
        in_specs=[pl.BlockSpec(memory_space=pltpu.SMEM)] + [pl.BlockSpec(memory_space=pltpu.HBM)] * 12,
        out_specs=(vm,) * 6,
        scratch_shapes=list(scratch.values()),
        compiler_params=pltpu.CompilerParams(
            collective_id=0, has_side_effects=True, vmem_limit_bytes=50 * 1024 * 1024
        ),
    )(
        mirror,
        *(
            pltpu.with_memory_space_constraint(v, pltpu.HBM)
            for v in (
                field,
                land.T,
                depth_weight,
                norm_gain.reshape(1, C),
                up_weight,
                up_bias,
                down_proj,
                layer_scale.reshape(1, C),
                section_gain,
                section_weight,
                section_bias,
                cotangent,
            )
        ),
    )
    results = (bott, gfield, gtaps, gup, gdown, gsec)
    anywhere = pl.BlockSpec(memory_space=pl.ANY)

    def write(*refs):
        copies = [pltpu.make_async_copy(refs[i], refs[6 + i], refs[12].at[i]) for i in range(6)]
        for copy in copies:
            copy.start()
        for copy in copies:
            copy.wait()

    bott, gfield, gtaps, gup, gdown, gsec = pl.pallas_call(
        write,
        out_shape=tuple(jax.ShapeDtypeStruct(x.shape, x.dtype) for x in results),
        in_specs=[vm] * 6,
        out_specs=(anywhere,) * 6,
        scratch_shapes=[pltpu.SemaphoreType.DMA((6,))],
        compiler_params=pltpu.CompilerParams(vmem_limit_bytes=16 * 1024 * 1024),
    )(*results)
    return bott, gfield, gtaps, gup, gdown, gsec.reshape(3, 512, C)


def solution(mesh):
    cell = P("lat", "lon", None)
    in_specs = (cell, P("lat", "lon")) + (P(),) * 10 + (cell,)
    out_specs = (cell, cell, P(), P(), P(), P())
    return jax.shard_map(
        on_device, mesh=mesh, in_specs=in_specs, out_specs=out_specs, check_vma=False
    )
```

```python
import functools
import math

import jax
import jax.numpy as jnp
from jax import lax
from jax.experimental import pallas as pl
from jax.experimental.pallas import tpu as pltpu
from jax.sharding import PartitionSpec as P

MESH = pl.DeviceIdType.MESH
F32 = jnp.float32
BF16 = jnp.bfloat16
epsilon = 1e-06

G = 16
RR = 8
CC = 32
C = 128
PITCH = 48
EC = CC + 6
ER = RR + 6
NZ = 8
NH = 8
M = 1024
CHUNKS = RR * CC * G // M
POS = M // G


def mean_mx(values):
    ones = jnp.full((C, C), 1.0 / C, BF16)
    return dot(values.astype(BF16), ones, 1, 0)


def norm_parts(values, exact=False):
    mean = mean_mx(values) if exact else jnp.mean(values, axis=-1, keepdims=True)
    center = values - mean
    rstd = lax.rsqrt(jnp.mean(center * center, axis=-1, keepdims=True) + epsilon)
    return center * rstd, rstd


def norm_back(grad_hat, normed_hat, rstd):
    second = jnp.mean(grad_hat * normed_hat, axis=-1, keepdims=True)
    return rstd * (grad_hat - mean_mx(grad_hat) - normed_hat * second)


def norm_back_wide(grad_hat, normed_hat, rstd):
    pair = jnp.concatenate([grad_hat.astype(BF16), (grad_hat * normed_hat).astype(BF16)], axis=1)
    ones, zeros = jnp.full((C, C), 1.0 / C, BF16), jnp.zeros((C, C), BF16)
    both = jnp.concatenate(
        [jnp.concatenate([ones, zeros], axis=1), jnp.concatenate([zeros, ones], axis=1)], axis=0
    )
    means = dot(pair, both, 1, 0)
    return rstd * (grad_hat - means[:, :C] - normed_hat * means[:, C:])


def gelu_parts(h):
    h = h.astype(BF16)
    e = jnp.exp2(h * h * jnp.asarray(-0.7213475204444817, BF16))
    cdf = jnp.asarray(0.5, BF16) + jnp.asarray(0.5, BF16) * lax.erf(h * jnp.asarray(0.7071067811865476, BF16))
    return h * cdf, cdf + h * (e * jnp.asarray(0.3989422804014327, BF16))


def tree(terms):
    while len(terms) > 1:
        terms = [a + b for a, b in zip(terms[::2], terms[1::2])] + terms[len(terms) & ~1 :]
    return terms[0]


def dot(a, b, ca, cb):
    return lax.dot_general(a, b, (((ca,), (cb,)), ((), ())), preferred_element_type=F32)


def rows(start, size, align=16):
    return pl.ds(pl.multiple_of(start, align), size)


def kernel(
    factor,
    mirror,
    x_field,
    x_land,
    x_taps_in,
    x_gain_in,
    x_up,
    x_bias_in,
    x_down,
    x_scale_in,
    x_sgain_in,
    x_sw,
    x_sbias_in,
    x_cot,
    bott,
    gfield,
    gtaps,
    gup,
    gdown,
    gsec,
    field,
    land,
    taps_in,
    gain_in,
    up,
    bias_in,
    down,
    scale_in,
    sgain_in,
    sw,
    sbias_in,
    cot,
    lsem,
    fbuf,
    d32,
    obuf,
    sh,
    hat,
    rstd,
    landb,
    hat1,
    rstd1,
    hat2,
    rstd2,
    hat3,
    rstd3,
    dgb,
    upacc,
    dtacc,
    secacc,
    tapacc,
    lt,
    cb32,
    cotb,
    asec,
    aden,
    sec_s1,
    sec_rq,
    sec_s3,
    sec_r3,
    sec_r4,
    sec_g3,
    sec_ga,
    den_s1,
    den_rq,
    den_s3,
    den_r3,
    den_r4,
    den_g3,
    den_ga,
    tl,
    th,
    tz,
    stl,
    str_,
    cl,
    cr,
    rs,
    rn,
    csl,
    csr,
    cnl,
    cnr,
    dcl,
    dcr,
    rst,
    rsb,
    drs,
    drn,
    dsl,
    dsr,
    dnl,
    dnr,
    fr1,
    fs2,
    fr2,
    fcat,
    zbuf,
    fg,
    hr1,
    hs2,
    hr2,
    ssem,
    rsem,
    ext,
    ext2,
    wb,
    normed,
    act,
    slope,
    lev0,
    lev1,
    lev2,
    p1,
    p2,
    p3,
    back1,
    back2,
    direct,
):
    loads = [
        pltpu.make_async_copy(a, b, lsem.at[i])
        for i, (a, b) in enumerate(
            (
                (x_field, field),
                (x_land, land),
                (x_taps_in, taps_in),
                (x_gain_in, gain_in),
                (x_up, up),
                (x_bias_in, bias_in),
                (x_down, down),
                (x_scale_in, scale_in),
                (x_sgain_in, sgain_in),
                (x_sw, sw),
                (x_sbias_in, sbias_in),
                (x_cot, cot),
            )
        )
    ]
    for copy in loads:
        copy.start()

    lat = lax.axis_index("lat")
    lon = lax.axis_index("lon")
    hi, z = lon // NZ, lax.rem(lon, NZ)
    core, xl = lax.rem(lat, 2), lat // 2
    right, left = lax.rem(lon + 1, NH * NZ), lax.rem(lon + NH * NZ - 1, NH * NZ)
    north, south = lat == 3, lat == 0

    counter = [0]

    def take(n):
        counter[0] += n
        return counter[0] - n

    def remote(src, dst, sem, to):
        return pltpu.make_async_remote_copy(
            src_ref=src,
            dst_ref=dst,
            send_sem=ssem.at[sem],
            recv_sem=rsem.at[sem],
            device_id=to,
            device_id_type=MESH,
        )

    def hi_peer(j):
        h = lax.rem(hi + j, NH)
        return h, (lat, h * NZ + z)

    def z_peer(j):
        t = lax.rem(z + j, NZ)
        return t, (lat, hi * NZ + t)

    barrier = pltpu.get_barrier_semaphore()

    def greet(to):
        pl.semaphore_signal(barrier, inc=1, device_id=to, device_id_type=MESH)

    greet((lat, left))
    greet((lat, right))
    for dl in (-1, 1):

        @pl.when((lat + dl >= 0) & (lat + dl < 4))
        def _():
            greet((lat + dl, left))
            greet((lat + dl, right))

    for j in range(1, 4):
        greet((lax.rem(lat + j, 4), lon))
    for j in range(1, NH):
        greet(hi_peer(j)[1])
    for j in range(1, NZ):
        greet(z_peer(j)[1])

    loads[0].wait()

    @pl.loop(0, 128)
    def _(i):
        fbuf[rows((i + 3) * PITCH + 8, CC, 8), :] = field[i].astype(F32)

    for j in range(3):
        stl[j] = fbuf[pl.ds(3 * PITCH + 8 + j, 128, stride=PITCH), :].astype(BF16)
        str_[j] = fbuf[pl.ds(3 * PITCH + 8 + CC - 3 + j, 128, stride=PITCH), :].astype(BF16)

    waits = 2 + 3 + (NH - 1) + (NZ - 1)
    pl.semaphore_wait(barrier, waits + jnp.where(south | north, 2, 4))

    def halo_copies(pieces):
        made = []
        for dl, dn, src, dst in pieces:
            sem = take(1)
            to_lon = right if dn == 1 else left if dn == -1 else lon
            copy = remote(src, dst, sem, (lat + dl, to_lon))
            made.append((dl, copy))
        return made

    def when_lat(dl, ok, fn):
        if dl == 0:
            fn()
        else:
            pl.when(ok)(fn)

    def halo_start(made):
        for dl, copy in made:
            when_lat(dl, (lat + dl >= 0) & (lat + dl < 4), copy.start)

    def halo_wait(made):
        for dl, copy in made:
            when_lat(dl, (lat + dl >= 0) & (lat + dl < 4), copy.wait_send)
            when_lat(dl, (lat - dl >= 0) & (lat - dl < 4), copy.wait_recv)

    halo = halo_copies(
        [
            (0, -1, stl, cr),
            (0, 1, str_, cl),
            (1, 0, field.at[pl.ds(125, 3)], rs),
            (-1, 0, field.at[pl.ds(0, 3)], rn),
            (1, 1, str_.at[:, pl.ds(112, 16)], csl),
            (1, -1, stl.at[:, pl.ds(112, 16)], csr),
            (-1, 1, str_.at[:, pl.ds(0, 16)], cnl),
            (-1, -1, stl.at[:, pl.ds(0, 16)], cnr),
        ]
    )
    halo_start(halo)

    shift = mirror[0]
    total = NH * NZ * CC

    def first_block(dev, width):
        base = lax.rem(shift - CC * dev - (width - 1) + (3 if width > CC else 0) + 2 * total, total)
        return base // CC, lax.rem(base, CC)

    def fold_exchange(src, buf1, stage2, buf2, width):
        sem1, sem2 = take(NH - 1), take(NZ - 1)

        def first():
            for j in range(1, NH):
                remote(src, buf1.at[hi], sem1 + j - 1, hi_peer(j)[1]).start()
            buf1[hi] = src[...]

        def held(dev):
            q = first_block(dev, width)[0]
            block = lax.rem(q + lax.rem(z + NH * NZ - q, NZ), NH * NZ)
            return block // NZ

        def second():
            for j in range(1, NH):
                h = lax.rem(hi + NH - j, NH)
                copy = remote(src, buf1.at[h], sem1 + j - 1, hi_peer(j)[1])
                copy.wait_send()
                copy.wait_recv()
            for j in range(1, NZ):
                t, to = z_peer(j)
                stage2[j - 1] = buf1[held(hi * NZ + t)]
                remote(stage2.at[j - 1], buf2.at[z], sem2 + j - 1, to).start()
            buf2[z] = buf1[held(lon)]

        def last():
            for j in range(1, NZ):
                t = lax.rem(z + NZ - j, NZ)
                copy = remote(stage2.at[j - 1], buf2.at[t], sem2 + j - 1, z_peer(j)[1])
                copy.wait_send()
                copy.wait_recv()
            q, off = first_block(lon, width)
            for m in range(3 if width > CC else 2):
                fcat[:, pl.ds(m * CC, CC), :] = buf2[lax.rem(q + m, NZ)].astype(F32)
            return off

        return first, second, last

    fold1, fold2, fold3 = fold_exchange(field.at[pl.ds(125, 3)], fr1, fs2, fr2, CC + 6)
    pl.when(north)(fold1)

    for copy in loads[1:]:
        copy.wait()

    tapf = taps_in[...].astype(F32)
    for t in range(49):
        wb[t] = jnp.broadcast_to(tapf[t : t + 1], (G, C)).astype(BF16)
    gain = gain_in[...].astype(F32)
    bias = bias_in[...].astype(F32).reshape(1, 512)
    scale = scale_in[...].astype(F32)

    lt[...] = jnp.concatenate([land[...].astype(F32), jnp.zeros((C - CC, C), F32)], axis=0).T

    @pl.loop(0, RR)
    def _(r):
        v = lt[pl.ds(r, G, stride=RR), :]
        for c in range(CC):
            landb[rows((r * CC + c) * G, G), :] = jnp.broadcast_to(v[:, c : c + 1], (G, C))

    for g in range(G):
        cb32[pl.ds(g, 4, stride=G), :] = cot[g].astype(F32)
    cotb[...] = cb32[...].astype(BF16)

    def gather_rows(r0, r1, c0, c1):
        @pl.loop(r0, r1)
        def _(r):
            for c in range(c0, c1):
                ext[rows((r * EC + c) * G, G), :] = fbuf[
                    pl.ds(r * PITCH + 5 + c, G, stride=RR * PITCH), :
                ].astype(BF16)

    gather_rows(3, 11, 3, 3 + CC)
    halo_wait(halo)
    for j in range(3):
        fbuf[pl.ds(3 * PITCH + 5 + j, 128, stride=PITCH), :] = cl[j].astype(F32)
        fbuf[pl.ds(3 * PITCH + 8 + CC + j, 128, stride=PITCH), :] = cr[j].astype(F32)

    @pl.when(south)
    def _():
        fbuf[pl.ds(0, 3 * PITCH), :] = jnp.zeros((3 * PITCH, C), F32)

    @pl.when(jnp.logical_not(south))
    def _():
        for k in range(3):
            fbuf[pl.ds(k * PITCH + 8, CC), :] = rs[k].astype(F32)
            for j in range(3):
                fbuf[pl.ds(k * PITCH + 5 + j, 1), :] = csl[j].astype(F32)[13 + k : 14 + k]
                fbuf[pl.ds(k * PITCH + 8 + CC + j, 1), :] = csr[j].astype(F32)[13 + k : 14 + k]

    @pl.when(jnp.logical_not(north))
    def _():
        for k in range(3):
            fbuf[pl.ds((131 + k) * PITCH + 8, CC), :] = rn[k].astype(F32)
            for j in range(3):
                fbuf[pl.ds((131 + k) * PITCH + 5 + j, 1), :] = cnl[j].astype(F32)[k : k + 1]
                fbuf[pl.ds((131 + k) * PITCH + 8 + CC + j, 1), :] = cnr[j].astype(F32)[k : k + 1]

    gather_rows(0, 3, 0, EC)
    gather_rows(3, 11, 0, 3)
    gather_rows(3, 11, 3 + CC, EC)
    pl.when(north)(fold2)

    def last_rows():
        @pl.when(north)
        def _():
            off = fold3()
            for k in range(3):
                for i in range(EC):
                    fbuf[pl.ds((131 + k) * PITCH + 5 + i, 1), :] = fcat[2 - k, pl.ds(off + EC - 1 - i, 1), :]

        gather_rows(11, 14, 0, EC)

    def conv(src, r, cb, flip):
        outs = []
        for c in range(8):
            total_ = None
            for group in ((0, 1), (2, 3), (4, 5, 6)):
                terms = []
                for a in group:
                    line = []
                    for b in range(7):
                        t = 48 - (7 * a + b) if flip else 7 * a + b
                        x = src[rows(((r + a) * EC + cb * 8 + c + b) * G, G), :].reshape(1, G, C)
                        line.append(x * wb[t][None])
                    terms.append(tree(line))
                term = tree(terms).astype(F32)
                total_ = term if total_ is None else total_ + term
            outs.append(total_)
        return jnp.concatenate(outs, axis=0)

    @pl.loop(0, RR)
    def _(r):
        pl.when(r == 5)(last_rows)

        @pl.loop(0, 4)
        def _(cb):
            hat[rows((r * CC + cb * 8) * G, 8 * G), :] = conv(ext, r, cb, False).reshape(8 * G, C)

    def forward1(k):
        at = rows(k * M, M)
        dh, ds = norm_parts(hat[at, :])
        hat[at, :] = dh
        rstd[at, :] = jnp.broadcast_to(ds, dh.shape)
        nm = (dh * gain).astype(BF16)
        normed[at, :] = nm
        active, slp = gelu_parts(dot(nm, up[...], 1, 0) + bias)
        act[at, :] = active
        slope[at, :] = slp
        return active

    def forward2(k, active):
        at = rows(k * M, M)
        mixed = dot(active, down[...], 1, 0)
        x = jnp.concatenate([ext[rows(((2 * k + 3 + i) * EC + 3) * G, M // 2), :].astype(F32) for i in range(2)], axis=0)
        lev0[at, :] = (landb[at, :] * (x + scale * mixed)).astype(BF16)

    @pl.loop(0, CHUNKS)
    def _(k):
        forward2(k, forward1(k))

    def section(s, count, cols, src, hats, rstds, patches, put):
        sg = sgain_in[s : s + 1].astype(F32)
        sb = sbias_in[s : s + 1].astype(F32)
        n = cols * G
        half = cols // 2

        def step(i):
            parts = []
            for a in range(2):
                at = rows((2 * i + a) * n, n)
                h, rs_ = norm_parts(src[at, :].astype(F32), True)
                hats[at, :] = h
                rstds[at, :] = jnp.broadcast_to(rs_, h.shape)
                sn = (h * sg).astype(BF16).reshape(half, 2, G, C)
                parts += [sn[:, b].reshape(half * G, C) for b in range(2)]
            p = jnp.concatenate(parts, axis=1)
            patches[rows(i * half * G, half * G), :] = p
            put(i, (dot(p, sw[s], 1, 0) + sb).astype(BF16))

        if count == 1:
            step(0)
        else:
            pl.loop(0, count)(step)

    def put1(i, v):
        lev1[rows(i * 256, 256), :] = v

    def put2(i, v):
        lev2[rows(i * 128, 128), :] = v

    def put3(i, v):
        v = v.astype(F32)
        for j in range(4):
            cb32[pl.ds(j, G, stride=4), :] = v[j * G : (j + 1) * G]
        for g in range(G):
            bott[g] = cb32[pl.ds(g * 4, 4), :].astype(BF16)

    section(0, 4, 32, lev0, hat1, rstd1, p1, put1)
    section(1, 2, 16, lev1, hat2, rstd2, p2, put2)
    section(2, 1, 8, lev2, hat3, rstd3, p3, put3)

    def section_back(s, count, cols, src, hats, rstds, patches, put):
        sg = sgain_in[s : s + 1].astype(F32)
        n = cols * G
        half = cols // 2
        secacc[s] = jnp.zeros((C, 4 * C), F32)

        def step(i):
            at = rows(i * half * G, half * G)
            u = src[at, :]
            secacc[s] += dot(u, patches[at, :], 0, 0)
            spread = dot(u, sw[s], 1, 1)
            for a in range(2):
                at2 = rows((2 * i + a) * n, n)
                hh = hats[at2, :].reshape(half, 2, G, C)
                rr = rstds[at2, :].reshape(half, 2, G, C)
                outs = []
                for b in range(2):
                    q = 2 * a + b
                    g = spread[:, q * C : (q + 1) * C] * sg
                    back = norm_back(g, hh[:, b].reshape(half * G, C), rr[:, b].reshape(half * G, C))
                    outs.append(back.astype(BF16).reshape(half, G, C))
                put(at2, jnp.stack(outs, axis=1).reshape(n, C))

        if count == 1:
            step(0)
        else:
            pl.loop(0, count)(step)

    def putb2(at, v):
        back2[at, :] = v

    def putb1(at, v):
        back1[at, :] = v

    def putb0(at, v):
        direct[at, :] = (landb[at, :] * v.astype(F32)).astype(BF16)

    section_back(2, 1, 8, cotb, hat3, rstd3, p3, putb2)
    section_back(1, 2, 16, back2, hat2, rstd2, p2, putb1)
    section_back(0, 4, 32, back1, hat1, rstd1, p1, putb0)

    bsec = dict(s1=sec_s1, rq=sec_rq, s3=sec_s3, r3=sec_r3, r4=sec_r4, g3=sec_g3, ga=sec_ga)
    bden = dict(s1=den_s1, rq=den_rq, s3=den_s3, r3=den_r3, r4=den_r4, g3=den_g3, ga=den_ga)
    def reduction(size, full, b):
        quarter, piece = size // 4, size // 32
        sem1, sem6 = take(3), take(3)
        sem3, sem4, sem5 = take(NH - 1), take(NZ - 1), take(NH - 1)

        def lat_peer(j):
            to = lax.rem(lat + j, 4)
            return to, (to, lon)

        def first():
            b["s1"][...] = full[...].astype(BF16)
            for j in range(1, 4):
                t, to = lat_peer(j)
                remote(b["s1"].at[rows(t * quarter, quarter)], b["rq"].at[lat], sem1 + j - 1, to).start()

        def third():
            total_ = full[rows(lat * quarter, quarter), :]
            for j in range(1, 4):
                frm = lax.rem(lat + 4 - j, 4)
                copy = remote(b["s1"].at[pl.ds(0, quarter)], b["rq"].at[frm], sem1 + j - 1, lat_peer(j)[1])
                copy.wait_send()
                copy.wait_recv()
                total_ = total_ + b["rq"][frm].astype(F32)
            b["s3"][...] = total_.astype(BF16)
            for j in range(1, NH):
                h, to = hi_peer(j)
                remote(b["s3"].at[rows(h * piece, piece)], b["r3"].at[hi], sem3 + j - 1, to).start()
            b["r3"][hi] = b["s3"][rows(hi * piece, piece), :]

        def total8(buf):
            part = buf[0].astype(F32)
            for i in range(1, 8):
                part = part + buf[i].astype(F32)
            return part.astype(BF16)

        def fourth():
            for j in range(1, NH):
                h = lax.rem(hi + NH - j, NH)
                copy = remote(b["s3"].at[pl.ds(0, piece)], b["r3"].at[h], sem3 + j - 1, hi_peer(j)[1])
                copy.wait_send()
                copy.wait_recv()
            b["r4"][z] = total8(b["r3"])
            for j in range(1, NZ):
                remote(b["r4"].at[z], b["r4"].at[z], sem4 + j - 1, z_peer(j)[1]).start()

        def fifth():
            for j in range(1, NZ):
                t = lax.rem(z + NZ - j, NZ)
                copy = remote(b["r4"].at[z], b["r4"].at[t], sem4 + j - 1, z_peer(j)[1])
                copy.wait_send()
                copy.wait_recv()
            b["g3"][hi] = total8(b["r4"])
            for j in range(1, NH):
                remote(b["g3"].at[hi], b["g3"].at[hi], sem5 + j - 1, hi_peer(j)[1]).start()

        def sixth():
            for j in range(1, NH):
                h = lax.rem(hi + NH - j, NH)
                copy = remote(b["g3"].at[hi], b["g3"].at[h], sem5 + j - 1, hi_peer(j)[1])
                copy.wait_send()
                copy.wait_recv()
            for j in range(1, 4):
                remote(b["g3"], b["ga"].at[lat], sem6 + j - 1, lat_peer(j)[1]).start()

        def last(out):
            def place(t, v):
                out[rows(t * quarter, quarter), :] = v.reshape(quarter, C).astype(F32) * factor

            place(lat, b["g3"][...])
            for j in range(1, 4):
                frm = lax.rem(lat + 4 - j, 4)
                copy = remote(b["g3"], b["ga"].at[frm], sem6 + j - 1, lat_peer(j)[1])
                copy.wait_send()
                copy.wait_recv()
                place(frm, b["ga"][frm])

        return first, third, fourth, fifth, sixth, last

    rs1, rs3, rs4, rs5, rs6, rs7 = reduction(1536, asec, bsec)
    rd1, rd3, rd4, rd5, rd6, rd7 = reduction(1024, aden, bden)

    for s in range(3):
        for q in range(4):
            asec[pl.ds((4 * s + q) * C, C), :] = secacc[s, :, q * C : (q + 1) * C].T
    rs1()

    upacc[...] = jnp.zeros_like(upacc)
    dtacc[...] = jnp.zeros_like(dtacc)

    def backward1(k):
        at = rows(k * M, M)
        mg = (direct[at, :].astype(F32) * scale).astype(BF16)
        dtacc[...] += dot(mg, act[at, :], 0, 0)
        return (dot(mg, down[...], 1, 1) * slope[at, :].astype(F32)).astype(BF16)

    def backward2(k, hg):
        at = rows(k * M, M)
        upacc[...] += dot(normed[at, :], hg, 0, 0)
        ng = dot(hg, up[...], 1, 1) * gain
        dg = norm_back_wide(ng, hat[at, :], rstd[at, :]).astype(BF16)
        for i in range(2):
            part = dg[i * M // 2 : (i + 1) * M // 2]
            dgb[2 * k + i] = part.reshape(POS // 2, G, C)
            ext2[rows(((2 * k + i + 3) * EC + 3) * G, M // 2), :] = part
            d32[rows(((2 * k + i) * EC + 3) * G, M // 2), :] = part.astype(F32)

    @pl.loop(0, CHUNKS)
    def _(k):
        backward2(k, backward1(k))
        pl.when(k == 2)(rs3)

    for i in range(3):
        rst[i] = d32[pl.ds(((5 + i) * EC + 3) * G + 15, CC, stride=G), :].astype(BF16)
        rsb[i] = d32[pl.ds((i * EC + 3) * G, CC, stride=G), :].astype(BF16)

    halo2 = halo_copies(
        [
            (0, -1, dgb.at[:, pl.ds(0, 3)], dcr),
            (0, 1, dgb.at[:, pl.ds(CC - 3, 3)], dcl),
            (1, 0, rst, drs),
            (-1, 0, rsb, drn),
            (1, 1, rst.at[:, pl.ds(16, 16)], dsl),
            (1, -1, rst.at[:, pl.ds(0, 16)], dsr),
            (-1, 1, rsb.at[:, pl.ds(16, 16)], dnl),
            (-1, -1, rsb.at[:, pl.ds(0, 16)], dnr),
        ]
    )
    halo_start(halo2)

    for q in range(4):
        aden[pl.ds(q * C, C), :] = upacc[:, q * C : (q + 1) * C]
        aden[pl.ds((4 + q) * C, C), :] = dtacc[:, q * C : (q + 1) * C].T
    rd1()

    tapacc[...] = jnp.zeros_like(tapacc)

    @pl.loop(0, RR)
    def _(r):
        @pl.loop(0, 4)
        def _(cb):
            d = ext2[rows(((r + 3) * EC + 3 + cb * 8) * G, 8 * G), :].reshape(8, G, C)
            for a in range(7):
                for b in range(7):
                    x = ext[rows(((r + a) * EC + cb * 8 + b) * G, 8 * G), :]
                    p = x.reshape(8, G, C) * d
                    t = tree([p[i] for i in range(8)]).astype(F32)
                    tapacc[7 * a + b] += t[:8] + t[8:]

        pl.when(r == 1)(rs4)
        pl.when(r == 3)(rd3)
        pl.when(r == 6)(rs5)

    rd4()

    def tap_stage(buf, peers, me):
        sem = take(len(peers))

        def start(value):
            buf[me] = value.astype(BF16)
            for i, (_, to) in enumerate(peers):
                remote(buf.at[me], buf.at[me], sem + i, to).start()

        def finish():
            for i, (frm, to) in enumerate(peers):
                copy = remote(buf.at[me], buf.at[frm], sem + i, to)
                copy.wait_send()
                copy.wait_recv()
            out = buf[0].astype(F32)
            for i in range(1, buf.shape[0]):
                out = out + buf[i].astype(F32)
            return out

        return start, finish

    lat_peers = [(lax.rem(lat + 4 - j, 4), (lax.rem(lat + j, 4), lon)) for j in range(1, 4)]
    hi_peers = [(lax.rem(hi + NH - j, NH), hi_peer(j)[1]) for j in range(1, NH)]
    z_peers = [(lax.rem(z + NZ - j, NZ), z_peer(j)[1]) for j in range(1, NZ)]
    tl_start, tl_finish = tap_stage(tl, lat_peers, lat)
    th_start, th_finish = tap_stage(th, hi_peers, hi)
    tz_start, tz_finish = tap_stage(tz, z_peers, z)
    tl_start(jnp.concatenate([jnp.sum(tapacc[...], axis=1), jnp.zeros((15, C), F32)], axis=0))

    halo_wait(halo2)

    @pl.when(south)
    def _():
        drs[...] = jnp.zeros_like(drs)
        dsl[...] = jnp.zeros_like(dsl)
        dsr[...] = jnp.zeros_like(dsr)

    @pl.when(north)
    def _():
        drn[...] = jnp.zeros_like(drn)
        dnl[...] = jnp.zeros_like(dnl)
        dnr[...] = jnp.zeros_like(dnr)

    @pl.loop(0, RR)
    def _(r):
        for j in range(3):
            ext2[rows(((r + 3) * EC + j) * G, G), :] = dcl[r, j]
            ext2[rows(((r + 3) * EC + 3 + CC + j) * G, G), :] = dcr[r, j]
            d32[rows((r * EC + j) * G, G), :] = dcl[r, j].astype(F32)
            d32[rows((r * EC + 3 + CC + j) * G, G), :] = dcr[r, j].astype(F32)

    fg1, fg2, fg3 = fold_exchange(fg, hr1, hs2, hr2, CC)

    @pl.when(north)
    def _():
        for i in range(3):
            for cut, at in ((0, 0), (8, 8), (16, 16), (24, 24), (30, 30)):
                zbuf[i, pl.ds(at, 8), :] = d32[pl.ds(((5 + i) * EC + cut) * G + 15, 8, stride=G), :]
        for k in range(1, 4):
            total_ = None
            for a in range(k + 3, 7):
                for b in range(7):
                    term = zbuf[k - a + 5, pl.ds(6 - b, CC), :] * tapf[7 * a + b : 7 * a + b + 1]
                    total_ = term if total_ is None else total_ + term
            fg[k - 1] = total_.astype(BF16)
        fg1()

    for k in range(6):
        low = k < 3
        r = k + 5 if low else k - 3
        edge, el, er = (drs, dsl, dsr) if low else (drn, dnl, dnr)
        i = k if low else k - 3
        line = 7 if low else 24
        for c in range(EC):
            sh[pl.ds(c * 32 + 8, G), :] = d32[pl.ds((r * EC + c) * G, G), :]
        sh[pl.ds(3 * 32 + line, CC, stride=32), :] = edge[i].astype(F32)
        lft, rgt = el[i].astype(F32), er[i].astype(F32)
        for j in range(3):
            sh[pl.ds(j * 32 + line, 1), :] = lft[13 + j : 14 + j]
            sh[pl.ds((CC + 3 + j) * 32 + line, 1), :] = rgt[j : j + 1]
        to = k if low else k + 8
        for c in range(EC):
            ext2[pl.ds((to * EC + c) * G, G), :] = sh[pl.ds(c * 32 + (7 if low else 9), G), :].astype(BF16)

    @pl.loop(0, RR)
    def _(r):
        @pl.loop(0, 4)
        def _(cb):
            v = conv(ext2, r, cb, True)
            v = v + direct[rows((r * CC + cb * 8) * G, 8 * G), :].astype(F32).reshape(8, G, C)
            for j in range(8):
                obuf[pl.ds(r * CC + cb * 8 + j, G, stride=RR * CC), :] = v[j]

        @pl.when(r == 1)
        def _():
            th_start(tl_finish())
            pl.when(north)(fg2)
            rs6()

        pl.when(r == 1)(rd5)

        @pl.when(r == 5)
        def _():
            rs7(gsec)

        @pl.when(r == 4)
        def _():
            rd6()
            tz_start(th_finish())

    @pl.when(north)
    def _():
        off = fg3()
        for k in range(1, 4):
            for i in range(CC):
                at = pl.ds((128 - k) * CC + i, 1)
                obuf[at, :] += fcat[k - 1, pl.ds(off + CC - 1 - i, 1), :]

    @pl.loop(0, 128)
    def _(i):
        gfield[i] = obuf[rows(i * CC, CC), :].astype(BF16)

    rd7(aden)
    for q in range(4):
        gup[:, q * C : (q + 1) * C] = aden[pl.ds(q * C, C), :]
    gdown[...] = aden[pl.ds(4 * C, 4 * C), :]
    gtaps[...] = tz_finish()[:49] * factor


def on_device(field, land, mirror, depth_weight, norm_gain, up_weight, up_bias, down_proj, layer_scale, section_gain, section_weight, section_bias, cotangent):
    factor = 1.0 / math.sqrt(512 * 2048 / 64.0)
    vm = pl.BlockSpec(memory_space=pltpu.VMEM)
    n = RR * CC * G

    def f(*shape):
        return pltpu.VMEM(shape, F32)

    def h(*shape):
        return pltpu.VMEM(shape, BF16)

    sems = 128
    scratch = dict(
        field=h(128, CC, C),
        land=pltpu.VMEM((CC, 128), jnp.int32),
        taps_in=h(49, C),
        gain_in=h(1, C),
        up=h(C, 512),
        bias_in=h(512),
        down=h(512, C),
        scale_in=h(1, C),
        sgain_in=h(3, C),
        sw=h(3, 512, C),
        sbias_in=h(3, C),
        cot=h(G, 4, C),
        lsem=pltpu.SemaphoreType.DMA((12,)),
        fbuf=f(134 * PITCH, C),
        d32=f(RR * EC * G, C),
        obuf=f(n, C),
        sh=f(EC * 32, C),
        hat=f(n, C),
        rstd=f(n, C),
        landb=f(n, C),
        hat1=f(n, C),
        rstd1=f(n, C),
        hat2=f(n // 4, C),
        rstd2=f(n // 4, C),
        hat3=f(n // 16, C),
        rstd3=f(n // 16, C),
        dgb=h(RR, CC, G, C),
        upacc=f(C, 512),
        dtacc=f(C, 512),
        secacc=f(3, C, 512),
        tapacc=f(49, 8, C),
        lt=f(C, C),
        cb32=f(64, C),
        cotb=h(64, C),
        asec=f(1536, C),
        aden=f(1024, C),
        sec_s1=h(1536, C),
        sec_rq=h(4, 384, C),
        sec_s3=h(384, C),
        sec_r3=h(NH, 48, C),
        sec_r4=h(NZ, 48, C),
        sec_g3=h(NH, 48, C),
        sec_ga=h(4, NH, 48, C),
        den_s1=h(1024, C),
        den_rq=h(4, 256, C),
        den_s3=h(256, C),
        den_r3=h(NH, 32, C),
        den_r4=h(NZ, 32, C),
        den_g3=h(NH, 32, C),
        den_ga=h(4, NH, 32, C),
        tl=h(4, 64, C),
        th=h(NH, 64, C),
        tz=h(NZ, 64, C),
        stl=h(3, 128, C),
        str_=h(3, 128, C),
        cl=h(3, 128, C),
        cr=h(3, 128, C),
        rs=h(3, CC, C),
        rn=h(3, CC, C),
        csl=h(3, 16, C),
        csr=h(3, 16, C),
        cnl=h(3, 16, C),
        cnr=h(3, 16, C),
        dcl=h(RR, 3, G, C),
        dcr=h(RR, 3, G, C),
        rst=h(3, CC, C),
        rsb=h(3, CC, C),
        drs=h(3, CC, C),
        drn=h(3, CC, C),
        dsl=h(3, 16, C),
        dsr=h(3, 16, C),
        dnl=h(3, 16, C),
        dnr=h(3, 16, C),
        fr1=h(NH, 3, CC, C),
        fs2=h(NZ - 1, 3, CC, C),
        fr2=h(NZ, 3, CC, C),
        fcat=f(3, 3 * CC, C),
        zbuf=f(3, 40, C),
        fg=h(3, CC, C),
        hr1=h(NH, 3, CC, C),
        hs2=h(NZ - 1, 3, CC, C),
        hr2=h(NZ, 3, CC, C),
        ssem=pltpu.SemaphoreType.DMA((sems,)),
        rsem=pltpu.SemaphoreType.DMA((sems,)),
    )
    scoped = dict(
        ext=h(ER * EC * G, C),
        ext2=h(ER * EC * G, C),
        wb=h(49, G, C),
        normed=h(n, C),
        act=h(n, 512),
        slope=h(n, 512),
        lev0=h(n, C),
        lev1=h(n // 4, C),
        lev2=h(n // 16, C),
        p1=h(n // 4, 512),
        p2=h(n // 16, 512),
        p3=h(n // 64, 512),
        back1=h(n // 4, C),
        back2=h(n // 16, C),
        direct=h(n, C),
    )

    def whole(*refs):
        pl.run_scoped(functools.partial(kernel, factor, *refs), **scoped)

    bott, gfield, gtaps, gup, gdown, gsec = pl.pallas_call(
        whole,
        out_shape=(
            jax.ShapeDtypeStruct((G, 4, C), BF16),
            jax.ShapeDtypeStruct((128, CC, C), BF16),
            jax.ShapeDtypeStruct((49, C), F32),
            jax.ShapeDtypeStruct((C, 512), F32),
            jax.ShapeDtypeStruct((512, C), F32),
            jax.ShapeDtypeStruct((1536, C), F32),
        ),
        in_specs=[pl.BlockSpec(memory_space=pltpu.SMEM)] + [pl.BlockSpec(memory_space=pltpu.HBM)] * 12,
        out_specs=(vm,) * 6,
        scratch_shapes=list(scratch.values()),
        compiler_params=pltpu.CompilerParams(
            collective_id=0, has_side_effects=True, vmem_limit_bytes=50 * 1024 * 1024
        ),
    )(
        mirror,
        *(
            pltpu.with_memory_space_constraint(v, pltpu.HBM)
            for v in (
                field,
                land.T,
                depth_weight,
                norm_gain.reshape(1, C),
                up_weight,
                up_bias,
                down_proj,
                layer_scale.reshape(1, C),
                section_gain,
                section_weight,
                section_bias,
                cotangent,
            )
        ),
    )
    results = (bott, gfield, gtaps, gup, gdown, gsec)
    anywhere = pl.BlockSpec(memory_space=pl.ANY)

    def write(*refs):
        copies = [pltpu.make_async_copy(refs[i], refs[6 + i], refs[12].at[i]) for i in range(6)]
        for copy in copies:
            copy.start()
        for copy in copies:
            copy.wait()

    bott, gfield, gtaps, gup, gdown, gsec = pl.pallas_call(
        write,
        out_shape=tuple(jax.ShapeDtypeStruct(x.shape, x.dtype) for x in results),
        in_specs=[vm] * 6,
        out_specs=(anywhere,) * 6,
        scratch_shapes=[pltpu.SemaphoreType.DMA((6,))],
        compiler_params=pltpu.CompilerParams(vmem_limit_bytes=16 * 1024 * 1024),
    )(*results)
    return bott, gfield, gtaps, gup, gdown, gsec.reshape(3, 512, C)


def solution(mesh):
    cell = P("lat", "lon", None)
    in_specs = (cell, P("lat", "lon")) + (P(),) * 10 + (cell,)
    out_specs = (cell, cell, P(), P(), P(), P())
    return jax.shard_map(
        on_device, mesh=mesh, in_specs=in_specs, out_specs=out_specs, check_vma=False
    )
```
